32 devices in a mesh: gx: 4 (over y, x), gy: 2 (over core), gz: 4 (over z).
Axes of the slice: x: 2, y: 2, z: 4, core: 2. Of those that a mesh axis runs over, the one named last changes fastest.
Arguments:
- load_vector: float32 [32, 32, 2048], P(('gx', 'gy', 'gz')), may hold values from -24 to 24
- matrix_tiles: float32 [512, 7, 128, 128], P(('gx', 'gy', 'gz')), may hold values from -1 to 6, as said below
- tile_cols: int32 [512, 7], P(('gx', 'gy', 'gz')), may hold values from 0 to 15, as said below
- interior_inv: float32 [384, 128, 128], P(('gx', 'gy', 'gz')), may hold values from -0.1 to 0.3, as said below
- schur_inv: float32 [32, 512, 512], P(('gx', 'gy', 'gz')), may hold values from -0.1 to 0.3, as said below
- coarse_basis: float32 [32, 128, 2048], P(('gx', 'gy', 'gz')), may hold values from -0.125 to 0.125
- coarse_inv: float32 [32, 256, 256], P(('gx', 'gy', 'gz')), may hold values from -0.2 to 0.8, as said below
- row_map: int32 [32, 4, 128], P(('gx', 'gy', 'gz')), may hold values from 0 to 127, each once within a row
- face_link: int32 [32, 4], P(('gx', 'gy', 'gz')), may hold values from 0 to 1, as said below
- coarse_id: int32 [32, 4], P(('gx', 'gy', 'gz')), may hold values from 0 to 31, as said below
Outputs:
- solution: float32 [32, 32, 2048], P(('gx', 'gy', 'gz'))
- residual: float32 [32, 32, 2048], P(('gx', 'gy', 'gz'))
The draws below stay inside these ranges and needn't reach their ends.
Inputs may be any that keep to these rules, and one draw needn't show every extreme that they name: `matrix_tiles`: tile 0 of each block row is its diagonal tile; each subdomain's matrix is symmetric positive definite: the tile of block row i in column block j is the transpose of the tile of block row j in column block i. `tile_cols`: tile 0 of block row i sits in column block i; tiles 1 to 6 sit in column blocks i + a, i - a, i + b, i - b, i + c, i - c modulo 16, for three distinct offsets a, b, c of that subdomain between 1 and (15) // 2; every column block holds exactly 7 tiles. `interior_inv`: each block is symmetric positive definite. `schur_inv`: symmetric positive definite. `coarse_inv`: symmetric positive definite. For partners d and e of round r, entry k of row_map[d, r] and of row_map[e, r] name the same shared unknown. `face_link`: equal for the two partners of a round. coarse_id = owner * 8 + slot, owner being a gz index within the subdomain's line of 4 devices; blocks with the same target are summed. Each subdomain sends at most 2 blocks to one owner and exactly 2 to some owner.
All inputs are finite; a program needn't handle non-finite values.
Results may differ from the reference program's by a relative error of at most 0.00018.
Values sent between devices are 32-bit elements; how exact they have to be, the bound alone decides.
No kernel may reach another device: no remote copies, remote signals or barrier semaphores. Data moves between devices by JAX's collectives and lax.ppermute only.
A program may use at most 64 MiB of HBM per device.

```python
import math
import jax
import jax.numpy as jnp
from jax import lax

BS = 128
NIN = 12
NRHS = 32
TPR = 7
CW = 32
CB = 4
SCAP = 2
OCAP = 8
ITERS = 2
NB = 16
NL = 2048
NI = 512
N_GY = 2
N_GZ = 4
DEVICES = 32


def dominant(key, count, order, diagonal_value, spread):
    noise = jnp.clip(jax.random.normal(key, (count, order, order), jnp.float32), -5.0, 5.0)
    sym_noise = 0.5 * (noise + jnp.swapaxes(noise, 1, 2))
    return diagonal_value * jnp.eye(order, dtype=jnp.float32)[None] + sym_noise * (spread / (2.0 * math.sqrt(order)))


def band_offsets(key):
    half_span = (NB - 1) // 2
    scores = jax.random.randint(jax.random.fold_in(key, 13), (DEVICES, half_span), 0, 1 << 20)
    scores = scores * half_span + jnp.arange(half_span, dtype=jnp.int32)[None, :]
    order = jnp.argsort(scores, axis=1)
    return (order[:, :3] + 1).astype(jnp.int32)


def draw_load_vector(key, part):
    key_one = jax.random.fold_in(jax.random.fold_in(key, 11), 0)
    ramp = 1.0 + 2.0 * jnp.arange(DEVICES, dtype=jnp.float32) / max(DEVICES - 1, 1)
    ramp = ramp[:, None, None]
    base_vals = jnp.clip(jax.random.normal(key_one, (DEVICES, NRHS, NL), jnp.float32), -5.0, 5.0)
    return 1.5 * base_vals * ramp


def draw_matrix_tiles(key, part):
    offsets = band_offsets(key)
    key_diag, key_band = jax.random.split(jax.random.fold_in(key, 12))
    scale_tile = 0.35 / math.sqrt(BS)
    diag_noise = jnp.clip(jax.random.normal(key_diag, (DEVICES, NB, BS, BS), jnp.float32), -5.0, 5.0)
    diag_tiles = 5.0 * jnp.eye(BS, dtype=jnp.float32)[None, None] + (diag_noise + jnp.swapaxes(diag_noise, 2, 3)) * (scale_tile / math.sqrt(2.0))
    upper = jnp.clip(jax.random.normal(key_band, (DEVICES, NB, 3, BS, BS), jnp.float32), -5.0, 5.0) * scale_tile
    dev_ids = jnp.arange(DEVICES, dtype=jnp.int32)[:, None, None]
    row_ids = jnp.arange(NB, dtype=jnp.int32)[None, :, None]
    band_ids = jnp.arange(3, dtype=jnp.int32)[None, None, :]
    source_rows = (row_ids - offsets[:, None, :]) % NB
    lower = jnp.swapaxes(upper[dev_ids, source_rows, band_ids], 3, 4)
    paired = jnp.stack([upper, lower], axis=3).reshape(DEVICES, NB, 6, BS, BS)
    tiles = jnp.concatenate([diag_tiles[:, :, None], paired], axis=2)
    return tiles.reshape(DEVICES * NB, TPR, BS, BS)


def draw_tile_cols(key, part):
    offsets = band_offsets(key)
    row_ids = jnp.arange(NB, dtype=jnp.int32)[None, :]
    columns = [jnp.broadcast_to(row_ids, (DEVICES, NB))]
    for band_no in range(3):
        shift = offsets[:, band_no][:, None]
        columns.append((row_ids + shift) % NB)
        columns.append((row_ids - shift) % NB)
    return jnp.stack(columns, axis=2).reshape(DEVICES * NB, TPR).astype(jnp.int32)


def draw_interior_inv(key, part):
    return dominant(jax.random.fold_in(key, 14), DEVICES * NIN, BS, 0.2, 0.09)


def draw_schur_inv(key, part):
    return dominant(jax.random.fold_in(key, 17), DEVICES, NI, 0.2, 0.09)


def draw_coarse_inv(key, part):
    return dominant(jax.random.fold_in(key, 18), DEVICES, OCAP * CW, 0.6, 0.27)


def draw_face_link(key, part):
    depth_z = N_GZ.bit_length() - 1
    depth_y = N_GY.bit_length() - 1
    levels = jax.random.randint(jax.random.fold_in(key, 15), (4, DEVICES), 0, 4)
    device_ids = jnp.arange(DEVICES, dtype=jnp.int32)
    columns = []
    for round_no, bit_pos in enumerate([0, 1, depth_z, depth_z + depth_y]):
        lower = jnp.bitwise_and(device_ids, DEVICES - 1 - (1 << bit_pos))
        columns.append((levels[round_no][lower] > 0).astype(jnp.int32))
    return jnp.stack(columns, axis=1)


def draw_coarse_id(key, part):
    subkeys = jax.random.split(jax.random.fold_in(key, 16), 4)
    groups = DEVICES // N_GZ
    device_ids = jnp.arange(DEVICES, dtype=jnp.int32)
    busiest = jax.random.randint(subkeys[0], (groups,), 0, N_GZ)[device_ids // N_GZ]
    others = (busiest[:, None] + 1 + jax.random.randint(subkeys[1], (DEVICES, CB - SCAP), 0, N_GZ - 1)) % N_GZ
    owners = jnp.concatenate([jnp.broadcast_to(busiest[:, None], (DEVICES, SCAP)), others], axis=1)
    rotation = jax.random.randint(subkeys[2], (DEVICES, 1), 0, CB)
    positions = (jnp.arange(CB, dtype=jnp.int32)[None, :] + rotation) % CB
    owners = jnp.take_along_axis(owners, positions, axis=1)
    slot_ids = jax.random.randint(subkeys[3], (DEVICES, CB), 0, OCAP)
    return (owners * OCAP + slot_ids).astype(jnp.int32)


def shard_levels(own_key, shape, cuts, least, high):
    level = 1.0
    for position, parts in cuts:
        heights = jax.random.uniform(jax.random.fold_in(jax.random.fold_in(own_key, 6), position), (parts,), jnp.float32, least / len(cuts), high / len(cuts))
        level = level * jnp.repeat(jnp.exp(heights), shape[position] // parts).reshape((-1,) + (1,) * (len(shape) - 1 - position))
    return level


def normal_values(own_key, dims, width, bound, cuts=(), held_as=jnp.bfloat16):
    array = width * jax.random.normal(own_key, dims, jnp.float32)
    if cuts:
        array = array * shard_levels(own_key, dims, cuts, -0.22, 0.18)
    return jnp.clip(array, -bound, bound).astype(held_as)


def setup_inputs(seed: int = 0) -> dict:
    key_of = jax.random.split(jax.random.key(seed), 11)
    return {
        "load_vector": draw_load_vector(jax.random.fold_in(key_of[10], 71), 0),
        "matrix_tiles": draw_matrix_tiles(jax.random.fold_in(key_of[10], 71), 0),
        "tile_cols": draw_tile_cols(jax.random.fold_in(key_of[10], 71), 0),
        "interior_inv": draw_interior_inv(jax.random.fold_in(key_of[10], 71), 0),
        "schur_inv": draw_schur_inv(jax.random.fold_in(key_of[10], 71), 0),
        "coarse_basis": normal_values(key_of[5], (DEVICES, CB * CW, NL), NL ** -0.5, 0.125, ((0, 32),), jnp.float32),
        "coarse_inv": draw_coarse_inv(jax.random.fold_in(key_of[10], 71), 0),
        "row_map": jax.vmap(lambda own: jax.random.permutation(own, BS))(jax.random.split(key_of[7], DEVICES * 4)).reshape((DEVICES, 4, BS)).astype(jnp.int32),
        "face_link": draw_face_link(jax.random.fold_in(key_of[10], 71), 0),
        "coarse_id": draw_coarse_id(jax.random.fold_in(key_of[10], 71), 0),
    }


HIGH = lax.Precision.HIGHEST


def swap_bits():
    depth_z = N_GZ.bit_length() - 1
    depth_y = N_GY.bit_length() - 1
    return [0, 1, depth_z, depth_z + depth_y]


def assemble(vector, row_map, face_link):
    offset = NIN * BS
    device_ids = jnp.arange(DEVICES, dtype=jnp.int32)
    pieces = [vector[:, :, :offset]]
    for round_no, bit_pos in enumerate(swap_bits()):
        face_rows = vector[:, :, offset + round_no * BS:offset + (round_no + 1) * BS]
        onehot = (row_map[:, round_no, :, None] == jnp.arange(BS, dtype=jnp.int32)[None, None, :]).astype(jnp.float32)
        outgoing = jnp.einsum('dnj,dkj->dnk', face_rows, onehot, precision=HIGH)
        partner = jnp.bitwise_xor(device_ids, 1 << bit_pos)
        incoming = outgoing[partner]
        returned = jnp.einsum('dnk,dkj->dnj', incoming, onehot, precision=HIGH)
        link_vals = face_link[:, round_no].astype(jnp.float32)[:, None, None]
        pieces.append(face_rows + link_vals * returned)
    return jnp.concatenate(pieces, axis=2)


def row_weights(face_link):
    weight_parts = [jnp.ones((DEVICES, NIN * BS), jnp.float32)]
    for round_no in range(4):
        scale_face = 1.0 - 0.5 * face_link[:, round_no].astype(jnp.float32)
        weight_parts.append(jnp.broadcast_to(scale_face[:, None], (DEVICES, BS)))
    return jnp.concatenate(weight_parts, axis=1)[:, None, :]


def apply_matrix(matrix_tiles, tile_cols, vector, row_map, face_link):
    tiles_dev = matrix_tiles.reshape(DEVICES, NB, TPR, BS, BS)
    cols_dev = tile_cols.reshape(DEVICES, NB, TPR)

    def one_device(items):
        tiles_one, cols_one, vector_one = items
        picked = vector_one.reshape(NRHS, NB, BS)[:, cols_one]
        return jnp.einsum('rtij,nrtj->nri', tiles_one, picked, precision=HIGH).reshape(NRHS, NL)

    product = lax.map(one_device, (tiles_dev, cols_dev, vector))
    return assemble(product, row_map, face_link)


def precondition(resid, weight, interior_inv, schur_inv, coarse_basis, coarse_inv, row_map, face_link, coarse_id):
    offset = NIN * BS
    scaled = weight * resid
    inner_part = jnp.einsum('dbij,dnbj->dnbi', interior_inv.reshape(DEVICES, NIN, BS, BS),
                            scaled[:, :, :offset].reshape(DEVICES, NRHS, NIN, BS), precision=HIGH)
    inner_part = inner_part.reshape(DEVICES, NRHS, offset)
    outer_part = jnp.einsum('dij,dnj->dni', schur_inv, scaled[:, :, offset:], precision=HIGH)
    contrib = jnp.einsum('dcl,dnl->dcn', coarse_basis, scaled, precision=HIGH).reshape(DEVICES * CB, CW * NRHS)
    base_row = (jnp.arange(DEVICES, dtype=jnp.int32) // N_GZ) * (N_GZ * OCAP)
    target = (base_row[:, None] + coarse_id.astype(jnp.int32)).reshape(DEVICES * CB)
    gathered = jax.ops.segment_sum(contrib, target, num_segments=DEVICES * OCAP)
    solved = jnp.einsum('dij,djn->din', coarse_inv, gathered.reshape(DEVICES, OCAP * CW, NRHS), precision=HIGH)
    picked = solved.reshape(DEVICES * OCAP, CW * NRHS)[target].reshape(DEVICES, CB * CW, NRHS)
    correction = jnp.einsum('dcn,dcl->dnl', picked, coarse_basis, precision=HIGH)
    local_sum = jnp.concatenate([inner_part, outer_part], axis=2) + correction
    return assemble(weight * local_sum, row_map, face_link)


def reference(load_vector, matrix_tiles, tile_cols, interior_inv, schur_inv, coarse_basis, coarse_inv, row_map, face_link, coarse_id):
    weight = row_weights(face_link)

    def inner_product(left, right):
        return jnp.sum(weight * left * right, axis=(0, 2))

    def precond(resid):
        return precondition(resid, weight, interior_inv, schur_inv, coarse_basis, coarse_inv, row_map, face_link, coarse_id)

    resid = assemble(load_vector, row_map, face_link)
    solution = jnp.zeros_like(resid)
    precond_res = precond(resid)
    direction = precond_res
    rho_now = inner_product(resid, precond_res)
    for turn_no in range(ITERS):
        product_dir = apply_matrix(matrix_tiles, tile_cols, direction, row_map, face_link)
        step_len = (rho_now / inner_product(direction, product_dir))[None, :, None]
        solution = solution + step_len * direction
        resid = resid - step_len * product_dir
        if turn_no + 1 < ITERS:
            precond_res = precond(resid)
            rho_next = inner_product(resid, precond_res)
            direction = precond_res + (rho_next / rho_now)[None, :, None] * direction
            rho_now = rho_next
    return solution, resid
```

```python
import jax
import jax.numpy as jnp
from jax import lax
from jax.experimental import pallas as pl
from jax.experimental.pallas import tpu as pltpu
from jax.sharding import PartitionSpec as P

BS = 128
NIN = 12
NF = 4
NRHS = 32
CW = 32
CB = 4
OCAP = 8
NB = 16
TPR = 7
NL = 2048
AXES = ("gx", "gy", "gz")
F32 = jnp.float32
BF16 = jnp.bfloat16
NN = (((1,), (0,)), ((), ()))
NT = (((1,), (1,)), ((), ()))


def mm(left, right, dims=NN):
    return lax.dot_general(left, right, dims, preferred_element_type=F32)


def halves(value):
    high = value.astype(BF16)
    return high, (value - high.astype(F32)).astype(BF16)


def dot_halves(left, right, dims=NN):
    (lh, ll), (rh, rl) = left, right
    rows = lh.shape[0]
    both = mm(jnp.concatenate([lh, ll], axis=0), rh, dims)
    return both[:rows] + both[rows:] + mm(lh, rl, dims)


def select_lanes(value, onehot):
    rows = value.shape[0]
    high, rest = halves(value)
    low = (value - high.astype(F32) - rest.astype(F32)).astype(BF16)
    out = mm(jnp.concatenate([high, rest, low], axis=0), onehot)
    return out[:rows] + out[rows : 2 * rows] + out[2 * rows :]


def lanes(block):
    return slice(block * BS, (block + 1) * BS)


def weight_of(link_ref, face):
    return 1.0 - 0.5 * link_ref[0, face].astype(F32)


def interior_body(x_ref, inv_ref, basis_ref, inner_ref, part_ref, *, flat):
    pieces = []
    for b in range(NIN):
        xb = halves(x_ref[:, lanes(b)] if flat else x_ref[b])
        pieces.append(xb)
        inner_ref[b] = dot_halves(xb, halves(inv_ref[b]))
    cat = tuple(jnp.concatenate([p[h] for p in pieces], axis=1) for h in range(2))
    part_ref[...] = dot_halves(cat, halves(basis_ref[:, : NIN * BS]), NT)


def face_solve(faces, link_ref, schur_ref, basis_ref, part_ref, outer_ref, contrib_ref):
    scaled = halves(
        jnp.concatenate([faces[r] * weight_of(link_ref, r) for r in range(NF)], axis=1)
    )
    outer = dot_halves(scaled, halves(schur_ref[...]))
    for r in range(NF):
        outer_ref[r] = outer[:, lanes(r)]
    contrib_ref[...] = part_ref[...] + dot_halves(
        scaled, halves(basis_ref[:, NIN * BS :]), NT
    )


def first_faces_body(
    x_ref, in0, in1, in2, in3, map_ref, link_ref, schur_ref, basis_ref, part_ref,
    face_ref, outer_ref, contrib_ref, swap_ref,
):
    faces = []
    rows = lax.broadcasted_iota(jnp.int32, (BS, BS), 0).astype(F32)
    for r, inc in enumerate((in0, in1, in2, in3)):
        mine = (rows == map_ref[r : r + 1, :].astype(F32)).astype(F32).astype(BF16)
        theirs = (rows == inc[NRHS : NRHS + 1, :]).astype(F32).astype(BF16)
        link = link_ref[0, r].astype(F32)
        swap_ref[r] = mm(mine, theirs, NT).astype(BF16)
        came = select_lanes(inc[:NRHS, :], mm(theirs, mine, NT).astype(BF16))
        faces.append(x_ref[:, lanes(NIN + r)] + link * came)
        face_ref[r] = faces[-1]
    face_solve(faces, link_ref, schur_ref, basis_ref, part_ref, outer_ref, contrib_ref)


def next_faces_body(
    y_ref, in0, in1, in2, in3, link_ref, schur_ref, basis_ref, part_ref,
    face_ref, outer_ref, contrib_ref,
):
    faces = []
    for r, inc in enumerate((in0, in1, in2, in3)):
        faces.append(y_ref[NIN + r] + inc[...])
        face_ref[r] = faces[-1]
    face_solve(faces, link_ref, schur_ref, basis_ref, part_ref, outer_ref, contrib_ref)


def send_face(value, face, link_ref, swap_ref, out_ref):
    out_ref[...] = select_lanes(value, swap_ref[face]) * link_ref[0, face].astype(F32)


def correct(contribs, table, outer_ref, basis_ref, link_ref, swap_ref, back_ref, face_ref, outs):
    back = dot_halves(halves(jnp.concatenate(contribs, axis=1)), table, NT)
    back_ref[...] = back
    corr = dot_halves(halves(back), halves(basis_ref[:, NIN * BS :]))
    for r in range(NF):
        value = weight_of(link_ref, r) * (outer_ref[r] + corr[:, lanes(r)])
        face_ref[r] = value
        send_face(value, r, link_ref, swap_ref, outs[r])


def first_coarse_body(*refs, line):
    target_ref, coarse_ref, id_ref, own_ref = refs[:4]
    others = refs[4 : 3 + line]
    outer_ref, basis_ref, link_ref, swap_ref = refs[3 + line : 7 + line]
    high_ref, low_ref, back_ref, face_ref = refs[7 + line : 11 + line]
    outs = refs[11 + line :]
    targets = jnp.concatenate([target_ref[0:1, :]] + [o[NRHS : NRHS + 1, :] for o in others], axis=1)
    width = line * CB * CW
    rows = lax.broadcasted_iota(jnp.int32, (OCAP * CW, width), 0)
    for b in range(CB):
        block = id_ref[0, b]
        owner = block // OCAP
        start = pl.multiple_of((block % OCAP) * CW, CW)
        picked = (
            (rows + owner * (OCAP * CW)).astype(F32) == targets
        ).astype(F32).astype(BF16)
        high, low = halves(coarse_ref[owner, pl.ds(start, CW), :])
        both = mm(jnp.concatenate([high, low], axis=0), picked)
        high_ref[b * CW : (b + 1) * CW, :] = both[:CW].astype(BF16)
        low_ref[b * CW : (b + 1) * CW, :] = both[CW:].astype(BF16)
    contribs = [own_ref[...]] + [o[:NRHS, :] for o in others]
    correct(contribs, (high_ref[...], low_ref[...]), outer_ref, basis_ref, link_ref, swap_ref,
            back_ref, face_ref, outs)


def next_coarse_body(*refs, line):
    contribs = [ref[...] for ref in refs[:line]]
    high_ref, low_ref, outer_ref, basis_ref, link_ref, swap_ref = refs[line : 6 + line]
    back_ref, face_ref = refs[6 + line : 8 + line]
    correct(contribs, (high_ref[...], low_ref[...]), outer_ref, basis_ref, link_ref, swap_ref,
            back_ref, face_ref, refs[8 + line :])


def add_row(x, i, tiles_ref, cols_ref, acc_ref, base):
    wide = jnp.concatenate([tiles_ref[(i - base) * TPR + t] for t in range(TPR)], axis=1)
    out = dot_halves(halves(x), halves(wide))
    places = [cols_ref[i, t] for t in range(TPR)]
    before = [acc_ref[place] for place in places]
    for t in range(TPR):
        acc_ref[places[t]] = before[t] + out[:, lanes(t)]


def own_apply_body(inner_ref, back_ref, basis_ref, face_ref, tiles_ref, cols_ref, z_ref, acc_ref):
    acc_ref[...] = jnp.zeros_like(acc_ref)
    back = halves(back_ref[...])
    for b in range(NIN):
        z_ref[b] = inner_ref[b] + dot_halves(back, halves(basis_ref[:, lanes(b)]))
    for i in range(NB):
        x = z_ref[i] if i < NIN else face_ref[i - NIN]
        add_row(x, i, tiles_ref, cols_ref, acc_ref, 0)


def face_apply_body(
    acc_ref, in0, in1, in2, in3, face_ref, tiles_ref, cols_ref, link_ref, swap_ref,
    y_ref, z_ref, out0, out1, out2, out3,
):
    y_ref[...] = acc_ref[...]
    for r, inc in enumerate((in0, in1, in2, in3)):
        came = inc[...]
        z_ref[r] = face_ref[r] + came
        add_row(came, NIN + r, tiles_ref, cols_ref, y_ref, 0)
    for r, out in enumerate((out0, out1, out2, out3)):
        send_face(y_ref[NIN + r], r, link_ref, swap_ref, out)


def dots_body(load_ref, zi_ref, zf_ref, y_ref, wi_ref, wf_ref, v_ref, out_ref):
    sums = [jnp.zeros((NRHS, BS), F32) for _ in range(6)]
    for b in range(NB):
        load = load_ref[:, lanes(b)]
        z = zi_ref[b] if b < NIN else zf_ref[b - NIN]
        w = wi_ref[b] if b < NIN else wf_ref[b - NIN]
        y, v = y_ref[b], v_ref[b]
        for k, (left, right) in enumerate(((load, z), (z, y), (load, w), (y, w), (z, v), (w, v))):
            sums[k] = sums[k] + left * right
    place = lax.broadcasted_iota(jnp.int32, (NRHS, BS), 1)
    case = lax.broadcasted_iota(jnp.int32, (NRHS, BS), 0)
    for row in range(2):
        total = jnp.zeros((NRHS, BS), F32)
        for k in range(4 * row, min(4 * row + 4, 6)):
            column = jnp.sum(sums[k], axis=1, keepdims=True)
            total = total + jnp.where(place == case + NRHS * (k % 4), column, 0.0)
        out_ref[row : row + 1, :] = jnp.sum(total, axis=0, keepdims=True)


def final_body(
    coef_ref, load_ref, rf_ref, zi_ref, zf_ref, y_ref, qf_ref, wi_ref, wf_ref, v_ref,
    in0, in1, in2, in3, sol_ref, res_ref,
):
    first = coef_ref[:, 0:1]
    second = coef_ref[:, 1:2]
    for b in range(NB):
        if b < NIN:
            r, z, q, w, v = load_ref[:, lanes(b)], zi_ref[b], y_ref[b], wi_ref[b], v_ref[b]
        else:
            f = b - NIN
            v = v_ref[b] + (in0, in1, in2, in3)[f][...]
            r, z, q, w = rf_ref[f], zf_ref[f], qf_ref[f], wf_ref[f]
        sol_ref[0, :, lanes(b)] = first * z - second * w
        res_ref[0, :, lanes(b)] = r - first * q + second * v


def f32(*shape):
    return jax.ShapeDtypeStruct(shape, F32)


def bf16(*shape):
    return jax.ShapeDtypeStruct(shape, BF16)


SMEM = pl.BlockSpec(memory_space=pltpu.SMEM)
VMEM = pl.BlockSpec(memory_space=pltpu.VMEM)


def call(body, name, outs, specs, *args):
    return pl.pallas_call(
        body,
        name=name,
        out_shape=outs,
        in_specs=specs,
        out_specs=[VMEM] * len(outs),
        compiler_params=pltpu.CompilerParams(vmem_limit_bytes=40 << 20),
    )(*args)


def on_device(
    load_vector, matrix_tiles, tile_cols, interior_inv, schur_inv, coarse_basis, coarse_inv,
    row_map, face_link, coarse_id,
):
    load = load_vector[0]
    basis = coarse_basis[0]
    schur = schur_inv[0]
    maps = row_map[0]
    tiles = matrix_tiles.reshape(NB * TPR, BS, BS)
    line = lax.axis_size("gz")
    devices = line * lax.axis_size("gy") * lax.axis_size("gx")
    depth_z = line.bit_length() - 1
    depth_y = lax.axis_size("gy").bit_length() - 1
    masks = [1, 2, 1 << depth_z, 1 << (depth_z + depth_y)]

    def trade(value, mask):
        return lax.ppermute(value, AXES, [(i, i ^ mask) for i in range(devices)])

    def trade_faces(faces):
        return [trade(face, mask) for face, mask in zip(faces, masks)]

    def trade_line(value):
        return [trade(value, mask) for mask in range(1, line)]

    coarse_all = lax.all_gather(coarse_inv[0], "gz", axis=0)
    pad = jnp.zeros((7, BS), F32)
    came = trade_faces(
        [
            jnp.concatenate([load[:, lanes(NIN + r)], maps[r : r + 1].astype(F32), pad], axis=0)
            for r in range(NF)
        ]
    )
    block = f32(NIN, NRHS, BS)
    face = f32(NF, NRHS, BS)
    small = f32(NRHS, BS)
    inner, part = call(
        lambda *refs: interior_body(*refs, flat=True), "interior_load", [block, small], [VMEM] * 3,
        load, interior_inv, basis,
    )
    r_face, outer, contrib, swap = call(
        first_faces_body, "faces_load", [face, face, small, bf16(NF, BS, BS)],
        [VMEM] * 6 + [SMEM] + [VMEM] * 3,
        load, *came, maps, face_link, schur, basis, part,
    )
    target = (coarse_id[0].astype(F32)[:, None] * CW + jnp.arange(CW, dtype=F32)[None, :]).reshape(1, CB * CW)
    target = jnp.concatenate([target, pad], axis=0)
    others = trade_line(jnp.concatenate([contrib, target], axis=0))
    width = line * CB * CW
    high, low, back, u_face, *sends = call(
        lambda *refs: first_coarse_body(*refs, line=line), "coarse_load",
        [bf16(BS, width), bf16(BS, width), small, face] + [small] * NF,
        [VMEM, VMEM, SMEM] + [VMEM] * line + [VMEM, VMEM, SMEM, VMEM],
        target, coarse_all, coarse_id, contrib, *others, outer, basis, face_link, swap,
    )

    def apply(inner, back, u_face, sends, stage):
        came = trade_faces(sends)
        z, acc = call(
            own_apply_body, "own_" + stage, [block, f32(NB, NRHS, BS)], [VMEM] * 5 + [SMEM],
            inner, back, basis, u_face, tiles, tile_cols,
        )
        y, z_face, *sends = call(
            face_apply_body, "face_" + stage, [f32(NB, NRHS, BS), face] + [small] * NF,
            [VMEM] * 7 + [SMEM, SMEM, VMEM],
            acc, *came, u_face, tiles, tile_cols, face_link, swap,
        )
        return z, z_face, y, sends

    z, z_face, y, sends = apply(inner, back, u_face, sends, "first")
    came = trade_faces(sends)
    inner, part = call(
        lambda *refs: interior_body(*refs, flat=False), "interior_image", [block, small], [VMEM] * 3,
        y, interior_inv, basis,
    )
    q_face, outer, contrib = call(
        next_faces_body, "faces_image", [face, face, small],
        [VMEM] * 5 + [SMEM] + [VMEM] * 3,
        y, *came, face_link, schur, basis, part,
    )
    others = trade_line(contrib)
    back, u_face, *sends = call(
        lambda *refs: next_coarse_body(*refs, line=line), "coarse_image",
        [small, face] + [small] * NF,
        [VMEM] * (line + 4) + [SMEM, VMEM],
        contrib, *others, high, low, outer, basis, face_link, swap,
    )
    w, w_face, v, sends = apply(inner, back, u_face, sends, "second")
    came = trade_faces(sends)
    (dots,) = call(dots_body, "dots", [f32(2, BS)], [VMEM] * 7, load, z, z_face, y, w, w_face, v)
    spread = lax.all_to_all(jnp.broadcast_to(dots[None], (devices, 2, BS)), AXES, 0, 0)
    total = jnp.sum(spread, axis=0).reshape(8, NRHS)
    rz, zq, rw, qw, zv, wv = [total[k] for k in range(6)]
    alpha = rz / zq
    rho = rz - alpha * (rw + zq) + alpha * alpha * qw
    grow = 1.0 + rho / rz
    curve = grow * grow * zq - grow * alpha * (zv + qw) + alpha * alpha * wv
    step = rho / curve
    coef = jnp.stack([alpha + step * grow, step * alpha], axis=1)
    out = f32(1, NRHS, NL)
    return tuple(
        call(
            final_body, "combine", [out, out], [VMEM] * 14,
            coef, load, r_face, z, z_face, y, q_face, w, w_face, v, *came,
        )
    )


def solution(mesh):
    lead = P(AXES, None, None)
    flat = P(AXES, None)
    in_specs = (lead, P(AXES, None, None, None), flat, lead, lead, lead, lead, lead, flat, flat)
    return jax.shard_map(
        on_device, mesh=mesh, in_specs=in_specs, out_specs=(lead, lead), check_vma=False
    )
```

```python
import jax
import jax.numpy as jnp
from jax import lax
from jax.experimental import pallas as pl
from jax.experimental.pallas import tpu as pltpu
from jax.sharding import PartitionSpec as P

BS = 128
NIN = 12
NF = 4
NRHS = 32
CW = 32
CB = 4
OCAP = 8
NB = 16
TPR = 7
NL = 2048
AXES = ("gx", "gy", "gz")
F32 = jnp.float32
BF16 = jnp.bfloat16
NN = (((1,), (0,)), ((), ()))
NT = (((1,), (1,)), ((), ()))


def mm(left, right, dims=NN):
    return lax.dot_general(left, right, dims, preferred_element_type=F32)


def halves(value):
    high = value.astype(BF16)
    return high, (value - high.astype(F32)).astype(BF16)


def dot_halves(left, right, dims=NN):
    (lh, ll), (rh, rl) = left, right
    rows = lh.shape[0]
    both = mm(jnp.concatenate([lh, ll], axis=0), rh, dims)
    return both[:rows] + both[rows:] + mm(lh, rl, dims)


def select_lanes(value, onehot):
    rows = value.shape[0]
    high, rest = halves(value)
    low = (value - high.astype(F32) - rest.astype(F32)).astype(BF16)
    out = mm(jnp.concatenate([high, rest, low], axis=0), onehot)
    return out[:rows] + out[rows : 2 * rows] + out[2 * rows :]


def lanes(block):
    return slice(block * BS, (block + 1) * BS)


def start_all(sems, *pairs):
    copies = [pltpu.make_async_copy(src, dst, sems.at[k]) for k, (src, dst) in enumerate(pairs)]
    for copy in copies:
        copy.start()
    return copies


def prepare_body(
    load_ref, map_ref, id_ref, link_ref, target_ref, column_ref, weight_ref, side0, side1, side2, side3,
    ids, links, maps, faces, sems,
):
    copies = start_all(
        sems,
        (id_ref, ids),
        (link_ref, links),
        (map_ref, maps),
        (load_ref.at[0, :, NIN * BS :], faces),
    )
    copies[0].wait()
    lane = lax.broadcasted_iota(jnp.int32, (8, BS), 1)
    row = lax.broadcasted_iota(jnp.int32, (BS, BS), 0)
    target = lane % CW
    column = row % CW
    for b in range(CB):
        target = jnp.where(lane // CW == b, target + ids[0, b] * CW, target)
        column = jnp.where(row // CW == b, column + ids[0, b] * CW, column)
    target_ref[...] = target.astype(F32)
    column_ref[...] = column.astype(F32)
    copies[1].wait()
    for r in range(NF):
        link = jnp.full((1, BS), links[0, r], jnp.int32).astype(F32)
        weight_ref[r : r + 1, :] = 1.0 - 0.5 * link
        weight_ref[NF + r : NF + r + 1, :] = link
    copies[2].wait()
    copies[3].wait()
    for r, out in enumerate((side0, side1, side2, side3)):
        out[:NRHS, :] = faces[:, lanes(r)]
        out[NRHS:, :] = jnp.broadcast_to(maps[0, r : r + 1, :], (8, BS)).astype(F32)


def interior_body(
    x_ref, inv_ref, basis_ref, schur_ref,
    inner_ref, part_ref, schur_high, schur_low, basis_high, basis_low, *scratch, flat,
):
    inv, basis, schur = scratch[:3]
    sems = scratch[-1]
    pairs = [(inv_ref, inv), (basis_ref.at[0], basis), (schur_ref.at[0], schur)]
    if flat:
        pairs.append((x_ref.at[0, :, : NIN * BS], scratch[3]))
    copies = start_all(sems, *pairs)
    if flat:
        copies[3].wait()
    copies[0].wait()
    pieces = []
    for b in range(NIN):
        xb = halves(scratch[3][:, lanes(b)] if flat else x_ref[b])
        pieces.append(xb)
        inner_ref[b] = dot_halves(xb, halves(inv[b]))
    cat = tuple(jnp.concatenate([p[h] for p in pieces], axis=1) for h in range(2))
    copies[1].wait()
    part_ref[...] = dot_halves(cat, halves(basis[:, : NIN * BS]), NT)
    basis_high[...], basis_low[...] = halves(basis[:, NIN * BS :])
    copies[2].wait()
    schur_high[...], schur_low[...] = halves(schur[...])


def face_solve(faces, mats, weight_ref, part_ref, outer_ref, contrib_ref):
    schur_high, schur_low, basis_high, basis_low = mats
    scaled = halves(
        jnp.concatenate([faces[r] * weight_ref[r : r + 1, :] for r in range(NF)], axis=1)
    )
    contrib_ref[:NRHS, :] = part_ref[...] + dot_halves(
        scaled, (basis_high[...], basis_low[...]), NT
    )
    outer = dot_halves(scaled, (schur_high[...], schur_low[...]))
    for r in range(NF):
        outer_ref[r] = outer[:, lanes(r)]


def first_faces_body(
    own0, own1, own2, own3, in0, in1, in2, in3, target_ref, weight_ref,
    schur_high, schur_low, basis_high, basis_low, part_ref,
    face_ref, outer_ref, contrib_ref, swap_ref,
):
    faces = []
    rows = lax.broadcasted_iota(jnp.int32, (BS, BS), 0).astype(F32)
    for r, (own, inc) in enumerate(zip((own0, own1, own2, own3), (in0, in1, in2, in3))):
        mine = (rows == own[NRHS : NRHS + 1, :]).astype(F32).astype(BF16)
        theirs = (rows == inc[NRHS : NRHS + 1, :]).astype(F32).astype(BF16)
        link = weight_ref[NF + r : NF + r + 1, :]
        swap_ref[r] = (mm(mine, theirs, NT) * link).astype(BF16)
        came = select_lanes(inc[:NRHS, :], (mm(theirs, mine, NT) * link).astype(BF16))
        faces.append(own[:NRHS, :] + came)
        face_ref[r] = faces[-1]
    contrib_ref[NRHS:, :] = target_ref[...]
    mats = (schur_high, schur_low, basis_high, basis_low)
    face_solve(faces, mats, weight_ref, part_ref, outer_ref, contrib_ref)


def next_faces_body(
    y_ref, in0, in1, in2, in3, weight_ref, schur_high, schur_low, basis_high, basis_low, part_ref,
    face_ref, outer_ref, contrib_ref,
):
    faces = []
    for r, inc in enumerate((in0, in1, in2, in3)):
        faces.append(y_ref[NIN + r] + inc[...])
        face_ref[r] = faces[-1]
    mats = (schur_high, schur_low, basis_high, basis_low)
    face_solve(faces, mats, weight_ref, part_ref, outer_ref, contrib_ref)


def correct(contribs, table, outer_ref, basis, weight_ref, swap_ref, back_ref, face_ref, outs):
    back = dot_halves(halves(jnp.concatenate(contribs, axis=1)), table, NT)
    back_ref[...] = back
    corr = dot_halves(halves(back), basis)
    for r in range(NF):
        value = weight_ref[r : r + 1, :] * (outer_ref[r] + corr[:, lanes(r)])
        face_ref[r] = value
        outs[r][...] = select_lanes(value, swap_ref[r])


def first_coarse_body(*refs, line):
    coarse_hbm, column_ref = refs[:2]
    sides = refs[2 : 2 + line]
    outer_ref, basis_high, basis_low, weight_ref, swap_ref = refs[2 + line : 7 + line]
    high_ref, low_ref, back_ref, face_ref = refs[7 + line : 11 + line]
    outs = refs[11 + line : 11 + line + NF]
    coarse, sems = refs[11 + line + NF :]
    copies = start_all(sems, *[(coarse_hbm.at[o], coarse.at[o]) for o in range(line)])
    targets = jnp.concatenate([side[NRHS : NRHS + 1, :] for side in sides], axis=1)
    own = OCAP * CW
    rows = lax.broadcasted_iota(jnp.int32, (own, line * CB * CW), 0).astype(F32)
    places = lax.broadcasted_iota(jnp.int32, (BS, own), 1).astype(F32)
    column = jnp.concatenate([column_ref[...]] * (own // BS), axis=1)
    table = jnp.zeros((2 * BS, line * CB * CW), F32)
    for o in range(line):
        pick = (rows + float(o * own) == targets).astype(F32).astype(BF16)
        take = (places + float(o * own) == column).astype(F32).astype(BF16)
        copies[o].wait()
        high, low = halves(coarse[o])
        both = jnp.concatenate([mm(take, high).astype(BF16), mm(take, low).astype(BF16)], axis=0)
        table = table + mm(both, pick)
    high_ref[...] = table[:BS].astype(BF16)
    low_ref[...] = table[BS:].astype(BF16)
    contribs = [side[:NRHS, :] for side in sides]
    correct(contribs, (high_ref[...], low_ref[...]), outer_ref, (basis_high[...], basis_low[...]),
            weight_ref, swap_ref, back_ref, face_ref, outs)


def next_coarse_body(*refs, line):
    contribs = [ref[...] for ref in refs[:line]]
    high_ref, low_ref, outer_ref, basis_high, basis_low, weight_ref, swap_ref = refs[line : 7 + line]
    back_ref, face_ref = refs[7 + line : 9 + line]
    correct(contribs, (high_ref[...], low_ref[...]), outer_ref, (basis_high[...], basis_low[...]),
            weight_ref, swap_ref, back_ref, face_ref, refs[9 + line :])


def add_row(x, i, wide, cols_ref, acc_ref):
    out = dot_halves(halves(x), wide)
    places = [cols_ref[t, i] for t in range(TPR)]
    before = [acc_ref[place] for place in places]
    for t in range(TPR):
        acc_ref[places[t]] = before[t] + out[:, lanes(t)]


def own_apply_body(
    inner_ref, back_ref, basis_ref, face_ref, tiles_ref, cols_ref, z_ref, acc_ref, wide_high, wide_low,
    basis, tiles, sems,
):
    pairs = [(basis_ref.at[0, :, : NIN * BS], basis)]
    pairs += [(tiles_ref.at[i], tiles.at[i]) for i in range(NB)]
    copies = start_all(sems, *pairs)
    acc_ref[...] = jnp.zeros_like(acc_ref)
    back = halves(back_ref[...])
    copies[0].wait()
    for b in range(NIN):
        z_ref[b] = inner_ref[b] + dot_halves(back, halves(basis[:, lanes(b)]))
    for i in range(NB):
        copies[1 + i].wait()
        wide = halves(jnp.concatenate([tiles[i, t] for t in range(TPR)], axis=1))
        if i >= NIN:
            wide_high[i - NIN], wide_low[i - NIN] = wide
        add_row(z_ref[i] if i < NIN else face_ref[i - NIN], i, wide, cols_ref, acc_ref)


def face_apply_body(
    acc_ref, in0, in1, in2, in3, face_ref, wide_high, wide_low, cols_ref, swap_ref,
    y_ref, z_ref, out0, out1, out2, out3,
):
    y_ref[...] = acc_ref[...]
    for r, inc in enumerate((in0, in1, in2, in3)):
        came = inc[...]
        z_ref[r] = face_ref[r] + came
        add_row(came, NIN + r, (wide_high[r], wide_low[r]), cols_ref, y_ref)
    for r, out in enumerate((out0, out1, out2, out3)):
        out[...] = select_lanes(y_ref[NIN + r], swap_ref[r])


def dots_body(load_hbm, zi, zf, y, wi, wf_ref, v_ref, out_ref, load_ref, sems):
    (copy,) = start_all(sems, (load_hbm.at[0], load_ref))
    copy.wait()
    sums = [jnp.zeros((NRHS, BS), F32) for _ in range(6)]
    for b in range(NB):
        load = load_ref[:, lanes(b)]
        z = zi[b] if b < NIN else zf[b - NIN]
        w = wi[b] if b < NIN else wf_ref[b - NIN]
        q, v = y[b], v_ref[b]
        for k, (left, right) in enumerate(((load, z), (z, q), (load, w), (q, w), (z, v), (w, v))):
            sums[k] = sums[k] + left * right
    place = lax.broadcasted_iota(jnp.int32, (NRHS, BS), 1)
    case = lax.broadcasted_iota(jnp.int32, (NRHS, BS), 0)
    for row in range(2):
        total = jnp.zeros((NRHS, BS), F32)
        for k in range(4 * row, min(4 * row + 4, 6)):
            column = jnp.sum(sums[k], axis=1, keepdims=True)
            total = total + jnp.where(place == case + NRHS * (k % 4), column, 0.0)
        total = jnp.sum(total, axis=0, keepdims=True)
        out_ref[:, row : row + 1, :] = jnp.broadcast_to(total[None], (out_ref.shape[0], 1, BS))


def final_body(
    dots_ref, in0, in1, in2, in3, load_h, rf, zi, zf, y, qf, wi, wf, v, sol_ref, res_ref, load, sems,
):
    copies = start_all(sems, (load_h.at[0, :, : NIN * BS], load))
    place = lax.broadcasted_iota(jnp.int32, (NRHS, BS), 1)
    case = lax.broadcasted_iota(jnp.int32, (NRHS, BS), 0)
    total = jnp.sum(dots_ref[...], axis=0)
    rz, zq, rw, qw, zv, wv = [
        jnp.sum(
            jnp.where(place == case + NRHS * (k % 4), total[k // 4 : k // 4 + 1, :], 0.0),
            axis=1,
            keepdims=True,
        )
        for k in range(6)
    ]
    alpha = rz / zq
    rho = rz - alpha * (rw + zq) + alpha * alpha * qw
    grow = 1.0 + rho / rz
    curve = grow * grow * zq - grow * alpha * (zv + qw) + alpha * alpha * wv
    step = rho / curve
    first = alpha + step * grow
    second = step * alpha
    for copy in copies:
        copy.wait()
    for b in range(NB):
        if b < NIN:
            r_b, z_b, q_b, w_b, v_b = load[:, lanes(b)], zi[b], y[b], wi[b], v[b]
        else:
            f = b - NIN
            r_b, z_b, q_b, w_b = rf[f], zf[f], qf[f], wf[f]
            v_b = v[b] + (in0, in1, in2, in3)[f][...]
        sol_ref[0, :, lanes(b)] = first * z_b - second * w_b
        res_ref[0, :, lanes(b)] = r_b - first * q_b + second * v_b


def f32(*shape):
    return jax.ShapeDtypeStruct(shape, F32)


def bf16(*shape):
    return jax.ShapeDtypeStruct(shape, BF16)


SMEM = pl.BlockSpec(memory_space=pltpu.SMEM)
VMEM = pl.BlockSpec(memory_space=pltpu.VMEM)
HBM = pl.BlockSpec(memory_space=pltpu.HBM)


def call(body, name, outs, specs, *args, scratch=(), copies=0):
    scratch = [pltpu.VMEM(shape, F32) if isinstance(shape, tuple) else shape for shape in scratch]
    if copies:
        scratch.append(pltpu.SemaphoreType.DMA((copies,)))
    args = [
        pltpu.with_memory_space_constraint(arg, pltpu.HBM) if spec is HBM else arg
        for arg, spec in zip(args, specs, strict=True)
    ]
    return pl.pallas_call(
        body,
        name=name,
        out_shape=outs,
        in_specs=specs,
        out_specs=[VMEM] * len(outs),
        scratch_shapes=scratch,
        compiler_params=pltpu.CompilerParams(vmem_limit_bytes=16 << 20),
    )(*args)


def on_device(
    load_vector, matrix_tiles, tile_cols, interior_inv, schur_inv, coarse_basis, coarse_inv,
    row_map, face_link, coarse_id,
):
    cols = tile_cols.T
    line = lax.axis_size("gz")
    devices = line * lax.axis_size("gy") * lax.axis_size("gx")
    depth_z = line.bit_length() - 1
    depth_y = lax.axis_size("gy").bit_length() - 1
    masks = [1, 2, 1 << depth_z, 1 << (depth_z + depth_y)]

    def trade(value, mask):
        return lax.ppermute(value, AXES, [(i, i ^ mask) for i in range(devices)])

    def trade_faces(faces):
        return [trade(face, mask) for face, mask in zip(faces, masks)]

    def trade_line(value):
        return [trade(value, mask) for mask in range(1, line)]

    coarse_all = lax.all_gather(coarse_inv[0], "gz", axis=0)
    inside = (NIN, NRHS, BS)
    around = (NF, NRHS, BS)
    every = (NB, NRHS, BS)
    block, face, small, side = f32(*inside), f32(*around), f32(NRHS, BS), f32(NRHS + 8, BS)
    nf = NF * BS
    width = line * CB * CW
    target, column, weight, *sides = call(
        prepare_body, "prepare", [f32(8, BS), f32(BS, BS), f32(2 * NF, BS)] + [side] * NF, [HBM] * 4,
        load_vector, row_map, coarse_id, face_link,
        scratch=[pltpu.SMEM((1, CB), jnp.int32), pltpu.SMEM((1, NF), jnp.int32),
                 pltpu.VMEM((1, NF, BS), jnp.int32), (NRHS, nf)],
        copies=4,
    )
    came = trade_faces(sides)

    def inside_solve(x, stage):
        flat = stage == "load"
        outs = [block, small, bf16(nf, nf), bf16(nf, nf), bf16(BS, nf), bf16(BS, nf)]
        scratch = [(NIN, BS, BS), (BS, NL), (nf, nf)] + [(NRHS, NIN * BS)] * flat
        return call(
            lambda *refs: interior_body(*refs, flat=flat), "interior_" + stage, outs,
            [HBM if flat else VMEM] + [HBM] * 3, x, interior_inv, coarse_basis, schur_inv,
            scratch=scratch, copies=4,
        )

    inner, part, *mats = inside_solve(load_vector, "load")
    r_face, outer, contrib, swap = call(
        first_faces_body, "faces_load", [face, face, side, bf16(NF, BS, BS)], [VMEM] * 15,
        *sides, *came, target, weight, *mats, part,
    )
    others = trade_line(contrib)
    high, low, back, u_face, *sends = call(
        lambda *refs: first_coarse_body(*refs, line=line), "coarse_load",
        [bf16(BS, width), bf16(BS, width), small, face] + [small] * NF, [HBM] + [VMEM] * (line + 6),
        coarse_all, column, contrib, *others, outer, *mats[2:], weight, swap,
        scratch=[(line, OCAP * CW, OCAP * CW)], copies=line,
    )

    def apply(inner, back, u_face, sends, stage):
        came = trade_faces(sends)
        wide = bf16(NF, BS, TPR * BS)
        z, acc, *wides = call(
            own_apply_body, "own_" + stage, [block, f32(*every), wide, wide],
            [VMEM, VMEM, HBM, VMEM, HBM, SMEM],
            inner, back, coarse_basis, u_face, matrix_tiles, cols,
            scratch=[(BS, NIN * BS), (NB, TPR, BS, BS)], copies=1 + NB,
        )
        y, z_face, *sends = call(
            face_apply_body, "face_" + stage, [f32(*every), face] + [small] * NF,
            [VMEM] * 8 + [SMEM, VMEM],
            acc, *came, u_face, *wides, cols, swap,
        )
        return z, z_face, y, sends

    z, z_face, y, sends = apply(inner, back, u_face, sends, "first")
    came = trade_faces(sends)
    inner, part, *mats = inside_solve(y, "image")
    q_face, outer, contrib = call(
        next_faces_body, "faces_image", [face, face, small], [VMEM] * 11,
        y, *came, weight, *mats, part,
    )
    others = trade_line(contrib)
    back, u_face, *sends = call(
        lambda *refs: next_coarse_body(*refs, line=line), "coarse_image",
        [small, face] + [small] * NF, [VMEM] * (line + 7),
        contrib, *others, high, low, outer, *mats[2:], weight, swap,
    )
    w, w_face, v, sends = apply(inner, back, u_face, sends, "second")
    came = trade_faces(sends)
    (dots,) = call(
        dots_body, "dots", [f32(devices, 2, BS)], [HBM] + [VMEM] * 6,
        load_vector, z, z_face, y, w, w_face, v, scratch=[(NRHS, NL)], copies=1,
    )
    spread = lax.all_to_all(dots, AXES, 0, 0)
    out = f32(1, NRHS, NL)
    return tuple(
        call(
            final_body, "combine", [out, out], [VMEM] * 5 + [HBM] + [VMEM] * 8,
            spread, *came, load_vector, r_face, z, z_face, y, q_face, w, w_face, v,
            scratch=[(NRHS, NIN * BS)], copies=1,
        )
    )


def solution(mesh):
    lead = P(AXES, None, None)
    flat = P(AXES, None)
    in_specs = (lead, P(AXES, None, None, None), flat, lead, lead, lead, lead, lead, flat, flat)
    return jax.shard_map(
        on_device, mesh=mesh, in_specs=in_specs, out_specs=(lead, lead), check_vma=False
    )
```

```python
import jax
import jax.numpy as jnp
from jax import lax
from jax.experimental import pallas as pl
from jax.experimental.pallas import tpu as pltpu
from jax.sharding import PartitionSpec as P

BS = 128
NIN = 12
NF = 4
NRHS = 32
CW = 32
CB = 4
OCAP = 8
SCAP = 2
AHEAD = 4
NB = 16
TPR = 7
NL = 2048
AXES = ("gx", "gy", "gz")
F32 = jnp.float32
BF16 = jnp.bfloat16
NN = (((1,), (0,)), ((), ()))
NT = (((1,), (1,)), ((), ()))


def mm(left, right, dims=NN):
    return lax.dot_general(left, right, dims, preferred_element_type=F32)


def halves(value):
    high = value.astype(BF16)
    return high, (value - high.astype(F32)).astype(BF16)


def dot_halves(left, right, dims=NN):
    (lh, ll), (rh, rl) = left, right
    rows = lh.shape[0]
    both = mm(jnp.concatenate([lh, ll], axis=0), rh, dims)
    return both[:rows] + both[rows:] + mm(lh, rl, dims)


def select_lanes(value, onehot):
    rows = value.shape[0]
    high, rest = halves(value)
    low = (value - high.astype(F32) - rest.astype(F32)).astype(BF16)
    out = mm(jnp.concatenate([high, rest, low], axis=0), onehot)
    return out[:rows] + out[rows : 2 * rows] + out[2 * rows :]


def lanes(block):
    return slice(block * BS, (block + 1) * BS)


def start_all(sems, *pairs):
    copies = [pltpu.make_async_copy(src, dst, sems.at[k]) for k, (src, dst) in enumerate(pairs)]
    for copy in copies:
        copy.start()
    return copies


def prepare_body(
    load_ref, map_ref, id_ref, link_ref, target_ref, column_ref, weight_ref, side0, side1, side2, side3,
    ids, links, maps, faces, sems,
):
    copies = start_all(
        sems,
        (id_ref, ids),
        (link_ref, links),
        (map_ref, maps),
        (load_ref.at[0, :, NIN * BS :], faces),
    )
    copies[0].wait()
    along = lax.broadcasted_iota(jnp.int32, (8, BS), 1)
    down = lax.broadcasted_iota(jnp.int32, (BS, BS), 0)
    target, place = along % CW, along % CW
    column, spot = down % CW, down % CW
    for b in range(CB):
        start = ids[0, b] * CW
        before = jnp.int32(0)
        for other in range(b):
            before = before + jnp.where(ids[0, other] // OCAP == ids[0, b] // OCAP, CW, 0)
        target = jnp.where(along // CW == b, target + start, target)
        place = jnp.where(along // CW == b, place + before, place)
        column = jnp.where(down // CW == b, column + start, column)
        spot = jnp.where(down // CW == b, spot + before, spot)
    line = lax.broadcasted_iota(jnp.int32, (8, BS), 0)
    target = jnp.where(line == 1, place, target).astype(F32)
    target_ref[...] = target
    column_ref[0] = column
    column_ref[1] = spot
    copies[1].wait()
    for r in range(NF):
        link = jnp.full((1, BS), links[0, r], jnp.int32).astype(F32)
        weight_ref[r : r + 1, :] = 1.0 - 0.5 * link
        weight_ref[NF + r : NF + r + 1, :] = link
    copies[2].wait()
    copies[3].wait()
    for r, out in enumerate((side0, side1, side2, side3)):
        out[:NRHS, :] = faces[:, lanes(r)]
        out[NRHS : NRHS + 8, :] = jnp.broadcast_to(maps[0, r : r + 1, :], (8, BS)).astype(F32)
        out[NRHS + 8 :, :] = target


def interior_body(
    x_ref, inv_ref, basis_ref, schur_ref,
    *rest, flat,
):
    if flat:
        coarse_ref, *rest = rest
    inner_ref, part_ref, schur_high, schur_low, basis_high, basis_low, *scratch = rest
    if flat:
        coarse_parts, *scratch = scratch
    inv, basis, schur = scratch[:3]
    sems = scratch[-1]
    pairs = [(inv_ref, inv), (basis_ref.at[0], basis), (schur_ref.at[0], schur)]
    if flat:
        pairs.append((x_ref.at[0, :, : NIN * BS], scratch[3]))
        pairs.append((coarse_ref.at[0], scratch[4]))
    copies = start_all(sems, *pairs)
    if flat:
        copies[3].wait()
    copies[0].wait()
    pieces = []
    for b in range(NIN):
        xb = halves(scratch[3][:, lanes(b)] if flat else x_ref[b])
        pieces.append(xb)
        inner_ref[b] = dot_halves(xb, halves(inv[b]))
    cat = tuple(jnp.concatenate([p[h] for p in pieces], axis=1) for h in range(2))
    copies[1].wait()
    part_ref[...] = dot_halves(cat, halves(basis[:, : NIN * BS]), NT)
    basis_high[...], basis_low[...] = halves(basis[:, NIN * BS :])
    copies[2].wait()
    schur_high[...], schur_low[...] = halves(schur[...])
    if flat:
        copies[4].wait()
        value = scratch[4][...]
        for k in range(3):
            coarse_parts[k] = value.astype(BF16)
            value = value - coarse_parts[k].astype(F32)


def face_solve(faces, mats, weight_ref, part_ref, outer_ref, contrib_ref):
    schur_high, schur_low, basis_high, basis_low = mats
    scaled = halves(
        jnp.concatenate([faces[r] * weight_ref[r : r + 1, :] for r in range(NF)], axis=1)
    )
    contrib_ref[:NRHS, :] = part_ref[...] + dot_halves(
        scaled, (basis_high[...], basis_low[...]), NT
    )
    outer = dot_halves(scaled, (schur_high[...], schur_low[...]))
    for r in range(NF):
        outer_ref[r] = outer[:, lanes(r)]


def first_faces_body(
    own0, own1, own2, own3, in0, in1, in2, in3, target_ref, weight_ref,
    schur_high, schur_low, basis_high, basis_low, part_ref, coarse_ref, *rest, line,
):
    targets = [target_ref[...], in0[NRHS + 8 :, :], in1[NRHS + 8 :, :]] + [
        ref[...] for ref in rest[: line - 3]
    ]
    face_ref, outer_ref, contrib_ref, swap_ref, all_ref, rows_ref, *sides = rest[line - 3 :]
    faces = []
    rows = lax.broadcasted_iota(jnp.int32, (BS, BS), 0).astype(F32)
    for r, (own, inc) in enumerate(zip((own0, own1, own2, own3), (in0, in1, in2, in3))):
        mine = (rows == own[NRHS : NRHS + 1, :]).astype(F32).astype(BF16)
        theirs = (rows == inc[NRHS : NRHS + 1, :]).astype(F32).astype(BF16)
        link = weight_ref[NF + r : NF + r + 1, :]
        swap_ref[r] = (mm(mine, theirs, NT) * link).astype(BF16)
        came = select_lanes(inc[:NRHS, :], (mm(theirs, mine, NT) * link).astype(BF16))
        faces.append(own[:NRHS, :] + came)
        face_ref[r] = faces[-1]
    mats = (schur_high, schur_low, basis_high, basis_low)
    face_solve(faces, mats, weight_ref, part_ref, outer_ref, contrib_ref)
    here = lax.axis_index("gz")
    own = OCAP * CW
    slots = lax.broadcasted_iota(jnp.int32, (SCAP * CW, BS), 0)
    places = lax.broadcasted_iota(jnp.int32, (own, BS), 0)
    all_ref[...] = jnp.concatenate([t[0:1, :] for t in targets], axis=1)
    for m, target in enumerate(targets):
        goal = target.astype(jnp.int32)
        into = (slots == goal[1:2, :]).astype(F32).astype(BF16)
        out_of = (places == goal[0:1, :] - here * own).astype(F32).astype(BF16)
        take = mm(into, out_of, NT).astype(BF16)
        rows = mm(take, coarse_ref[0]) + mm(take, coarse_ref[1]) + mm(take, coarse_ref[2])
        if m == 0:
            rows_ref[: SCAP * CW, :] = rows[:, :BS]
            rows_ref[SCAP * CW :, :] = rows[:, BS:]
        else:
            sides[m - 1][:NRHS, :] = contrib_ref[...]
            sides[m - 1][NRHS : NRHS + SCAP * CW, :] = rows[:, :BS]
            sides[m - 1][NRHS + SCAP * CW :, :] = rows[:, BS:]


def next_faces_body(
    y_ref, in0, in1, in2, in3, weight_ref, schur_high, schur_low, basis_high, basis_low, part_ref,
    face_ref, outer_ref, contrib_ref,
):
    faces = []
    for r, inc in enumerate((in0, in1, in2, in3)):
        faces.append(y_ref[NIN + r] + inc[...])
        face_ref[r] = faces[-1]
    mats = (schur_high, schur_low, basis_high, basis_low)
    face_solve(faces, mats, weight_ref, part_ref, outer_ref, contrib_ref)


def finish(back, outer_ref, basis, weight_ref, swap_ref, back_ref, face_ref, outs):
    back_ref[...] = back
    corr = dot_halves(halves(back), basis)
    for r in range(NF):
        value = weight_ref[r : r + 1, :] * (outer_ref[r] + corr[:, lanes(r)])
        face_ref[r] = value
        outs[r][...] = select_lanes(value, swap_ref[r])


def owner_rows(side, m):
    first = NRHS if m else 0
    return jnp.concatenate(
        [side[first : first + SCAP * CW, :], side[first + SCAP * CW :, :]], axis=1
    )


def pick_of(all_ref, owner):
    rows = lax.broadcasted_iota(jnp.int32, (OCAP * CW, all_ref.shape[1]), 0)
    return (rows + owner * (OCAP * CW) == all_ref[...].astype(jnp.int32)).astype(F32).astype(BF16)


def first_coarse_body(own_ref, rows_ref, all_ref, target_ref, *refs, line):
    sides = (rows_ref,) + refs[: line - 1]
    outer_ref, basis_high, basis_low, weight_ref, swap_ref, back_ref, face_ref, *outs = refs[line - 1 :]
    here = lax.axis_index("gz")
    contribs = halves(jnp.concatenate([own_ref[...]] + [s[:NRHS, :] for s in sides[1:]], axis=1))
    stack = jnp.concatenate(contribs, axis=0)
    slots = lax.broadcasted_iota(jnp.int32, (SCAP * CW, BS), 0)
    goal = target_ref[...].astype(jnp.int32)
    back = jnp.zeros((NRHS, BS), F32)
    for m in range(line):
        owner = jnp.bitwise_xor(here, m)
        both = mm(stack, pick_of(all_ref, owner), NT)
        solved = dot_halves(halves(both[:NRHS] + both[NRHS:]), halves(owner_rows(sides[m], m)), NT)
        mine = (slots == goal[1:2, :]) & (goal[0:1, :] // (OCAP * CW) == owner)
        back = back + select_lanes(solved, mine.astype(F32).astype(BF16))
    finish(back, outer_ref, (basis_high[...], basis_low[...]), weight_ref, swap_ref, back_ref, face_ref, outs)


def table_body(rows_ref, all_ref, column_ref, *refs, line):
    sides = (rows_ref,) + refs[: line - 1]
    high_ref, low_ref = refs[line - 1 :]
    here = lax.axis_index("gz")
    slots = lax.broadcasted_iota(jnp.int32, (BS, BS), 1)
    table = jnp.zeros((2 * BS, all_ref.shape[1]), F32)
    for m in range(line):
        owner = jnp.bitwise_xor(here, m)
        mine = (slots == column_ref[1]) & (column_ref[0] // (OCAP * CW) == owner)
        take = mine.astype(F32).astype(BF16)[:, : SCAP * CW]
        high, low = halves(owner_rows(sides[m], m))
        both = jnp.concatenate([mm(take, high).astype(BF16), mm(take, low).astype(BF16)], axis=0)
        table = table + mm(both, pick_of(all_ref, owner))
    high_ref[...] = table[:BS].astype(BF16)
    low_ref[...] = table[BS:].astype(BF16)


def next_coarse_body(*refs, line):
    contribs = [ref[...] for ref in refs[:line]]
    high_ref, low_ref, outer_ref, basis_high, basis_low, weight_ref, swap_ref = refs[line : 7 + line]
    back_ref, face_ref = refs[7 + line : 9 + line]
    table = (high_ref[...], low_ref[...])
    back = dot_halves(halves(jnp.concatenate(contribs, axis=1)), table, NT)
    finish(back, outer_ref, (basis_high[...], basis_low[...]), weight_ref, swap_ref, back_ref, face_ref,
           refs[9 + line :])


def add_row(x, i, wide, cols_ref, acc_ref):
    out = dot_halves(halves(x), wide)
    places = [cols_ref[t, i] for t in range(TPR)]
    before = [acc_ref[place] for place in places]
    for t in range(TPR):
        acc_ref[places[t]] = before[t] + out[:, lanes(t)]


def own_apply_body(
    inner_ref, back_ref, basis_ref, face_ref, tiles_ref, cols_ref, z_ref, acc_ref, wide_high, wide_low,
    basis, tiles, sems,
):
    pairs = [(basis_ref.at[0, :, : NIN * BS], basis)]
    pairs += [(tiles_ref.at[i], tiles.at[i]) for i in range(NB)]
    copies = [pltpu.make_async_copy(src, dst, sems.at[k]) for k, (src, dst) in enumerate(pairs)]
    for copy in copies[: 1 + AHEAD]:
        copy.start()
    acc_ref[...] = jnp.zeros_like(acc_ref)
    back = halves(back_ref[...])
    copies[0].wait()
    for b in range(NIN):
        z_ref[b] = inner_ref[b] + dot_halves(back, halves(basis[:, lanes(b)]))
    for i in range(NB):
        copies[1 + i].wait()
        if i + AHEAD < NB:
            copies[1 + i + AHEAD].start()
        wide = halves(jnp.concatenate([tiles[i, t] for t in range(TPR)], axis=1))
        if i >= NIN:
            wide_high[i - NIN], wide_low[i - NIN] = wide
        add_row(z_ref[i] if i < NIN else face_ref[i - NIN], i, wide, cols_ref, acc_ref)


def face_apply_body(
    acc_ref, in0, in1, in2, in3, face_ref, wide_high, wide_low, cols_ref, swap_ref,
    y_ref, z_ref, out0, out1, out2, out3,
):
    y_ref[...] = acc_ref[...]
    for r, inc in enumerate((in0, in1, in2, in3)):
        came = inc[...]
        z_ref[r] = face_ref[r] + came
        add_row(came, NIN + r, (wide_high[r], wide_low[r]), cols_ref, y_ref)
    for r, out in enumerate((out0, out1, out2, out3)):
        out[...] = select_lanes(y_ref[NIN + r], swap_ref[r])


def dots_body(load_hbm, zi, zf, y, wi, wf_ref, v_ref, out_ref, load_ref, sems):
    (copy,) = start_all(sems, (load_hbm.at[0], load_ref))
    copy.wait()
    sums = [jnp.zeros((NRHS, BS), F32) for _ in range(6)]
    for b in range(NB):
        load = load_ref[:, lanes(b)]
        z = zi[b] if b < NIN else zf[b - NIN]
        w = wi[b] if b < NIN else wf_ref[b - NIN]
        q, v = y[b], v_ref[b]
        for k, (left, right) in enumerate(((load, z), (z, q), (load, w), (q, w), (z, v), (w, v))):
            sums[k] = sums[k] + left * right
    place = lax.broadcasted_iota(jnp.int32, (NRHS, BS), 1)
    case = lax.broadcasted_iota(jnp.int32, (NRHS, BS), 0)
    for row in range(2):
        total = jnp.zeros((NRHS, BS), F32)
        for k in range(4 * row, min(4 * row + 4, 6)):
            column = jnp.sum(sums[k], axis=1, keepdims=True)
            total = total + jnp.where(place == case + NRHS * (k % 4), column, 0.0)
        total = jnp.sum(total, axis=0, keepdims=True)
        out_ref[:, row : row + 1, :] = jnp.broadcast_to(total[None], (out_ref.shape[0], 1, BS))


def final_body(
    dots_ref, in0, in1, in2, in3, load_h, rf, zi, zf, y, qf, wi, wf, v, sol_ref, res_ref, load, sems,
):
    copies = start_all(sems, (load_h.at[0, :, : NIN * BS], load))
    place = lax.broadcasted_iota(jnp.int32, (NRHS, BS), 1)
    case = lax.broadcasted_iota(jnp.int32, (NRHS, BS), 0)
    total = jnp.sum(dots_ref[...], axis=0)
    rz, zq, rw, qw, zv, wv = [
        jnp.sum(
            jnp.where(place == case + NRHS * (k % 4), total[k // 4 : k // 4 + 1, :], 0.0),
            axis=1,
            keepdims=True,
        )
        for k in range(6)
    ]
    alpha = rz / zq
    rho = rz - alpha * (rw + zq) + alpha * alpha * qw
    grow = 1.0 + rho / rz
    curve = grow * grow * zq - grow * alpha * (zv + qw) + alpha * alpha * wv
    step = rho / curve
    first = alpha + step * grow
    second = step * alpha
    for copy in copies:
        copy.wait()
    for b in range(NB):
        if b < NIN:
            r_b, z_b, q_b, w_b, v_b = load[:, lanes(b)], zi[b], y[b], wi[b], v[b]
        else:
            f = b - NIN
            r_b, z_b, q_b, w_b = rf[f], zf[f], qf[f], wf[f]
            v_b = v[b] + (in0, in1, in2, in3)[f][...]
        sol_ref[0, :, lanes(b)] = first * z_b - second * w_b
        res_ref[0, :, lanes(b)] = r_b - first * q_b + second * v_b


def f32(*shape):
    return jax.ShapeDtypeStruct(shape, F32)


def bf16(*shape):
    return jax.ShapeDtypeStruct(shape, BF16)


SMEM = pl.BlockSpec(memory_space=pltpu.SMEM)
VMEM = pl.BlockSpec(memory_space=pltpu.VMEM)
HBM = pl.BlockSpec(memory_space=pltpu.HBM)


def call(body, name, outs, specs, *args, scratch=(), copies=0):
    scratch = [pltpu.VMEM(shape, F32) if isinstance(shape, tuple) else shape for shape in scratch]
    if copies:
        scratch.append(pltpu.SemaphoreType.DMA((copies,)))
    args = [
        pltpu.with_memory_space_constraint(arg, pltpu.HBM) if spec is HBM else arg
        for arg, spec in zip(args, specs, strict=True)
    ]
    return pl.pallas_call(
        body,
        name=name,
        out_shape=outs,
        in_specs=specs,
        out_specs=[VMEM] * len(outs),
        scratch_shapes=scratch,
        compiler_params=pltpu.CompilerParams(vmem_limit_bytes=16 << 20),
    )(*args)


def on_device(
    load_vector, matrix_tiles, tile_cols, interior_inv, schur_inv, coarse_basis, coarse_inv,
    row_map, face_link, coarse_id,
):
    cols = tile_cols.T
    line = lax.axis_size("gz")
    devices = line * lax.axis_size("gy") * lax.axis_size("gx")
    depth_z = line.bit_length() - 1
    depth_y = lax.axis_size("gy").bit_length() - 1
    masks = [1, 2, 1 << depth_z, 1 << (depth_z + depth_y)]

    def trade(value, mask):
        return lax.ppermute(value, AXES, [(i, i ^ mask) for i in range(devices)])

    def trade_faces(faces):
        return [trade(face, mask) for face, mask in zip(faces, masks)]

    def trade_line(value):
        return [trade(value, mask) for mask in range(1, line)]

    inside = (NIN, NRHS, BS)
    around = (NF, NRHS, BS)
    every = (NB, NRHS, BS)
    block, face, small, side = f32(*inside), f32(*around), f32(NRHS, BS), f32(NRHS + 16, BS)
    nf = NF * BS
    width = line * CB * CW
    target, column, weight, *sides = call(
        prepare_body, "prepare", [f32(8, BS), jax.ShapeDtypeStruct((2, BS, BS), jnp.int32), f32(2 * NF, BS)] + [side] * NF, [HBM] * 4,
        load_vector, row_map, coarse_id, face_link,
        scratch=[pltpu.SMEM((1, CB), jnp.int32), pltpu.SMEM((1, NF), jnp.int32),
                 pltpu.VMEM((1, NF, BS), jnp.int32), (NRHS, nf)],
        copies=4,
    )
    came = trade_faces(sides)
    far = [trade(target, mask) for mask in range(3, line)]

    def inside_solve(x, stage):
        flat = stage == "load"
        outs = [block, small, bf16(nf, nf), bf16(nf, nf), bf16(BS, nf), bf16(BS, nf)]
        scratch = [(NIN, BS, BS), (BS, NL), (nf, nf)]
        args = [x, interior_inv, coarse_basis, schur_inv]
        if flat:
            own = OCAP * CW
            outs.append(bf16(3, own, own))
            scratch += [(NRHS, NIN * BS), (own, own)]
            args.append(coarse_inv)
        return call(
            lambda *refs: interior_body(*refs, flat=flat), "interior_" + stage, outs,
            [HBM if flat else VMEM] + [HBM] * (len(args) - 1), *args, scratch=scratch, copies=5,
        )

    inner, part, *mats, coarse_parts = inside_solve(load_vector, "load")
    width = line * CB * CW
    half = 2 * SCAP * CW
    r_face, outer, contrib, swap, targets, rows, *sides = call(
        lambda *refs: first_faces_body(*refs, line=line), "faces_load",
        [face, face, small, bf16(NF, BS, BS), f32(1, width), f32(half, BS)]
        + [f32(NRHS + half, BS)] * (line - 1),
        [VMEM] * (13 + line),
        *sides, *came, target, weight, *mats, part, coarse_parts, *far,
    )
    others = [trade(value, mask) for value, mask in zip(sides, range(1, line))]
    back, u_face, *sends = call(
        lambda *refs: first_coarse_body(*refs, line=line), "coarse_load",
        [small, face] + [small] * NF, [VMEM] * (line + 8),
        contrib, rows, targets, target, *others, outer, *mats[2:], weight, swap,
    )

    def apply(inner, back, u_face, sends, stage):
        came = trade_faces(sends)
        wide = bf16(NF, BS, TPR * BS)
        z, acc, *wides = call(
            own_apply_body, "own_" + stage, [block, f32(*every), wide, wide],
            [VMEM, VMEM, HBM, VMEM, HBM, SMEM],
            inner, back, coarse_basis, u_face, matrix_tiles, cols,
            scratch=[(BS, NIN * BS), (NB, TPR, BS, BS)], copies=1 + NB,
        )
        y, z_face, *sends = call(
            face_apply_body, "face_" + stage, [f32(*every), face] + [small] * NF,
            [VMEM] * 8 + [SMEM, VMEM],
            acc, *came, u_face, *wides, cols, swap,
        )
        return z, z_face, y, sends

    z, z_face, y, sends = apply(inner, back, u_face, sends, "first")
    came = trade_faces(sends)
    inner, part, *mats = inside_solve(y, "image")
    high, low = call(
        lambda *refs: table_body(*refs, line=line), "table", [bf16(BS, width), bf16(BS, width)],
        [VMEM] * (line + 2), rows, targets, column, *others,
    )
    q_face, outer, contrib = call(
        next_faces_body, "faces_image", [face, face, small], [VMEM] * 11,
        y, *came, weight, *mats, part,
    )
    others = trade_line(contrib)
    back, u_face, *sends = call(
        lambda *refs: next_coarse_body(*refs, line=line), "coarse_image",
        [small, face] + [small] * NF, [VMEM] * (line + 7),
        contrib, *others, high, low, outer, *mats[2:], weight, swap,
    )
    w, w_face, v, sends = apply(inner, back, u_face, sends, "second")
    came = trade_faces(sends)
    (dots,) = call(
        dots_body, "dots", [f32(devices, 2, BS)], [HBM] + [VMEM] * 6,
        load_vector, z, z_face, y, w, w_face, v, scratch=[(NRHS, NL)], copies=1,
    )
    spread = lax.all_to_all(dots, AXES, 0, 0)
    out = f32(1, NRHS, NL)
    return tuple(
        call(
            final_body, "combine", [out, out], [VMEM] * 5 + [HBM] + [VMEM] * 8,
            spread, *came, load_vector, r_face, z, z_face, y, q_face, w, w_face, v,
            scratch=[(NRHS, NIN * BS)], copies=1,
        )
    )


def solution(mesh):
    lead = P(AXES, None, None)
    flat = P(AXES, None)
    in_specs = (lead, P(AXES, None, None, None), flat, lead, lead, lead, lead, lead, flat, flat)
    return jax.shard_map(
        on_device, mesh=mesh, in_specs=in_specs, out_specs=(lead, lead), check_vma=False
    )
```

```python
import jax
import jax.numpy as jnp
from jax import lax
from jax.experimental import pallas as pl
from jax.experimental.pallas import tpu as pltpu
from jax.sharding import PartitionSpec as P

BS = 128
NIN = 12
NF = 4
NRHS = 32
CW = 32
CB = 4
OCAP = 8
SCAP = 2
CHUNKS = (4, 4, 3, 1)
NB = 16
TPR = 7
NL = 2048
AXES = ("gx", "gy", "gz")
F32 = jnp.float32
BF16 = jnp.bfloat16
NN = (((1,), (0,)), ((), ()))
NT = (((1,), (1,)), ((), ()))


def mm(left, right, dims=NN):
    return lax.dot_general(left, right, dims, preferred_element_type=F32)


def halves(value):
    high = value.astype(BF16)
    return high, (value - high.astype(F32)).astype(BF16)


def dot_halves(left, right, dims=NN):
    (lh, ll), (rh, rl) = left, right
    rows = lh.shape[0]
    both = mm(jnp.concatenate([lh, ll], axis=0), rh, dims)
    return both[:rows] + both[rows:] + mm(lh, rl, dims)


def select_lanes(value, onehot):
    rows = value.shape[0]
    high, rest = halves(value)
    low = (value - high.astype(F32) - rest.astype(F32)).astype(BF16)
    out = mm(jnp.concatenate([high, rest, low], axis=0), onehot)
    return out[:rows] + out[rows : 2 * rows] + out[2 * rows :]


def lanes(block):
    return slice(block * BS, (block + 1) * BS)


def start_all(sems, *pairs):
    copies = [pltpu.make_async_copy(src, dst, sems.at[k]) for k, (src, dst) in enumerate(pairs)]
    for copy in copies:
        copy.start()
    return copies


def prepare_body(
    load_ref, map_ref, id_ref, link_ref, target_ref, column_ref, weight_ref, side0, side1, side2, side3,
    ids, links, maps, faces, sems,
):
    copies = start_all(
        sems,
        (id_ref, ids),
        (link_ref, links),
        (map_ref, maps),
        (load_ref.at[0, :, NIN * BS :], faces),
    )
    copies[0].wait()
    along = lax.broadcasted_iota(jnp.int32, (8, BS), 1)
    down = lax.broadcasted_iota(jnp.int32, (BS, BS), 0)
    target, place = along % CW, along % CW
    column, spot = down % CW, down % CW
    for b in range(CB):
        start = ids[0, b] * CW
        before = jnp.int32(0)
        for other in range(b):
            before = before + jnp.where(ids[0, other] // OCAP == ids[0, b] // OCAP, CW, 0)
        target = jnp.where(along // CW == b, target + start, target)
        place = jnp.where(along // CW == b, place + before, place)
        column = jnp.where(down // CW == b, column + start, column)
        spot = jnp.where(down // CW == b, spot + before, spot)
    line = lax.broadcasted_iota(jnp.int32, (8, BS), 0)
    target = jnp.where(line == 1, place, target).astype(F32)
    target_ref[...] = target
    column_ref[0] = column
    column_ref[1] = spot
    copies[1].wait()
    for r in range(NF):
        link = jnp.full((1, BS), links[0, r], jnp.int32).astype(F32)
        weight_ref[r : r + 1, :] = 1.0 - 0.5 * link
        weight_ref[NF + r : NF + r + 1, :] = link
    copies[2].wait()
    copies[3].wait()
    for r, out in enumerate((side0, side1, side2, side3)):
        out[:NRHS, :] = faces[:, lanes(r)]
        out[NRHS : NRHS + 8, :] = jnp.broadcast_to(maps[0, r : r + 1, :], (8, BS)).astype(F32)
        out[NRHS + 8 :, :] = target


def face_rows(acc_ref, face_ref, tiles, cols, out_ref, spare_ref):
    spare_ref[...] = acc_ref[...]
    for r in range(NF):
        add_row(face_ref[r], NIN + r, tiles[r], cols, spare_ref)
    out_ref[...] = spare_ref[:NIN]


def solve_inside(x_of, inv, basis, schur, copies, inner_ref, part_ref, mats):
    schur_high, schur_low, basis_high, basis_low = mats
    copies[0].wait()
    pieces = []
    for b in range(NIN):
        xb = halves(x_of(b))
        pieces.append(xb)
        inner_ref[b] = dot_halves(xb, halves(inv[b]))
    cat = tuple(jnp.concatenate([p[h] for p in pieces], axis=1) for h in range(2))
    copies[1].wait()
    part_ref[...] = dot_halves(cat, halves(basis[:, : NIN * BS]), NT)
    basis_high[...], basis_low[...] = halves(basis[:, NIN * BS :])
    copies[2].wait()
    schur_high[...], schur_low[...] = halves(schur[...])


def load_inside_body(
    x_ref, inv_ref, basis_ref, schur_ref, coarse_ref,
    inner_ref, part_ref, schur_high, schur_low, basis_high, basis_low, coarse_parts,
    inv, basis, schur, x, coarse, sems,
):
    copies = start_all(
        sems, (inv_ref, inv), (basis_ref.at[0], basis), (schur_ref.at[0], schur),
        (x_ref.at[0, :, : NIN * BS], x), (coarse_ref.at[0], coarse),
    )
    copies[3].wait()
    mats = (schur_high, schur_low, basis_high, basis_low)
    solve_inside(lambda b: x[:, lanes(b)], inv, basis, schur, copies, inner_ref, part_ref, mats)
    copies[4].wait()
    value = coarse[...]
    for k in range(3):
        coarse_parts[k] = value.astype(BF16)
        value = value - coarse_parts[k].astype(F32)


def image_inside_body(
    acc_ref, face_ref, cols_ref, tiles_ref, inv_ref, basis_ref, schur_ref,
    y_ref, inner_ref, part_ref, schur_high, schur_low, basis_high, basis_low,
    inv, basis, schur, tiles, spare, cols, sems,
):
    copies = start_all(
        sems, (inv_ref, inv), (basis_ref.at[0], basis), (schur_ref.at[0], schur),
        (cols_ref, cols), (tiles_ref.at[NIN:], tiles),
    )
    copies[3].wait()
    copies[4].wait()
    face_rows(acc_ref, face_ref, [wide_of(tiles, r) for r in range(NF)], cols, y_ref, spare)
    mats = (schur_high, schur_low, basis_high, basis_low)
    solve_inside(lambda b: y_ref[b], inv, basis, schur, copies, inner_ref, part_ref, mats)


def last_image_body(acc_ref, face_ref, cols_ref, tiles_ref, y_ref, tiles, spare, cols, sems):
    copies = start_all(sems, (cols_ref, cols), (tiles_ref.at[NIN:], tiles))
    for copy in copies:
        copy.wait()
    face_rows(acc_ref, face_ref, [wide_of(tiles, r) for r in range(NF)], cols, y_ref, spare)


def face_block_body(tiles_ref, cols_ref, high_ref, low_ref, tiles, cols, sems):
    copies = start_all(sems, (cols_ref, cols), (tiles_ref.at[NIN:], tiles))
    high_ref[...] = jnp.zeros_like(high_ref)
    low_ref[...] = jnp.zeros_like(low_ref)
    for copy in copies:
        copy.wait()
    for r in range(NF):
        for t in range(TPR):
            place = cols[t, NIN + r] - NIN

            @pl.when(place >= 0)
            def _(r=r, t=t, place=place):
                high_ref[r, place], low_ref[r, place] = halves(tiles[r, t])


def face_solve(faces, mats, weight_ref, part_ref, outer_ref, contrib_ref):
    schur_high, schur_low, basis_high, basis_low = mats
    scaled = halves(
        jnp.concatenate([faces[r] * weight_ref[r : r + 1, :] for r in range(NF)], axis=1)
    )
    contrib_ref[:NRHS, :] = part_ref[...] + dot_halves(
        scaled, (basis_high[...], basis_low[...]), NT
    )
    outer = dot_halves(scaled, (schur_high[...], schur_low[...]))
    for r in range(NF):
        outer_ref[r] = outer[:, lanes(r)]


def first_faces_body(
    own0, own1, own2, own3, in0, in1, in2, in3, target_ref, weight_ref,
    schur_high, schur_low, basis_high, basis_low, part_ref, coarse_ref, *rest, line,
):
    targets = [target_ref[...], in0[NRHS + 8 :, :], in1[NRHS + 8 :, :]] + [
        ref[...] for ref in rest[: line - 3]
    ]
    face_ref, outer_ref, contrib_ref, swap_ref, all_ref, rows_ref, *sides = rest[line - 3 :]
    faces = []
    rows = lax.broadcasted_iota(jnp.int32, (BS, BS), 0).astype(F32)
    for r, (own, inc) in enumerate(zip((own0, own1, own2, own3), (in0, in1, in2, in3))):
        mine = (rows == own[NRHS : NRHS + 1, :]).astype(F32).astype(BF16)
        theirs = (rows == inc[NRHS : NRHS + 1, :]).astype(F32).astype(BF16)
        link = weight_ref[NF + r : NF + r + 1, :]
        swap_ref[r] = (mm(mine, theirs, NT) * link).astype(BF16)
        came = select_lanes(inc[:NRHS, :], (mm(theirs, mine, NT) * link).astype(BF16))
        faces.append(own[:NRHS, :] + came)
        face_ref[r] = faces[-1]
    mats = (schur_high, schur_low, basis_high, basis_low)
    face_solve(faces, mats, weight_ref, part_ref, outer_ref, contrib_ref)
    here = lax.axis_index("gz")
    own = OCAP * CW
    slots = lax.broadcasted_iota(jnp.int32, (SCAP * CW, BS), 0)
    places = lax.broadcasted_iota(jnp.int32, (own, BS), 0)
    all_ref[...] = jnp.concatenate([t[0:1, :] for t in targets], axis=1)
    for m, target in enumerate(targets):
        goal = target.astype(jnp.int32)
        into = (slots == goal[1:2, :]).astype(F32).astype(BF16)
        out_of = (places == goal[0:1, :] - here * own).astype(F32).astype(BF16)
        take = mm(into, out_of, NT).astype(BF16)
        rows = mm(take, coarse_ref[0]) + mm(take, coarse_ref[1]) + mm(take, coarse_ref[2])
        if m == 0:
            rows_ref[: SCAP * CW, :] = rows[:, :BS]
            rows_ref[SCAP * CW :, :] = rows[:, BS:]
        else:
            sides[m - 1][:NRHS, :] = contrib_ref[...]
            sides[m - 1][NRHS : NRHS + SCAP * CW, :] = rows[:, :BS]
            sides[m - 1][NRHS + SCAP * CW :, :] = rows[:, BS:]


def next_faces_body(
    y_ref, in0, in1, in2, in3, weight_ref, schur_high, schur_low, basis_high, basis_low, part_ref,
    face_ref, outer_ref, contrib_ref,
):
    faces = []
    for r, inc in enumerate((in0, in1, in2, in3)):
        faces.append(y_ref[r] + inc[...])
        face_ref[r] = faces[-1]
    mats = (schur_high, schur_low, basis_high, basis_low)
    face_solve(faces, mats, weight_ref, part_ref, outer_ref, contrib_ref)


def finish(back, outer_ref, basis, weight_ref, swap_ref, back_ref, face_ref, outs):
    back_ref[...] = back
    corr = dot_halves(halves(back), basis)
    for r in range(NF):
        value = weight_ref[r : r + 1, :] * (outer_ref[r] + corr[:, lanes(r)])
        face_ref[r] = value
        outs[r][...] = select_lanes(value, swap_ref[r])


def owner_rows(side, m):
    first = NRHS if m else 0
    return jnp.concatenate(
        [side[first : first + SCAP * CW, :], side[first + SCAP * CW :, :]], axis=1
    )


def pick_of(all_ref, owner):
    rows = lax.broadcasted_iota(jnp.int32, (OCAP * CW, all_ref.shape[1]), 0)
    return (rows + owner * (OCAP * CW) == all_ref[...].astype(jnp.int32)).astype(F32).astype(BF16)


def first_coarse_body(own_ref, rows_ref, all_ref, target_ref, *refs, line):
    sides = (rows_ref,) + refs[: line - 1]
    outer_ref, basis_high, basis_low, weight_ref, swap_ref, _, back_ref, face_ref, *outs = refs[line - 1 :]
    here = lax.axis_index("gz")
    contribs = halves(jnp.concatenate([own_ref[...]] + [s[:NRHS, :] for s in sides[1:]], axis=1))
    stack = jnp.concatenate(contribs, axis=0)
    slots = lax.broadcasted_iota(jnp.int32, (SCAP * CW, BS), 0)
    goal = target_ref[...].astype(jnp.int32)
    back = jnp.zeros((NRHS, BS), F32)
    for m in range(line):
        owner = jnp.bitwise_xor(here, m)
        both = mm(stack, pick_of(all_ref, owner), NT)
        solved = dot_halves(halves(both[:NRHS] + both[NRHS:]), halves(owner_rows(sides[m], m)), NT)
        mine = (slots == goal[1:2, :]) & (goal[0:1, :] // (OCAP * CW) == owner)
        back = back + select_lanes(solved, mine.astype(F32).astype(BF16))
    finish(back, outer_ref, (basis_high[...], basis_low[...]), weight_ref, swap_ref, back_ref, face_ref, outs)


def table_body(rows_ref, all_ref, column_ref, *refs, line):
    sides = (rows_ref,) + refs[: line - 1]
    high_ref, low_ref = refs[line - 1 :]
    here = lax.axis_index("gz")
    slots = lax.broadcasted_iota(jnp.int32, (BS, BS), 1)
    table = jnp.zeros((2 * BS, all_ref.shape[1]), F32)
    for m in range(line):
        owner = jnp.bitwise_xor(here, m)
        mine = (slots == column_ref[1]) & (column_ref[0] // (OCAP * CW) == owner)
        take = mine.astype(F32).astype(BF16)[:, : SCAP * CW]
        high, low = halves(owner_rows(sides[m], m))
        both = jnp.concatenate([mm(take, high).astype(BF16), mm(take, low).astype(BF16)], axis=0)
        table = table + mm(both, pick_of(all_ref, owner))
    high_ref[...] = table[:BS].astype(BF16)
    low_ref[...] = table[BS:].astype(BF16)


def next_coarse_body(*refs, line):
    contribs = [ref[...] for ref in refs[:line]]
    high_ref, low_ref, outer_ref, basis_high, basis_low, weight_ref, swap_ref = refs[line : 7 + line]
    back_ref, face_ref = refs[7 + line : 9 + line]
    table = (high_ref[...], low_ref[...])
    back = dot_halves(halves(jnp.concatenate(contribs, axis=1)), table, NT)
    finish(back, outer_ref, (basis_high[...], basis_low[...]), weight_ref, swap_ref, back_ref, face_ref,
           refs[9 + line :])


def add_row(x, i, wide, cols_ref, acc_ref):
    out = dot_halves(halves(x), wide)
    places = [cols_ref[t, i] for t in range(TPR)]
    before = [acc_ref[place] for place in places]
    for t in range(TPR):
        acc_ref[places[t]] = before[t] + out[:, lanes(t)]


def wide_of(tiles, i):
    return halves(jnp.concatenate([tiles[i, t] for t in range(TPR)], axis=1))


def own_apply(inner_ref, back_ref, basis_ref, tiles_ref, cols_ref, z_ref, acc_ref, basis, tiles, cols, sems):
    pairs = [(cols_ref, cols), (basis_ref.at[0, :, : NIN * BS], basis)]
    first = 0
    for count in CHUNKS:
        pairs.append((tiles_ref.at[first : first + count], tiles.at[first : first + count]))
        first += count
    copies = start_all(sems, *pairs)
    acc_ref[...] = jnp.zeros_like(acc_ref)
    back = halves(back_ref[...])
    copies[0].wait()
    copies[1].wait()
    corr = dot_halves(back, halves(basis[...]))
    for b in range(NIN):
        z_ref[b] = inner_ref[b] + corr[:, lanes(b)]
    first = 0
    for k, count in enumerate(CHUNKS):
        copies[2 + k].wait()
        for i in range(first, first + count):
            add_row(z_ref[i], i, wide_of(tiles, i), cols, acc_ref)
        first += count


def first_apply_body(*refs):
    own_apply(*refs)


def pair_sums(pairs):
    return [sum(left * right for left, right in blocks) for blocks in pairs]


def second_apply_body(
    inner_ref, back_ref, basis_ref, tiles_ref, cols_ref, load_hbm, zi, zf, yi, yf,
    z_ref, acc_ref, sums_ref, load_ref, basis, tiles, load, cols, sems, more,
):
    (copy,) = start_all(more, (load_hbm.at[0], load))
    own_apply(inner_ref, back_ref, basis_ref, tiles_ref, cols_ref, z_ref, acc_ref, basis, tiles, cols, sems)
    copy.wait()
    sums = pair_sums(
        (
            [(load[:, lanes(b)], zi[b]) for b in range(NIN)]
            + [(load[:, lanes(NIN + r)], zf[r]) for r in range(NF)],
            [(zi[b], yi[b]) for b in range(NIN)] + [(zf[r], yf[r]) for r in range(NF)],
            [(load[:, lanes(b)], z_ref[b]) for b in range(NIN)],
            [(yi[b], z_ref[b]) for b in range(NIN)],
            [(z_ref[b], acc_ref[b]) for b in range(NIN)],
        )
    )
    for k, value in enumerate(sums):
        sums_ref[k] = value
    for b in range(NB):
        load_ref[b] = load[:, lanes(b)]


def face_apply(acc_ref, incs, face_ref, block_high, block_low, swap_ref, y_ref, z_ref, outs):
    faces = [face_ref[r] + inc[...] for r, inc in enumerate(incs)]
    wide = [
        jnp.concatenate(
            [jnp.concatenate([ref[r, c] for c in range(NF)], axis=1) for r in range(NF)], axis=0
        )
        for ref in (block_high, block_low)
    ]
    more = dot_halves(halves(jnp.concatenate(faces, axis=1)), wide)
    for r, out in enumerate(outs):
        z_ref[r] = faces[r]
        y_ref[r] = acc_ref[NIN + r] + more[:, lanes(r)]
        out[...] = select_lanes(y_ref[r], swap_ref[r])
    return faces, more


def first_face_body(
    acc_ref, in0, in1, in2, in3, face_ref, block_high, block_low, swap_ref,
    y_ref, z_ref, out0, out1, out2, out3,
):
    face_apply(
        acc_ref, (in0, in1, in2, in3), face_ref, block_high, block_low, swap_ref, y_ref, z_ref,
        (out0, out1, out2, out3),
    )


def second_face_body(
    acc_ref, in0, in1, in2, in3, face_ref, block_high, block_low, swap_ref, sums_ref, load_ref, yf,
    y_ref, z_ref, dots_ref, out0, out1, out2, out3,
):
    faces, more = face_apply(
        acc_ref, (in0, in1, in2, in3), face_ref, block_high, block_low, swap_ref, y_ref, z_ref,
        (out0, out1, out2, out3),
    )
    late = pair_sums(
        (
            [(load_ref[NIN + r], faces[r]) for r in range(NF)],
            [(yf[r], faces[r]) for r in range(NF)],
            [(faces[r], 2.0 * acc_ref[NIN + r] + more[:, lanes(r)]) for r in range(NF)],
        )
    )
    sums = [sums_ref[0], sums_ref[1]] + [sums_ref[2 + k] + late[k] for k in range(3)]
    place = lax.broadcasted_iota(jnp.int32, (NRHS, BS), 1)
    case = lax.broadcasted_iota(jnp.int32, (NRHS, BS), 0)
    for row in range(2):
        total = jnp.zeros((NRHS, BS), F32)
        for k in range(4 * row, min(4 * row + 4, len(sums))):
            column = jnp.sum(sums[k], axis=1, keepdims=True)
            total = total + jnp.where(place == case + NRHS * (k % 4), column, 0.0)
        total = jnp.sum(total, axis=0, keepdims=True)
        dots_ref[:, row : row + 1, :] = jnp.broadcast_to(total[None], (dots_ref.shape[0], 1, BS))


def final_body(
    dots_ref, in0, in1, in2, in3, load, rf, zi, zf, yi, qf, wi, wf, vi, vf, sol_ref, res_ref,
):
    place = lax.broadcasted_iota(jnp.int32, (NRHS, BS), 1)
    case = lax.broadcasted_iota(jnp.int32, (NRHS, BS), 0)
    total = jnp.sum(dots_ref[...], axis=0)
    rz, zq, rw, qw, wv = [
        jnp.sum(
            jnp.where(place == case + NRHS * (k % 4), total[k // 4 : k // 4 + 1, :], 0.0),
            axis=1,
            keepdims=True,
        )
        for k in range(5)
    ]
    alpha = rz / zq
    rho = rz - alpha * (rw + zq) + alpha * alpha * qw
    grow = 1.0 + rho / rz
    curve = grow * grow * zq - 2.0 * grow * alpha * qw + alpha * alpha * wv
    step = rho / curve
    first = alpha + step * grow
    second = step * alpha
    for b in range(NB):
        if b < NIN:
            r_b, z_b, q_b, w_b, v_b = load[b], zi[b], yi[b], wi[b], vi[b]
        else:
            f = b - NIN
            r_b, z_b, q_b, w_b = rf[f], zf[f], qf[f], wf[f]
            v_b = vf[f] + (in0, in1, in2, in3)[f][...]
        sol_ref[0, :, lanes(b)] = first * z_b - second * w_b
        res_ref[0, :, lanes(b)] = r_b - first * q_b + second * v_b


def f32(*shape):
    return jax.ShapeDtypeStruct(shape, F32)


def bf16(*shape):
    return jax.ShapeDtypeStruct(shape, BF16)


SMEM = pl.BlockSpec(memory_space=pltpu.SMEM)
VMEM = pl.BlockSpec(memory_space=pltpu.VMEM)
HBM = pl.BlockSpec(memory_space=pltpu.HBM)


def call(body, name, outs, specs, *args, scratch=(), copies=0):
    scratch = [pltpu.VMEM(shape, F32) if isinstance(shape, tuple) else shape for shape in scratch]
    if copies:
        scratch.append(pltpu.SemaphoreType.DMA((copies,)))
    args = [
        pltpu.with_memory_space_constraint(arg, pltpu.HBM) if spec is HBM else arg
        for arg, spec in zip(args, specs, strict=True)
    ]
    return pl.pallas_call(
        body,
        name=name,
        out_shape=outs,
        in_specs=specs,
        out_specs=[VMEM] * len(outs),
        scratch_shapes=scratch,
        compiler_params=pltpu.CompilerParams(vmem_limit_bytes=16 << 20),
    )(*args)


def on_device(
    load_vector, matrix_tiles, tile_cols, interior_inv, schur_inv, coarse_basis, coarse_inv,
    row_map, face_link, coarse_id,
):
    cols = tile_cols.T
    line = lax.axis_size("gz")
    devices = line * lax.axis_size("gy") * lax.axis_size("gx")
    depth_z = line.bit_length() - 1
    depth_y = lax.axis_size("gy").bit_length() - 1
    masks = [1, 2, 1 << depth_z, 1 << (depth_z + depth_y)]

    def trade(value, mask):
        return lax.ppermute(value, AXES, [(i, i ^ mask) for i in range(devices)])

    def trade_faces(faces):
        return [trade(face, mask) for face, mask in zip(faces, masks)]

    def trade_line(value):
        return [trade(value, mask) for mask in range(1, line)]

    inside = (NIN, NRHS, BS)
    around = (NF, NRHS, BS)
    every = (NB, NRHS, BS)
    block, face, small, side = f32(*inside), f32(*around), f32(NRHS, BS), f32(NRHS + 16, BS)
    nf = NF * BS
    width = line * CB * CW
    target, column, weight, *sides = call(
        prepare_body, "prepare", [f32(8, BS), jax.ShapeDtypeStruct((2, BS, BS), jnp.int32), f32(2 * NF, BS)] + [side] * NF, [HBM] * 4,
        load_vector, row_map, coarse_id, face_link,
        scratch=[pltpu.SMEM((1, CB), jnp.int32), pltpu.SMEM((1, NF), jnp.int32),
                 pltpu.VMEM((1, NF, BS), jnp.int32), (NRHS, nf)],
        copies=4,
    )
    came = trade_faces(sides)
    far = [trade(target, mask) for mask in range(3, line)]

    own = OCAP * CW
    mat_outs = [block, small, bf16(nf, nf), bf16(nf, nf), bf16(BS, nf), bf16(BS, nf)]
    mat_scratch = [(NIN, BS, BS), (BS, NL), (nf, nf)]
    cols_scratch = pltpu.SMEM((TPR, NB), jnp.int32)
    face_tiles = (NF, TPR, BS, BS)

    inner, part, *mats, coarse_parts = call(
        load_inside_body, "inside_load", mat_outs + [bf16(3, own, own)], [HBM] * 5,
        load_vector, interior_inv, coarse_basis, schur_inv, coarse_inv,
        scratch=mat_scratch + [(NRHS, NIN * BS), (own, own)], copies=5,
    )
    width = line * CB * CW
    half = 2 * SCAP * CW
    r_face, outer, contrib, swap, targets, rows, *sides = call(
        lambda *refs: first_faces_body(*refs, line=line), "faces_load",
        [face, face, small, bf16(NF, BS, BS), f32(1, width), f32(half, BS)]
        + [f32(NRHS + half, BS)] * (line - 1),
        [VMEM] * (13 + line),
        *sides, *came, target, weight, *mats, part, coarse_parts, *far,
    )
    others = [trade(value, mask) for value, mask in zip(sides, range(1, line))]
    blocks = call(
        face_block_body, "face_block", [bf16(NF, NF, BS, BS)] * 2, [HBM] * 2, matrix_tiles, cols,
        scratch=[face_tiles, cols_scratch], copies=2,
    )
    back, u_face, *sends = call(
        lambda *refs: first_coarse_body(*refs, line=line), "coarse_load",
        [small, face] + [small] * NF, [VMEM] * (line + 9),
        contrib, rows, targets, target, *others, outer, *mats[2:], weight, swap, blocks[0],
    )

    came = trade_faces(sends)
    own_scratch = [(BS, NIN * BS), (NIN, TPR, BS, BS)]
    z, acc = call(
        first_apply_body, "own_first", [block, f32(*every)], [VMEM, VMEM] + [HBM] * 3,
        inner, back, coarse_basis, matrix_tiles, cols,
        scratch=own_scratch + [cols_scratch], copies=2 + len(CHUNKS),
    )
    y_face, z_face, *sends = call(
        first_face_body, "face_first", [face, face] + [small] * NF, [VMEM] * 9,
        acc, *came, u_face, *blocks, swap,
    )
    came = trade_faces(sends)
    y, inner, part, *mats = call(
        image_inside_body, "inside_image", [block] + mat_outs, [VMEM] * 2 + [HBM] * 5,
        acc, z_face, cols, matrix_tiles, interior_inv, coarse_basis, schur_inv,
        scratch=mat_scratch + [face_tiles, every, cols_scratch], copies=5,
    )
    high, low = call(
        lambda *refs: table_body(*refs, line=line), "table", [bf16(BS, width), bf16(BS, width)],
        [VMEM] * (line + 2), rows, targets, column, *others,
    )
    q_face, outer, contrib = call(
        next_faces_body, "faces_image", [face, face, small], [VMEM] * 11,
        y_face, *came, weight, *mats, part,
    )
    others = trade_line(contrib)
    back, u_face, *sends = call(
        lambda *refs: next_coarse_body(*refs, line=line), "coarse_image",
        [small, face] + [small] * NF, [VMEM] * (line + 7),
        contrib, *others, high, low, outer, *mats[2:], weight, swap,
    )
    came = trade_faces(sends)
    w, acc, sums, load = call(
        second_apply_body, "own_second", [block, f32(*every), f32(5, NRHS, BS), f32(*every)],
        [VMEM, VMEM] + [HBM] * 4 + [VMEM] * 4,
        inner, back, coarse_basis, matrix_tiles, cols, load_vector, z, z_face, y, y_face,
        scratch=own_scratch + [(NRHS, NL), cols_scratch, pltpu.SemaphoreType.DMA((2 + len(CHUNKS),))],
        copies=1,
    )
    v_face, w_face, dots, *sends = call(
        second_face_body, "face_second", [face, face, f32(devices, 2, BS)] + [small] * NF, [VMEM] * 12,
        acc, *came, u_face, *blocks, swap, sums, load, y_face,
    )
    spread = lax.all_to_all(dots, AXES, 0, 0)
    came = trade_faces(sends)
    (v,) = call(
        last_image_body, "inside_last", [block], [VMEM] * 2 + [HBM] * 2, acc, w_face, cols, matrix_tiles,
        scratch=[face_tiles, every, cols_scratch], copies=2,
    )
    out = f32(1, NRHS, NL)
    return tuple(
        call(
            final_body, "combine", [out, out], [VMEM] * 15,
            spread, *came, load, r_face, z, z_face, y, q_face, w, w_face, v, v_face,
        )
    )


def solution(mesh):
    lead = P(AXES, None, None)
    flat = P(AXES, None)
    in_specs = (lead, P(AXES, None, None, None), flat, lead, lead, lead, lead, lead, flat, flat)
    return jax.shard_map(
        on_device, mesh=mesh, in_specs=in_specs, out_specs=(lead, lead), check_vma=False
    )
```

```python
import jax
import jax.numpy as jnp
from jax import lax
from jax.experimental import pallas as pl
from jax.experimental.pallas import tpu as pltpu
from jax.sharding import PartitionSpec as P

BS = 128
NIN = 12
NF = 4
NRHS = 32
CW = 32
CB = 4
OCAP = 8
SCAP = 2
EARLY = 4
CHUNKS = (4, 3, 1)
NB = 16
TPR = 7
NL = 2048
AXES = ("gx", "gy", "gz")
F32 = jnp.float32
BF16 = jnp.bfloat16
NN = (((1,), (0,)), ((), ()))
NT = (((1,), (1,)), ((), ()))


def mm(left, right, dims=NN):
    return lax.dot_general(left, right, dims, preferred_element_type=F32)


def halves(value):
    high = value.astype(BF16)
    return high, (value - high.astype(F32)).astype(BF16)


def dot_halves(left, right, dims=NN):
    (lh, ll), (rh, rl) = left, right
    rows = lh.shape[0]
    both = mm(jnp.concatenate([lh, ll], axis=0), rh, dims)
    return both[:rows] + both[rows:] + mm(lh, rl, dims)


def select_lanes(value, onehot):
    rows = value.shape[0]
    high, rest = halves(value)
    low = (value - high.astype(F32) - rest.astype(F32)).astype(BF16)
    out = mm(jnp.concatenate([high, rest, low], axis=0), onehot)
    return out[:rows] + out[rows : 2 * rows] + out[2 * rows :]


def lanes(block):
    return slice(block * BS, (block + 1) * BS)


def start_all(sems, *pairs):
    copies = [pltpu.make_async_copy(src, dst, sems.at[k]) for k, (src, dst) in enumerate(pairs)]
    for copy in copies:
        copy.start()
    return copies


def prepare_body(
    load_ref, map_ref, id_ref, link_ref, target_ref, column_ref, weight_ref, side0, side1, side2, side3,
    ids, links, maps, faces, sems,
):
    copies = start_all(
        sems,
        (id_ref, ids),
        (link_ref, links),
        (map_ref, maps),
        (load_ref.at[0, :, NIN * BS :], faces),
    )
    copies[0].wait()
    along = lax.broadcasted_iota(jnp.int32, (8, BS), 1)
    down = lax.broadcasted_iota(jnp.int32, (BS, BS), 0)
    target, place = along % CW, along % CW
    column, spot = down % CW, down % CW
    for b in range(CB):
        start = ids[0, b] * CW
        before = jnp.int32(0)
        for other in range(b):
            before = before + jnp.where(ids[0, other] // OCAP == ids[0, b] // OCAP, CW, 0)
        target = jnp.where(along // CW == b, target + start, target)
        place = jnp.where(along // CW == b, place + before, place)
        column = jnp.where(down // CW == b, column + start, column)
        spot = jnp.where(down // CW == b, spot + before, spot)
    line = lax.broadcasted_iota(jnp.int32, (8, BS), 0)
    target = jnp.where(line == 1, place, target).astype(F32)
    target_ref[...] = target
    column_ref[0] = column
    column_ref[1] = spot
    copies[1].wait()
    for r in range(NF):
        link = jnp.full((1, BS), links[0, r], jnp.int32).astype(F32)
        weight_ref[r : r + 1, :] = 1.0 - 0.5 * link
        weight_ref[NF + r : NF + r + 1, :] = link
    copies[2].wait()
    copies[3].wait()
    for r, out in enumerate((side0, side1, side2, side3)):
        out[:NRHS, :] = faces[:, lanes(r)]
        out[NRHS : NRHS + 8, :] = jnp.broadcast_to(maps[0, r : r + 1, :], (8, BS)).astype(F32)
        out[NRHS + 8 :, :] = target


def face_rows(acc_ref, face_ref, tiles, cols, out_ref, spare_ref):
    spare_ref[...] = acc_ref[...]
    for r in range(NF):
        add_row(face_ref[r], NIN + r, tiles[r], cols, spare_ref)
    out_ref[...] = spare_ref[:NIN]


def solve_inside(x_of, inv, basis, copies, inner_ref, part_ref):
    copies[0].wait()
    pieces = []
    for b in range(NIN):
        xb = halves(x_of(b))
        pieces.append(xb)
        inner_ref[b] = dot_halves(xb, halves(inv[b]))
    cat = tuple(jnp.concatenate([p[h] for p in pieces], axis=1) for h in range(2))
    copies[1].wait()
    part_ref[...] = dot_halves(cat, halves(basis[:, : NIN * BS]), NT)


def load_inside_body(
    x_ref, inv_ref, basis_ref, schur_ref, coarse_ref,
    inner_ref, part_ref, schur_high, schur_low, basis_high, basis_low, coarse_parts,
    inv, basis, schur, x, coarse, sems,
):
    first, *copies = start_all(
        sems, (x_ref.at[0, :, : NIN * BS], x), (inv_ref, inv), (basis_ref.at[0], basis),
        (schur_ref.at[0], schur), (coarse_ref.at[0], coarse),
    )
    first.wait()
    solve_inside(lambda b: x[:, lanes(b)], inv, basis, copies, inner_ref, part_ref)
    basis_high[...], basis_low[...] = halves(basis[:, NIN * BS :])
    copies[2].wait()
    schur_high[...], schur_low[...] = halves(schur[...])
    copies[3].wait()
    value = coarse[...]
    for k in range(3):
        coarse_parts[k] = value.astype(BF16)
        value = value - coarse_parts[k].astype(F32)


def image_inside_body(
    acc_ref, face_ref, cols_ref, tiles_ref, inv_ref, basis_ref, y_ref, inner_ref, part_ref,
    inv, basis, tiles, spare, cols, sems,
):
    first, second, *copies = start_all(
        sems, (cols_ref, cols), (tiles_ref.at[NIN:], tiles), (inv_ref, inv),
        (basis_ref.at[0, :, : NIN * BS], basis),
    )
    first.wait()
    second.wait()
    face_rows(acc_ref, face_ref, [wide_of(tiles, r) for r in range(NF)], cols, y_ref, spare)
    solve_inside(lambda b: y_ref[b], inv, basis, copies, inner_ref, part_ref)


def last_image_body(acc_ref, face_ref, cols_ref, tiles_ref, y_ref, tiles, spare, cols, sems):
    copies = start_all(sems, (cols_ref, cols), (tiles_ref.at[NIN:], tiles))
    for copy in copies:
        copy.wait()
    face_rows(acc_ref, face_ref, [wide_of(tiles, r) for r in range(NF)], cols, y_ref, spare)


def scaled_faces(faces, weight_ref):
    return halves(
        jnp.concatenate([faces[r] * weight_ref[r : r + 1, :] for r in range(NF)], axis=1)
    )


def add_faces(faces, weight_ref, basis_high, basis_low, part_ref, contrib_ref):
    scaled = scaled_faces(faces, weight_ref)
    contrib_ref[...] = part_ref[...] + dot_halves(scaled, (basis_high[...], basis_low[...]), NT)


def solve_faces(face_ref, weight_ref, schur_high, schur_low, outer_ref):
    outer = dot_halves(scaled_faces(face_ref, weight_ref), (schur_high[...], schur_low[...]))
    for r in range(NF):
        outer_ref[r] = outer[:, lanes(r)]


def onehot(equal):
    return equal.astype(F32).astype(BF16)


def maps_of(own, inc):
    rows = lax.broadcasted_iota(jnp.int32, (BS, BS), 0).astype(F32)
    return onehot(rows == own[NRHS : NRHS + 1, :]), onehot(rows == inc[NRHS : NRHS + 1, :])


def rows_for(target, coarse_ref):
    here = lax.axis_index("gz")
    slots = lax.broadcasted_iota(jnp.int32, (SCAP * CW, BS), 0)
    places = lax.broadcasted_iota(jnp.int32, (OCAP * CW, BS), 0)
    goal = target.astype(jnp.int32)
    into = onehot(slots == goal[1:2, :])
    out_of = onehot(places == goal[0:1, :] - here * (OCAP * CW))
    take = mm(into, out_of, NT).astype(BF16)
    return mm(take, coarse_ref[0]) + mm(take, coarse_ref[1]) + mm(take, coarse_ref[2])


def put_rows(ref, first, rows):
    ref[first : first + SCAP * CW, :] = rows[:, :BS]
    ref[first + SCAP * CW : first + 2 * SCAP * CW, :] = rows[:, BS:]


def first_faces_body(
    own0, own1, own2, own3, in0, in1, in2, in3, target_ref, weight_ref,
    basis_high, basis_low, part_ref, coarse_ref, *rest, line,
):
    targets = [target_ref[...], in0[NRHS + 8 :, :], in1[NRHS + 8 :, :]] + [
        ref[...] for ref in rest[: line - 3]
    ]
    face_ref, contrib_ref, all_ref, *sides = rest[line - 3 :]
    faces = []
    for r, (own, inc) in enumerate(zip((own0, own1, own2, own3), (in0, in1, in2, in3))):
        mine, theirs = maps_of(own, inc)
        link = weight_ref[NF + r : NF + r + 1, :]
        came = select_lanes(inc[:NRHS, :], (mm(theirs, mine, NT) * link).astype(BF16))
        faces.append(own[:NRHS, :] + came)
        face_ref[r] = faces[-1]
    add_faces(faces, weight_ref, basis_high, basis_low, part_ref, contrib_ref)
    all_ref[...] = jnp.concatenate([t[0:1, :] for t in targets], axis=1)
    for side, target in zip(sides, targets[1:]):
        side[:NRHS, :] = contrib_ref[...]
        put_rows(side, NRHS, rows_for(target, coarse_ref))


def under_line_body(
    own0, own1, own2, own3, in0, in1, in2, in3, target_ref, weight_ref, face_ref, schur_high, schur_low,
    coarse_ref, all_ref, tiles_ref, cols_ref,
    basis_ref, high_ref, low_ref, outer_ref, swap_ref, rows_ref, pick_ref, mine_ref, early_ref, inside_ref,
    tiles, cols, sems, *, line,
):
    *copies, third, fourth = start_all(
        sems, (cols_ref, cols), (tiles_ref.at[NIN:], tiles), (tiles_ref.at[:EARLY], early_ref),
        (basis_ref.at[0, :, : NIN * BS], inside_ref),
    )
    solve_faces(face_ref, weight_ref, schur_high, schur_low, outer_ref)
    for r, (own, inc) in enumerate(zip((own0, own1, own2, own3), (in0, in1, in2, in3))):
        mine, theirs = maps_of(own, inc)
        swap_ref[r] = (mm(mine, theirs, NT) * weight_ref[NF + r : NF + r + 1, :]).astype(BF16)
    put_rows(rows_ref, 0, rows_for(target_ref[...], coarse_ref))
    here = lax.axis_index("gz")
    own = OCAP * CW
    goal = target_ref[...].astype(jnp.int32)
    slots = lax.broadcasted_iota(jnp.int32, (SCAP * CW, BS), 0)
    places = lax.broadcasted_iota(jnp.int32, (BS, own), 1)
    for e in range(line):
        down = jnp.broadcast_to(all_ref[:, lanes(e)], (BS, BS)).T.astype(jnp.int32)
        down = jnp.concatenate([down] * (own // BS), axis=1)
        for m in range(line):
            owner = jnp.bitwise_xor(here, m)
            pick_ref[lanes(e), m * own : (m + 1) * own] = onehot(places + owner * own == down)
    for m in range(line):
        owner = jnp.bitwise_xor(here, m)
        mine = (slots == goal[1:2, :]) & (goal[0:1, :] // own == owner)
        mine_ref[m * SCAP * CW : (m + 1) * SCAP * CW, :] = onehot(mine)
    high_ref[...] = jnp.zeros_like(high_ref)
    low_ref[...] = jnp.zeros_like(low_ref)
    for copy in copies:
        copy.wait()
    for r in range(NF):
        for t in range(TPR):
            place = cols[t, NIN + r] - NIN

            @pl.when(place >= 0)
            def _(r=r, t=t, place=place):
                high_ref[r, place], low_ref[r, place] = halves(tiles[r, t])

    third.wait()
    fourth.wait()


def next_faces_body(
    y_ref, in0, in1, in2, in3, weight_ref, basis_high, basis_low, part_ref, face_ref, contrib_ref,
):
    faces = []
    for r, inc in enumerate((in0, in1, in2, in3)):
        faces.append(y_ref[r] + inc[...])
        face_ref[r] = faces[-1]
    add_faces(faces, weight_ref, basis_high, basis_low, part_ref, contrib_ref)


def finish(back, outer_ref, basis, weight_ref, swap_ref, back_ref, face_ref, outs):
    back_ref[...] = back
    corr = dot_halves(halves(back), basis)
    for r in range(NF):
        value = weight_ref[r : r + 1, :] * (outer_ref[r] + corr[:, lanes(r)])
        face_ref[r] = value
        outs[r][...] = select_lanes(value, swap_ref[r])


def owner_rows(side, m):
    first = NRHS if m else 0
    return jnp.concatenate(
        [side[first : first + SCAP * CW, :], side[first + SCAP * CW :, :]], axis=1
    )


def pick_of(all_ref, owner):
    rows = lax.broadcasted_iota(jnp.int32, (OCAP * CW, all_ref.shape[1]), 0)
    return (rows + owner * (OCAP * CW) == all_ref[...].astype(jnp.int32)).astype(F32).astype(BF16)


def first_coarse_body(own_ref, rows_ref, pick_ref, mine_ref, *refs, line):
    sides = (rows_ref,) + refs[: line - 1]
    outer_ref, basis_high, basis_low, weight_ref, swap_ref, back_ref, face_ref, *outs = refs[line - 1 :]
    contribs = halves(jnp.concatenate([own_ref[...]] + [s[:NRHS, :] for s in sides[1:]], axis=1))
    both = mm(jnp.concatenate(contribs, axis=0), pick_ref[...])
    gathered = both[:NRHS] + both[NRHS:]
    own = OCAP * CW
    solved = [
        dot_halves(halves(gathered[:, m * own : (m + 1) * own]), halves(owner_rows(side, m)), NT)
        for m, side in enumerate(sides)
    ]
    back = select_lanes(jnp.concatenate(solved, axis=1), mine_ref[...])
    finish(back, outer_ref, (basis_high[...], basis_low[...]), weight_ref, swap_ref, back_ref, face_ref, outs)


def table_body(
    tiles_ref, basis_ref, rows_ref, all_ref, column_ref, face_ref, weight_ref, schur_high, schur_low, *refs, line
):
    sides = (rows_ref,) + refs[: line - 1]
    high_ref, low_ref, outer_ref, early_ref, inside_ref, sems = refs[line - 1 :]
    copies = start_all(
        sems, (tiles_ref.at[:EARLY], early_ref), (basis_ref.at[0, :, : NIN * BS], inside_ref)
    )
    solve_faces(face_ref, weight_ref, schur_high, schur_low, outer_ref)
    here = lax.axis_index("gz")
    slots = lax.broadcasted_iota(jnp.int32, (BS, BS), 1)
    table = jnp.zeros((2 * BS, all_ref.shape[1]), F32)
    for m in range(line):
        owner = jnp.bitwise_xor(here, m)
        mine = (slots == column_ref[1]) & (column_ref[0] // (OCAP * CW) == owner)
        take = mine.astype(F32).astype(BF16)[:, : SCAP * CW]
        high, low = halves(owner_rows(sides[m], m))
        both = jnp.concatenate([mm(take, high).astype(BF16), mm(take, low).astype(BF16)], axis=0)
        table = table + mm(both, pick_of(all_ref, owner))
    high_ref[...] = table[:BS].astype(BF16)
    low_ref[...] = table[BS:].astype(BF16)
    for copy in copies:
        copy.wait()


def next_coarse_body(*refs, line):
    contribs = [ref[...] for ref in refs[:line]]
    high_ref, low_ref, outer_ref, basis_high, basis_low, weight_ref, swap_ref = refs[line : 7 + line]
    back_ref, face_ref = refs[7 + line : 9 + line]
    table = (high_ref[...], low_ref[...])
    back = dot_halves(halves(jnp.concatenate(contribs, axis=1)), table, NT)
    finish(back, outer_ref, (basis_high[...], basis_low[...]), weight_ref, swap_ref, back_ref, face_ref,
           refs[9 + line :])


def add_row(x, i, wide, cols_ref, acc_ref):
    out = dot_halves(halves(x), wide)
    places = [cols_ref[t, i] for t in range(TPR)]
    before = [acc_ref[place] for place in places]
    for t in range(TPR):
        acc_ref[places[t]] = before[t] + out[:, lanes(t)]


def wide_of(tiles, i):
    return halves(jnp.concatenate([tiles[i, t] for t in range(TPR)], axis=1))


def own_apply(
    inner_ref, back_ref, early_ref, basis, tiles_ref, cols_ref, z_ref, acc_ref, tiles, cols, sems
):
    pairs = [(cols_ref, cols)]
    first = EARLY
    for count in CHUNKS:
        pairs.append(
            (tiles_ref.at[first : first + count], tiles.at[first - EARLY : first - EARLY + count])
        )
        first += count
    copies = start_all(sems, *pairs)
    acc_ref[...] = jnp.zeros_like(acc_ref)
    back = halves(back_ref[...])
    corr = dot_halves(back, halves(basis[...]))
    for b in range(NIN):
        z_ref[b] = inner_ref[b] + corr[:, lanes(b)]
    copies[0].wait()
    for i in range(EARLY):
        add_row(z_ref[i], i, wide_of(early_ref, i), cols, acc_ref)
    first = EARLY
    for k, count in enumerate(CHUNKS):
        copies[1 + k].wait()
        for i in range(first, first + count):
            add_row(z_ref[i], i, wide_of(tiles, i - EARLY), cols, acc_ref)
        first += count


def first_apply_body(*refs):
    own_apply(*refs)


def pair_sums(pairs):
    return [sum(left * right for left, right in blocks) for blocks in pairs]


def second_apply_body(
    inner_ref, back_ref, early_ref, basis, tiles_ref, cols_ref, load_hbm, zi, zf, yi, yf,
    z_ref, acc_ref, sums_ref, load_ref, tiles, load, cols, sems, more,
):
    (copy,) = start_all(more, (load_hbm.at[0], load))
    own_apply(inner_ref, back_ref, early_ref, basis, tiles_ref, cols_ref, z_ref, acc_ref, tiles, cols, sems)
    copy.wait()
    sums = pair_sums(
        (
            [(load[:, lanes(b)], zi[b]) for b in range(NIN)]
            + [(load[:, lanes(NIN + r)], zf[r]) for r in range(NF)],
            [(zi[b], yi[b]) for b in range(NIN)] + [(zf[r], yf[r]) for r in range(NF)],
            [(load[:, lanes(b)], z_ref[b]) for b in range(NIN)],
            [(yi[b], z_ref[b]) for b in range(NIN)],
            [(z_ref[b], acc_ref[b]) for b in range(NIN)],
        )
    )
    for k, value in enumerate(sums):
        sums_ref[k] = value
    for b in range(NB):
        load_ref[b] = load[:, lanes(b)]


def face_apply(acc_ref, incs, face_ref, block_high, block_low, swap_ref, y_ref, z_ref, outs):
    faces = [face_ref[r] + inc[...] for r, inc in enumerate(incs)]
    wide = [
        jnp.concatenate(
            [jnp.concatenate([ref[r, c] for c in range(NF)], axis=1) for r in range(NF)], axis=0
        )
        for ref in (block_high, block_low)
    ]
    more = dot_halves(halves(jnp.concatenate(faces, axis=1)), wide)
    for r, out in enumerate(outs):
        z_ref[r] = faces[r]
        y_ref[r] = acc_ref[NIN + r] + more[:, lanes(r)]
        out[...] = select_lanes(y_ref[r], swap_ref[r])
    return faces, more


def first_face_body(
    acc_ref, in0, in1, in2, in3, face_ref, block_high, block_low, swap_ref,
    y_ref, z_ref, out0, out1, out2, out3,
):
    face_apply(
        acc_ref, (in0, in1, in2, in3), face_ref, block_high, block_low, swap_ref, y_ref, z_ref,
        (out0, out1, out2, out3),
    )


def second_face_body(
    acc_ref, in0, in1, in2, in3, face_ref, block_high, block_low, swap_ref, sums_ref, load_ref, yf,
    y_ref, z_ref, dots_ref, out0, out1, out2, out3,
):
    faces, more = face_apply(
        acc_ref, (in0, in1, in2, in3), face_ref, block_high, block_low, swap_ref, y_ref, z_ref,
        (out0, out1, out2, out3),
    )
    late = pair_sums(
        (
            [(load_ref[NIN + r], faces[r]) for r in range(NF)],
            [(yf[r], faces[r]) for r in range(NF)],
            [(faces[r], 2.0 * acc_ref[NIN + r] + more[:, lanes(r)]) for r in range(NF)],
        )
    )
    sums = [sums_ref[0], sums_ref[1]] + [sums_ref[2 + k] + late[k] for k in range(3)]
    place = lax.broadcasted_iota(jnp.int32, (NRHS, BS), 1)
    case = lax.broadcasted_iota(jnp.int32, (NRHS, BS), 0)
    for row in range(2):
        total = jnp.zeros((NRHS, BS), F32)
        for k in range(4 * row, min(4 * row + 4, len(sums))):
            column = jnp.sum(sums[k], axis=1, keepdims=True)
            total = total + jnp.where(place == case + NRHS * (k % 4), column, 0.0)
        total = jnp.sum(total, axis=0, keepdims=True)
        dots_ref[:, row : row + 1, :] = jnp.broadcast_to(total[None], (dots_ref.shape[0], 1, BS))


def final_body(
    dots_ref, in0, in1, in2, in3, load, rf, zi, zf, yi, qf, wi, wf, vi, vf, sol_ref, res_ref,
):
    place = lax.broadcasted_iota(jnp.int32, (NRHS, BS), 1)
    case = lax.broadcasted_iota(jnp.int32, (NRHS, BS), 0)
    total = jnp.sum(dots_ref[...], axis=0)
    rz, zq, rw, qw, wv = [
        jnp.sum(
            jnp.where(place == case + NRHS * (k % 4), total[k // 4 : k // 4 + 1, :], 0.0),
            axis=1,
            keepdims=True,
        )
        for k in range(5)
    ]
    alpha = rz / zq
    rho = rz - alpha * (rw + zq) + alpha * alpha * qw
    grow = 1.0 + rho / rz
    curve = grow * grow * zq - 2.0 * grow * alpha * qw + alpha * alpha * wv
    step = rho / curve
    first = alpha + step * grow
    second = step * alpha
    for b in range(NB):
        if b < NIN:
            r_b, z_b, q_b, w_b, v_b = load[b], zi[b], yi[b], wi[b], vi[b]
        else:
            f = b - NIN
            r_b, z_b, q_b, w_b = rf[f], zf[f], qf[f], wf[f]
            v_b = vf[f] + (in0, in1, in2, in3)[f][...]
        sol_ref[0, :, lanes(b)] = first * z_b - second * w_b
        res_ref[0, :, lanes(b)] = r_b - first * q_b + second * v_b


def f32(*shape):
    return jax.ShapeDtypeStruct(shape, F32)


def bf16(*shape):
    return jax.ShapeDtypeStruct(shape, BF16)


SMEM = pl.BlockSpec(memory_space=pltpu.SMEM)
VMEM = pl.BlockSpec(memory_space=pltpu.VMEM)
HBM = pl.BlockSpec(memory_space=pltpu.HBM)


def call(body, name, outs, specs, *args, scratch=(), copies=0):
    scratch = [pltpu.VMEM(shape, F32) if isinstance(shape, tuple) else shape for shape in scratch]
    if copies:
        scratch.append(pltpu.SemaphoreType.DMA((copies,)))
    args = [
        pltpu.with_memory_space_constraint(arg, pltpu.HBM) if spec is HBM else arg
        for arg, spec in zip(args, specs, strict=True)
    ]
    return pl.pallas_call(
        body,
        name=name,
        out_shape=outs,
        in_specs=specs,
        out_specs=[VMEM] * len(outs),
        scratch_shapes=scratch,
        compiler_params=pltpu.CompilerParams(vmem_limit_bytes=16 << 20),
    )(*args)


def on_device(
    load_vector, matrix_tiles, tile_cols, interior_inv, schur_inv, coarse_basis, coarse_inv,
    row_map, face_link, coarse_id,
):
    cols = tile_cols.T
    line = lax.axis_size("gz")
    devices = line * lax.axis_size("gy") * lax.axis_size("gx")
    depth_z = line.bit_length() - 1
    depth_y = lax.axis_size("gy").bit_length() - 1
    masks = [1, 2, 1 << depth_z, 1 << (depth_z + depth_y)]

    def trade(value, mask):
        return lax.ppermute(value, AXES, [(i, i ^ mask) for i in range(devices)])

    def trade_faces(faces):
        return [trade(face, mask) for face, mask in zip(faces, masks)]

    def trade_line(value):
        return [trade(value, mask) for mask in range(1, line)]

    inside = (NIN, NRHS, BS)
    around = (NF, NRHS, BS)
    every = (NB, NRHS, BS)
    block, face, small, side = f32(*inside), f32(*around), f32(NRHS, BS), f32(NRHS + 16, BS)
    nf = NF * BS
    width = line * CB * CW
    target, column, weight, *sides = call(
        prepare_body, "prepare", [f32(8, BS), jax.ShapeDtypeStruct((2, BS, BS), jnp.int32), f32(2 * NF, BS)] + [side] * NF, [HBM] * 4,
        load_vector, row_map, coarse_id, face_link,
        scratch=[pltpu.SMEM((1, CB), jnp.int32), pltpu.SMEM((1, NF), jnp.int32),
                 pltpu.VMEM((1, NF, BS), jnp.int32), (NRHS, nf)],
        copies=4,
    )
    came = trade_faces(sides)
    far = [trade(target, mask) for mask in range(3, line)]

    own = OCAP * CW
    mat_outs = [block, small, bf16(nf, nf), bf16(nf, nf), bf16(BS, nf), bf16(BS, nf)]
    mat_scratch = [(NIN, BS, BS), (BS, NL), (nf, nf)]
    cols_scratch = pltpu.SMEM((TPR, NB), jnp.int32)
    face_tiles = (NF, TPR, BS, BS)

    inner, part, *mats, coarse_parts = call(
        load_inside_body, "inside_load", mat_outs + [bf16(3, own, own)], [HBM] * 5,
        load_vector, interior_inv, coarse_basis, schur_inv, coarse_inv,
        scratch=mat_scratch + [(NRHS, NIN * BS), (own, own)], copies=5,
    )
    width = line * CB * CW
    half = 2 * SCAP * CW
    own_sides = sides
    pre_outs = [f32(EARLY, TPR, BS, BS), f32(BS, NIN * BS)]
    r_face, contrib, targets, *sides = call(
        lambda *refs: first_faces_body(*refs, line=line), "faces_load",
        [face, small, f32(1, width)] + [f32(NRHS + half, BS)] * (line - 1), [VMEM] * (11 + line),
        *own_sides, *came, target, weight, *mats[2:], part, coarse_parts, *far,
    )
    others = [trade(value, mask) for value, mask in zip(sides, range(1, line))]
    block_high, block_low, outer, swap, rows, picks, mine, *early = call(
        lambda *refs: under_line_body(*refs, line=line), "under_line",
        [bf16(NF, NF, BS, BS)] * 2 + [face, bf16(NF, BS, BS), f32(half, BS)]
        + [bf16(width, line * own), bf16(line * SCAP * CW, BS)] + pre_outs,
        [VMEM] * 15 + [HBM] * 3,
        *own_sides, *came, target, weight, r_face, *mats[:2], coarse_parts, targets, matrix_tiles, cols, coarse_basis,
        scratch=[face_tiles, cols_scratch], copies=4,
    )
    back, u_face, *sends = call(
        lambda *refs: first_coarse_body(*refs, line=line), "coarse_load",
        [small, face] + [small] * NF, [VMEM] * (line + 8),
        contrib, rows, picks, mine, *others, outer, *mats[2:], weight, swap,
    )

    came = trade_faces(sends)
    own_scratch = [(NIN - EARLY, TPR, BS, BS)]
    z, acc = call(
        first_apply_body, "own_first", [block, f32(*every)], [VMEM] * 4 + [HBM] * 2,
        inner, back, *early, matrix_tiles, cols,
        scratch=own_scratch + [cols_scratch], copies=1 + len(CHUNKS),
    )
    y_face, z_face, *sends = call(
        first_face_body, "face_first", [face, face] + [small] * NF, [VMEM] * 9,
        acc, *came, u_face, block_high, block_low, swap,
    )
    came = trade_faces(sends)
    y, inner, part = call(
        image_inside_body, "inside_image", [block, block, small], [VMEM] * 2 + [HBM] * 4,
        acc, z_face, cols, matrix_tiles, interior_inv, coarse_basis,
        scratch=[(NIN, BS, BS), (BS, NIN * BS), face_tiles, every, cols_scratch], copies=4,
    )
    q_face, contrib = call(
        next_faces_body, "faces_image", [face, small], [VMEM] * 9,
        y_face, *came, weight, *mats[2:], part,
    )
    sides = trade_line(contrib)
    high, low, outer, *early = call(
        lambda *refs: table_body(*refs, line=line), "table", [bf16(BS, width)] * 2 + [face] + pre_outs,
        [HBM] * 2 + [VMEM] * (line + 6), matrix_tiles, coarse_basis, rows, targets, column, q_face, weight, *mats[:2], *others, copies=2,
    )
    back, u_face, *sends = call(
        lambda *refs: next_coarse_body(*refs, line=line), "coarse_image",
        [small, face] + [small] * NF, [VMEM] * (line + 7),
        contrib, *sides, high, low, outer, *mats[2:], weight, swap,
    )
    came = trade_faces(sends)
    w, acc, sums, load = call(
        second_apply_body, "own_second", [block, f32(*every), f32(5, NRHS, BS), f32(*every)],
        [VMEM] * 4 + [HBM] * 3 + [VMEM] * 4,
        inner, back, *early, matrix_tiles, cols, load_vector, z, z_face, y, y_face,
        scratch=own_scratch + [(NRHS, NL), cols_scratch, pltpu.SemaphoreType.DMA((1 + len(CHUNKS),))],
        copies=1,
    )
    v_face, w_face, dots, *sends = call(
        second_face_body, "face_second", [face, face, f32(devices, 2, BS)] + [small] * NF, [VMEM] * 12,
        acc, *came, u_face, block_high, block_low, swap, sums, load, y_face,
    )
    spread = lax.all_to_all(dots, AXES, 0, 0)
    came = trade_faces(sends)
    (v,) = call(
        last_image_body, "inside_last", [block], [VMEM] * 2 + [HBM] * 2, acc, w_face, cols, matrix_tiles,
        scratch=[face_tiles, every, cols_scratch], copies=2,
    )
    out = f32(1, NRHS, NL)
    return tuple(
        call(
            final_body, "combine", [out, out], [VMEM] * 15,
            spread, *came, load, r_face, z, z_face, y, q_face, w, w_face, v, v_face,
        )
    )


def solution(mesh):
    lead = P(AXES, None, None)
    flat = P(AXES, None)
    in_specs = (lead, P(AXES, None, None, None), flat, lead, lead, lead, lead, lead, flat, flat)
    return jax.shard_map(
        on_device, mesh=mesh, in_specs=in_specs, out_specs=(lead, lead), check_vma=False
    )
```

```python
import jax
import jax.numpy as jnp
from jax import lax
from jax.experimental import pallas as pl
from jax.experimental.pallas import tpu as pltpu
from jax.sharding import PartitionSpec as P

BS = 128
NIN = 12
NF = 4
NRHS = 32
CW = 32
CB = 4
OCAP = 8
SCAP = 2
EARLY = 6
LINE_PADS = (8, 16, 0)
CHUNKS = (4, 2)
NB = 16
TPR = 7
NL = 2048
AXES = ("gx", "gy", "gz")
F32 = jnp.float32
BF16 = jnp.bfloat16
NN = (((1,), (0,)), ((), ()))
NT = (((1,), (1,)), ((), ()))


def mm(left, right, dims=NN):
    return lax.dot_general(left, right, dims, preferred_element_type=F32)


def halves(value):
    high = value.astype(BF16)
    return high, (value - high.astype(F32)).astype(BF16)


def dot_halves(left, right, dims=NN):
    (lh, ll), (rh, rl) = left, right
    rows = lh.shape[0]
    both = mm(jnp.concatenate([lh, ll], axis=0), rh, dims)
    return both[:rows] + both[rows:] + mm(lh, rl, dims)


def select_lanes(value, onehot):
    rows = value.shape[0]
    high, rest = halves(value)
    low = (value - high.astype(F32) - rest.astype(F32)).astype(BF16)
    out = mm(jnp.concatenate([high, rest, low], axis=0), onehot)
    return out[:rows] + out[rows : 2 * rows] + out[2 * rows :]


def lanes(block):
    return slice(block * BS, (block + 1) * BS)


def start_all(sems, *pairs):
    copies = [pltpu.make_async_copy(src, dst, sems.at[k]) for k, (src, dst) in enumerate(pairs)]
    for copy in copies:
        copy.start()
    return copies


def prepare_body(
    load_ref, map_ref, id_ref, link_ref, target_ref, far_ref, column_ref, weight_ref, side0, side1, side2, side3,
    ids, links, maps, faces, sems,
):
    copies = start_all(
        sems,
        (id_ref, ids),
        (link_ref, links),
        (map_ref, maps),
        (load_ref.at[0, :, NIN * BS :], faces),
    )
    copies[0].wait()
    along = lax.broadcasted_iota(jnp.int32, (8, BS), 1)
    down = lax.broadcasted_iota(jnp.int32, (BS, BS), 0)
    target, place = along % CW, along % CW
    column, spot = down % CW, down % CW
    for b in range(CB):
        start = ids[0, b] * CW
        before = jnp.int32(0)
        for other in range(b):
            before = before + jnp.where(ids[0, other] // OCAP == ids[0, b] // OCAP, CW, 0)
        target = jnp.where(along // CW == b, target + start, target)
        place = jnp.where(along // CW == b, place + before, place)
        column = jnp.where(down // CW == b, column + start, column)
        spot = jnp.where(down // CW == b, spot + before, spot)
    line = lax.broadcasted_iota(jnp.int32, (8, BS), 0)
    target = jnp.where(line == 1, place, target).astype(F32)
    target_ref[...] = target
    far_ref[...] = jnp.zeros_like(far_ref)
    far_ref[:8, :] = target
    column_ref[0] = column
    column_ref[1] = spot
    copies[1].wait()
    for r in range(NF):
        link = jnp.full((1, BS), links[0, r], jnp.int32).astype(F32)
        weight_ref[r : r + 1, :] = 1.0 - 0.5 * link
        weight_ref[NF + r : NF + r + 1, :] = link
    copies[2].wait()
    copies[3].wait()
    for r, out in enumerate((side0, side1, side2, side3)):
        out[:NRHS, :] = faces[:, lanes(r)]
        out[NRHS : NRHS + 8, :] = jnp.broadcast_to(maps[0, r : r + 1, :], (8, BS)).astype(F32)
        out[NRHS + 8 :, :] = target


def face_rows(acc_ref, face_ref, tiles, cols, out_ref, spare_ref):
    spare_ref[...] = acc_ref[...]
    for r in range(NF):
        add_row(face_ref[r], NIN + r, tiles[r], cols, spare_ref)
    out_ref[...] = spare_ref[:NIN]


def solve_inside(x_of, inv, basis, copies, inner_ref, part_ref):
    copies[0].wait()
    pieces = []
    for b in range(NIN):
        xb = halves(x_of(b))
        pieces.append(xb)
        inner_ref[b] = dot_halves(xb, halves(inv[b]))
    cat = tuple(jnp.concatenate([p[h] for p in pieces], axis=1) for h in range(2))
    copies[1].wait()
    part_ref[...] = dot_halves(cat, halves(basis[:, : NIN * BS]), NT)


def load_inside_body(
    x_ref, inv_ref, basis_ref, schur_ref, coarse_ref,
    own0, own1, own2, own3,
    inner_ref, part_ref, schur_high, schur_low, basis_high, basis_low, coarse_parts, mine_ref,
    inv, basis, schur, x, coarse, sems,
):
    first, *copies = start_all(
        sems, (x_ref.at[0, :, : NIN * BS], x), (inv_ref, inv), (basis_ref.at[0], basis),
        (schur_ref.at[0], schur), (coarse_ref.at[0], coarse),
    )
    rows = lax.broadcasted_iota(jnp.int32, (BS, BS), 0).astype(F32)
    for r, side in enumerate((own0, own1, own2, own3)):
        mine_ref[r] = (rows == side[NRHS : NRHS + 1, :]).astype(F32).T.astype(BF16)
    first.wait()
    solve_inside(lambda b: x[:, lanes(b)], inv, basis, copies, inner_ref, part_ref)
    basis_high[...], basis_low[...] = halves(basis[:, NIN * BS :])
    copies[2].wait()
    schur_high[...], schur_low[...] = halves(schur[...])
    copies[3].wait()
    value = coarse[...]
    for k in range(3):
        coarse_parts[k] = value.astype(BF16)
        value = value - coarse_parts[k].astype(F32)


def image_inside_body(
    acc_ref, face_ref, cols_ref, tiles_ref, inv_ref, basis_ref, y_ref, inner_ref, part_ref,
    inv, basis, tiles, spare, cols, sems,
):
    first, second, *copies = start_all(
        sems, (cols_ref, cols), (tiles_ref.at[NIN:], tiles), (inv_ref, inv),
        (basis_ref.at[0, :, : NIN * BS], basis),
    )
    first.wait()
    second.wait()
    face_rows(acc_ref, face_ref, [wide_of(tiles, r) for r in range(NF)], cols, y_ref, spare)
    solve_inside(lambda b: y_ref[b], inv, basis, copies, inner_ref, part_ref)


def last_image_body(acc_ref, face_ref, cols_ref, tiles_ref, y_ref, tiles, spare, cols, sems):
    copies = start_all(sems, (cols_ref, cols), (tiles_ref.at[NIN:], tiles))
    for copy in copies:
        copy.wait()
    face_rows(acc_ref, face_ref, [wide_of(tiles, r) for r in range(NF)], cols, y_ref, spare)


def scaled_faces(faces, weight_ref):
    return halves(
        jnp.concatenate([faces[r] * weight_ref[r : r + 1, :] for r in range(NF)], axis=1)
    )


def add_faces(faces, weight_ref, basis_high, basis_low, part_ref, contrib_ref):
    scaled = scaled_faces(faces, weight_ref)
    contrib_ref[...] = part_ref[...] + dot_halves(scaled, (basis_high[...], basis_low[...]), NT)


def solve_faces(face_ref, weight_ref, schur_high, schur_low, outer_ref):
    outer = dot_halves(scaled_faces(face_ref, weight_ref), (schur_high[...], schur_low[...]))
    for r in range(NF):
        outer_ref[r] = outer[:, lanes(r)]


def onehot(equal):
    return equal.astype(F32).astype(BF16)


def maps_of(own, inc):
    rows = lax.broadcasted_iota(jnp.int32, (BS, BS), 0).astype(F32)
    return onehot(rows == own[NRHS : NRHS + 1, :]), onehot(rows == inc[NRHS : NRHS + 1, :])


def rows_for(targets, coarse_ref):
    here = lax.axis_index("gz")
    slots = lax.broadcasted_iota(jnp.int32, (SCAP * CW, BS), 0)
    places = lax.broadcasted_iota(jnp.int32, (OCAP * CW, BS), 0)
    takes = []
    for target in targets:
        goal = target.astype(jnp.int32)
        into = onehot(slots == goal[1:2, :])
        out_of = onehot(places == goal[0:1, :] - here * (OCAP * CW))
        takes.append(mm(into, out_of, NT).astype(BF16))
    take = jnp.concatenate(takes, axis=0)
    rows = mm(take, coarse_ref[0]) + mm(take, coarse_ref[1]) + mm(take, coarse_ref[2])
    return [rows[k * SCAP * CW : (k + 1) * SCAP * CW] for k in range(len(targets))]


def put_rows(ref, first, rows):
    ref[first : first + SCAP * CW, :] = rows[:, :BS]
    ref[first + SCAP * CW : first + 2 * SCAP * CW, :] = rows[:, BS:]


def first_faces_body(
    own0, own1, own2, own3, in0, in1, in2, in3, target_ref, weight_ref,
    basis_high, basis_low, part_ref, coarse_ref, turned_ref, *rest, line,
):
    targets = [target_ref[...], in0[NRHS + 8 :, :], in1[NRHS + 8 :, :]] + [
        ref[:8, :] for ref in rest[: line - 3]
    ]
    face_ref, contrib_ref, all_ref, *sides = rest[line - 3 :]
    faces = []
    for r, (own, inc) in enumerate(zip((own0, own1, own2, own3), (in0, in1, in2, in3))):
        theirs = maps_of(own, inc)[1]
        link = weight_ref[NF + r : NF + r + 1, :]
        came = select_lanes(inc[:NRHS, :], (mm(theirs, turned_ref[r]) * link).astype(BF16))
        faces.append(own[:NRHS, :] + came)
        face_ref[r] = faces[-1]
    add_faces(faces, weight_ref, basis_high, basis_low, part_ref, contrib_ref)
    all_ref[...] = jnp.concatenate([t[0:1, :] for t in targets], axis=1)
    for side, rows in zip(sides, rows_for(targets[1:], coarse_ref)):
        side[:NRHS, :] = contrib_ref[...]
        if side.shape[0] > NRHS + 2 * SCAP * CW:
            side[NRHS + 2 * SCAP * CW :, :] = jnp.zeros_like(side[NRHS + 2 * SCAP * CW :, :])
        put_rows(side, NRHS, rows)


def under_line_body(
    own0, own1, own2, own3, in0, in1, in2, in3, target_ref, weight_ref, face_ref, schur_high, schur_low,
    coarse_ref, all_ref, tiles_ref, cols_ref,
    basis_ref, high_ref, low_ref, outer_ref, swap_ref, rows_ref, pick_ref, mine_ref, early_ref, inside_ref,
    tiles, cols, sems, *, line,
):
    *copies, third, fourth = start_all(
        sems, (cols_ref, cols), (tiles_ref.at[NIN:], tiles), (tiles_ref.at[:EARLY], early_ref),
        (basis_ref.at[0, :, : NIN * BS], inside_ref),
    )
    solve_faces(face_ref, weight_ref, schur_high, schur_low, outer_ref)
    for r, (own, inc) in enumerate(zip((own0, own1, own2, own3), (in0, in1, in2, in3))):
        mine, theirs = maps_of(own, inc)
        swap_ref[r] = (mm(mine, theirs, NT) * weight_ref[NF + r : NF + r + 1, :]).astype(BF16)
    put_rows(rows_ref, 0, rows_for([target_ref[...]], coarse_ref)[0])
    here = lax.axis_index("gz")
    own = OCAP * CW
    goal = target_ref[...].astype(jnp.int32)
    slots = lax.broadcasted_iota(jnp.int32, (SCAP * CW, BS), 0)
    places = lax.broadcasted_iota(jnp.int32, (BS, own), 1)
    for e in range(line):
        down = jnp.broadcast_to(all_ref[:, lanes(e)], (BS, BS)).T.astype(jnp.int32)
        down = jnp.concatenate([down] * (own // BS), axis=1)
        for m in range(line):
            owner = jnp.bitwise_xor(here, m)
            pick_ref[lanes(e), m * own : (m + 1) * own] = onehot(places + owner * own == down)
    for m in range(line):
        owner = jnp.bitwise_xor(here, m)
        mine = (slots == goal[1:2, :]) & (goal[0:1, :] // own == owner)
        mine_ref[m * SCAP * CW : (m + 1) * SCAP * CW, :] = onehot(mine)
    high_ref[...] = jnp.zeros_like(high_ref)
    low_ref[...] = jnp.zeros_like(low_ref)
    for copy in copies:
        copy.wait()
    for r in range(NF):
        for t in range(TPR):
            place = cols[t, NIN + r] - NIN

            @pl.when(place >= 0)
            def _(r=r, t=t, place=place):
                high_ref[r, place], low_ref[r, place] = halves(tiles[r, t])

    third.wait()
    fourth.wait()


def next_faces_body(
    y_ref, in0, in1, in2, in3, weight_ref, basis_high, basis_low, part_ref, face_ref, contrib_ref,
):
    faces = []
    for r, inc in enumerate((in0, in1, in2, in3)):
        faces.append(y_ref[r] + inc[...])
        face_ref[r] = faces[-1]
    add_faces(faces, weight_ref, basis_high, basis_low, part_ref, contrib_ref)


def finish(back, outer_ref, basis, weight_ref, swap_ref, back_ref, face_ref, outs):
    back_ref[...] = back
    corr = dot_halves(halves(back), basis)
    for r in range(NF):
        value = weight_ref[r : r + 1, :] * (outer_ref[r] + corr[:, lanes(r)])
        face_ref[r] = value
        outs[r][...] = select_lanes(value, swap_ref[r])


def owner_rows(side, m):
    first = NRHS if m else 0
    return jnp.concatenate(
        [side[first : first + SCAP * CW, :], side[first + SCAP * CW : first + 2 * SCAP * CW, :]],
        axis=1,
    )


def pick_of(all_ref, owner):
    rows = lax.broadcasted_iota(jnp.int32, (OCAP * CW, all_ref.shape[1]), 0)
    return (rows + owner * (OCAP * CW) == all_ref[...].astype(jnp.int32)).astype(F32).astype(BF16)


def first_coarse_body(own_ref, rows_ref, pick_ref, mine_ref, *refs, line):
    sides = (rows_ref,) + refs[: line - 1]
    outer_ref, basis_high, basis_low, weight_ref, swap_ref, back_ref, face_ref, *outs = refs[line - 1 :]
    contribs = halves(jnp.concatenate([own_ref[...]] + [s[:NRHS, :] for s in sides[1:]], axis=1))
    both = mm(jnp.concatenate(contribs, axis=0), pick_ref[...])
    gathered = both[:NRHS] + both[NRHS:]
    own = OCAP * CW
    solved = [
        dot_halves(halves(gathered[:, m * own : (m + 1) * own]), halves(owner_rows(side, m)), NT)
        for m, side in enumerate(sides)
    ]
    back = select_lanes(jnp.concatenate(solved, axis=1), mine_ref[...])
    finish(back, outer_ref, (basis_high[...], basis_low[...]), weight_ref, swap_ref, back_ref, face_ref, outs)


def table_body(
    tiles_ref, basis_ref, rows_ref, all_ref, column_ref, face_ref, weight_ref, schur_high, schur_low, *refs, line
):
    sides = (rows_ref,) + refs[: line - 1]
    high_ref, low_ref, outer_ref, early_ref, inside_ref, sems = refs[line - 1 :]
    copies = start_all(
        sems, (tiles_ref.at[:EARLY], early_ref), (basis_ref.at[0, :, : NIN * BS], inside_ref)
    )
    solve_faces(face_ref, weight_ref, schur_high, schur_low, outer_ref)
    here = lax.axis_index("gz")
    slots = lax.broadcasted_iota(jnp.int32, (BS, BS), 1)
    table = jnp.zeros((2 * BS, all_ref.shape[1]), F32)
    for m in range(line):
        owner = jnp.bitwise_xor(here, m)
        mine = (slots == column_ref[1]) & (column_ref[0] // (OCAP * CW) == owner)
        take = mine.astype(F32).astype(BF16)[:, : SCAP * CW]
        high, low = halves(owner_rows(sides[m], m))
        both = jnp.concatenate([mm(take, high).astype(BF16), mm(take, low).astype(BF16)], axis=0)
        table = table + mm(both, pick_of(all_ref, owner))
    high_ref[...] = table[:BS].astype(BF16)
    low_ref[...] = table[BS:].astype(BF16)
    for copy in copies:
        copy.wait()


def next_coarse_body(*refs, line):
    contribs = [ref[...] for ref in refs[:line]]
    high_ref, low_ref, outer_ref, basis_high, basis_low, weight_ref, swap_ref = refs[line : 7 + line]
    back_ref, face_ref = refs[7 + line : 9 + line]
    table = (high_ref[...], low_ref[...])
    back = dot_halves(halves(jnp.concatenate(contribs, axis=1)), table, NT)
    finish(back, outer_ref, (basis_high[...], basis_low[...]), weight_ref, swap_ref, back_ref, face_ref,
           refs[9 + line :])


def add_row(x, i, wide, cols_ref, acc_ref):
    out = dot_halves(halves(x), wide)
    places = [cols_ref[t, i] for t in range(TPR)]
    before = [acc_ref[place] for place in places]
    for t in range(TPR):
        acc_ref[places[t]] = before[t] + out[:, lanes(t)]


def wide_of(tiles, i):
    return halves(jnp.concatenate([tiles[i, t] for t in range(TPR)], axis=1))


def own_apply(
    inner_ref, back_ref, early_ref, basis, tiles_ref, cols_ref, z_ref, acc_ref, tiles, cols, sems
):
    pairs = [(cols_ref, cols)]
    first = EARLY
    for count in CHUNKS:
        pairs.append(
            (tiles_ref.at[first : first + count], tiles.at[first - EARLY : first - EARLY + count])
        )
        first += count
    copies = start_all(sems, *pairs)
    acc_ref[...] = jnp.zeros_like(acc_ref)
    back = halves(back_ref[...])
    corr = dot_halves(back, halves(basis[...]))
    for b in range(NIN):
        z_ref[b] = inner_ref[b] + corr[:, lanes(b)]
    copies[0].wait()
    for i in range(EARLY):
        add_row(z_ref[i], i, wide_of(early_ref, i), cols, acc_ref)
    first = EARLY
    for k, count in enumerate(CHUNKS):
        copies[1 + k].wait()
        for i in range(first, first + count):
            add_row(z_ref[i], i, wide_of(tiles, i - EARLY), cols, acc_ref)
        first += count


def first_apply_body(*refs):
    own_apply(*refs)


def pair_sums(pairs):
    return [sum(left * right for left, right in blocks) for blocks in pairs]


def second_apply_body(
    inner_ref, back_ref, early_ref, basis, tiles_ref, cols_ref, load_hbm, zi, zf, yi, yf,
    z_ref, acc_ref, sums_ref, load_ref, tiles, load, cols, sems, more,
):
    (copy,) = start_all(more, (load_hbm.at[0], load))
    own_apply(inner_ref, back_ref, early_ref, basis, tiles_ref, cols_ref, z_ref, acc_ref, tiles, cols, sems)
    copy.wait()
    sums = pair_sums(
        (
            [(load[:, lanes(b)], zi[b]) for b in range(NIN)]
            + [(load[:, lanes(NIN + r)], zf[r]) for r in range(NF)],
            [(zi[b], yi[b]) for b in range(NIN)] + [(zf[r], yf[r]) for r in range(NF)],
            [(load[:, lanes(b)], z_ref[b]) for b in range(NIN)],
            [(yi[b], z_ref[b]) for b in range(NIN)],
            [(z_ref[b], acc_ref[b]) for b in range(NIN)],
        )
    )
    for k, value in enumerate(sums):
        sums_ref[k] = value
    for b in range(NB):
        load_ref[b] = load[:, lanes(b)]


def face_apply(acc_ref, incs, face_ref, block_high, block_low, swap_ref, y_ref, z_ref, outs):
    faces = [face_ref[r] + inc[...] for r, inc in enumerate(incs)]
    wide = [
        jnp.concatenate(
            [jnp.concatenate([ref[r, c] for c in range(NF)], axis=1) for r in range(NF)], axis=0
        )
        for ref in (block_high, block_low)
    ]
    more = dot_halves(halves(jnp.concatenate(faces, axis=1)), wide)
    for r, out in enumerate(outs):
        z_ref[r] = faces[r]
        y_ref[r] = acc_ref[NIN + r] + more[:, lanes(r)]
        out[...] = select_lanes(y_ref[r], swap_ref[r])
    return faces, more


def first_face_body(
    acc_ref, in0, in1, in2, in3, face_ref, block_high, block_low, swap_ref,
    y_ref, z_ref, out0, out1, out2, out3,
):
    face_apply(
        acc_ref, (in0, in1, in2, in3), face_ref, block_high, block_low, swap_ref, y_ref, z_ref,
        (out0, out1, out2, out3),
    )


def second_face_body(
    acc_ref, in0, in1, in2, in3, face_ref, block_high, block_low, swap_ref, sums_ref, load_ref, yf,
    y_ref, z_ref, dots_ref, out0, out1, out2, out3,
):
    faces, more = face_apply(
        acc_ref, (in0, in1, in2, in3), face_ref, block_high, block_low, swap_ref, y_ref, z_ref,
        (out0, out1, out2, out3),
    )
    late = pair_sums(
        (
            [(load_ref[NIN + r], faces[r]) for r in range(NF)],
            [(yf[r], faces[r]) for r in range(NF)],
            [(faces[r], 2.0 * acc_ref[NIN + r] + more[:, lanes(r)]) for r in range(NF)],
        )
    )
    sums = [sums_ref[0], sums_ref[1]] + [sums_ref[2 + k] + late[k] for k in range(3)]
    place = lax.broadcasted_iota(jnp.int32, (NRHS, BS), 1)
    case = lax.broadcasted_iota(jnp.int32, (NRHS, BS), 0)
    for row in range(2):
        total = jnp.zeros((NRHS, BS), F32)
        for k in range(4 * row, min(4 * row + 4, len(sums))):
            column = jnp.sum(sums[k], axis=1, keepdims=True)
            total = total + jnp.where(place == case + NRHS * (k % 4), column, 0.0)
        total = jnp.sum(total, axis=0, keepdims=True)
        dots_ref[:, row : row + 1, :] = jnp.broadcast_to(total[None], (dots_ref.shape[0], 1, BS))


def final_body(
    dots_ref, in0, in1, in2, in3, load, rf, zi, zf, yi, qf, wi, wf, vi, vf, sol_ref, res_ref,
):
    place = lax.broadcasted_iota(jnp.int32, (NRHS, BS), 1)
    case = lax.broadcasted_iota(jnp.int32, (NRHS, BS), 0)
    total = jnp.sum(dots_ref[...], axis=0)
    rz, zq, rw, qw, wv = [
        jnp.sum(
            jnp.where(place == case + NRHS * (k % 4), total[k // 4 : k // 4 + 1, :], 0.0),
            axis=1,
            keepdims=True,
        )
        for k in range(5)
    ]
    alpha = rz / zq
    rho = rz - alpha * (rw + zq) + alpha * alpha * qw
    grow = 1.0 + rho / rz
    curve = grow * grow * zq - 2.0 * grow * alpha * qw + alpha * alpha * wv
    step = rho / curve
    first = alpha + step * grow
    second = step * alpha
    for b in range(NB):
        if b < NIN:
            r_b, z_b, q_b, w_b, v_b = load[b], zi[b], yi[b], wi[b], vi[b]
        else:
            f = b - NIN
            r_b, z_b, q_b, w_b = rf[f], zf[f], qf[f], wf[f]
            v_b = vf[f] + (in0, in1, in2, in3)[f][...]
        sol_ref[0, :, lanes(b)] = first * z_b - second * w_b
        res_ref[0, :, lanes(b)] = r_b - first * q_b + second * v_b


def f32(*shape):
    return jax.ShapeDtypeStruct(shape, F32)


def bf16(*shape):
    return jax.ShapeDtypeStruct(shape, BF16)


SMEM = pl.BlockSpec(memory_space=pltpu.SMEM)
VMEM = pl.BlockSpec(memory_space=pltpu.VMEM)
HBM = pl.BlockSpec(memory_space=pltpu.HBM)


def call(body, name, outs, specs, *args, scratch=(), copies=0):
    scratch = [pltpu.VMEM(shape, F32) if isinstance(shape, tuple) else shape for shape in scratch]
    if copies:
        scratch.append(pltpu.SemaphoreType.DMA((copies,)))
    args = [
        pltpu.with_memory_space_constraint(arg, pltpu.HBM) if spec is HBM else arg
        for arg, spec in zip(args, specs, strict=True)
    ]
    return pl.pallas_call(
        body,
        name=name,
        out_shape=outs,
        in_specs=specs,
        out_specs=[VMEM] * len(outs),
        scratch_shapes=scratch,
        compiler_params=pltpu.CompilerParams(vmem_limit_bytes=16 << 20),
    )(*args)


def on_device(
    load_vector, matrix_tiles, tile_cols, interior_inv, schur_inv, coarse_basis, coarse_inv,
    row_map, face_link, coarse_id,
):
    cols = tile_cols.T
    line = lax.axis_size("gz")
    devices = line * lax.axis_size("gy") * lax.axis_size("gx")
    depth_z = line.bit_length() - 1
    depth_y = lax.axis_size("gy").bit_length() - 1
    masks = [1, 2, 1 << depth_z, 1 << (depth_z + depth_y)]

    def trade(value, mask):
        return lax.ppermute(value, AXES, [(i, i ^ mask) for i in range(devices)])

    def trade_faces(faces):
        return [trade(face, mask) for face, mask in zip(faces, masks)]

    def trade_line(value):
        return [trade(value, mask) for mask in range(1, line)]

    inside = (NIN, NRHS, BS)
    around = (NF, NRHS, BS)
    every = (NB, NRHS, BS)
    block, face, small, side = f32(*inside), f32(*around), f32(NRHS, BS), f32(NRHS + 16, BS)
    nf = NF * BS
    width = line * CB * CW
    target, for_far, column, weight, *sides = call(
        prepare_body, "prepare", [f32(8, BS), f32(NRHS + 64, BS), jax.ShapeDtypeStruct((2, BS, BS), jnp.int32), f32(2 * NF, BS)] + [side] * NF, [HBM] * 4,
        load_vector, row_map, coarse_id, face_link,
        scratch=[pltpu.SMEM((1, CB), jnp.int32), pltpu.SMEM((1, NF), jnp.int32),
                 pltpu.VMEM((1, NF, BS), jnp.int32), (NRHS, nf)],
        copies=4,
    )
    came = trade_faces(sides)
    far = [trade(for_far, mask) for mask in range(3, line)]

    own = OCAP * CW
    mat_outs = [block, small, bf16(nf, nf), bf16(nf, nf), bf16(BS, nf), bf16(BS, nf)]
    mat_scratch = [(NIN, BS, BS), (BS, NL), (nf, nf)]
    cols_scratch = pltpu.SMEM((TPR, NB), jnp.int32)
    face_tiles = (NF, TPR, BS, BS)

    inner, part, *mats, coarse_parts, turned = call(
        load_inside_body, "inside_load", mat_outs + [bf16(3, own, own), bf16(NF, BS, BS)],
        [HBM] * 5 + [VMEM] * NF, load_vector, interior_inv, coarse_basis, schur_inv, coarse_inv, *sides,
        scratch=mat_scratch + [(NRHS, NIN * BS), (own, own)], copies=5,
    )
    width = line * CB * CW
    half = 2 * SCAP * CW
    own_sides = sides
    pre_outs = [f32(EARLY, TPR, BS, BS), f32(BS, NIN * BS)]
    r_face, contrib, targets, *sides = call(
        lambda *refs: first_faces_body(*refs, line=line), "faces_load",
        [face, small, f32(1, width)] + [f32(NRHS + half + LINE_PADS[min(m, 3) - 1], BS) for m in range(1, line)], [VMEM] * (12 + line),
        *own_sides, *came, target, weight, *mats[2:], part, coarse_parts, turned, *far,
    )
    others = [trade(value, mask) for value, mask in zip(sides, range(1, line))]
    block_high, block_low, outer, swap, rows, picks, mine, *early = call(
        lambda *refs: under_line_body(*refs, line=line), "under_line",
        [bf16(NF, NF, BS, BS)] * 2 + [face, bf16(NF, BS, BS), f32(half, BS)]
        + [bf16(width, line * own), bf16(line * SCAP * CW, BS)] + pre_outs,
        [VMEM] * 15 + [HBM] * 3,
        *own_sides, *came, target, weight, r_face, *mats[:2], coarse_parts, targets, matrix_tiles, cols, coarse_basis,
        scratch=[face_tiles, cols_scratch], copies=4,
    )
    back, u_face, *sends = call(
        lambda *refs: first_coarse_body(*refs, line=line), "coarse_load",
        [small, face] + [small] * NF, [VMEM] * (line + 8),
        contrib, rows, picks, mine, *others, outer, *mats[2:], weight, swap,
    )

    came = trade_faces(sends)
    own_scratch = [(NIN - EARLY, TPR, BS, BS)]
    z, acc = call(
        first_apply_body, "own_first", [block, f32(*every)], [VMEM] * 4 + [HBM] * 2,
        inner, back, *early, matrix_tiles, cols,
        scratch=own_scratch + [cols_scratch], copies=1 + len(CHUNKS),
    )
    y_face, z_face, *sends = call(
        first_face_body, "face_first", [face, face] + [small] * NF, [VMEM] * 9,
        acc, *came, u_face, block_high, block_low, swap,
    )
    came = trade_faces(sends)
    y, inner, part = call(
        image_inside_body, "inside_image", [block, block, small], [VMEM] * 2 + [HBM] * 4,
        acc, z_face, cols, matrix_tiles, interior_inv, coarse_basis,
        scratch=[(NIN, BS, BS), (BS, NIN * BS), face_tiles, every, cols_scratch], copies=4,
    )
    q_face, contrib = call(
        next_faces_body, "faces_image", [face, small], [VMEM] * 9,
        y_face, *came, weight, *mats[2:], part,
    )
    sides = trade_line(contrib)
    high, low, outer, *early = call(
        lambda *refs: table_body(*refs, line=line), "table", [bf16(BS, width)] * 2 + [face] + pre_outs,
        [HBM] * 2 + [VMEM] * (line + 6), matrix_tiles, coarse_basis, rows, targets, column, q_face, weight, *mats[:2], *others, copies=2,
    )
    back, u_face, *sends = call(
        lambda *refs: next_coarse_body(*refs, line=line), "coarse_image",
        [small, face] + [small] * NF, [VMEM] * (line + 7),
        contrib, *sides, high, low, outer, *mats[2:], weight, swap,
    )
    came = trade_faces(sends)
    w, acc, sums, load = call(
        second_apply_body, "own_second", [block, f32(*every), f32(5, NRHS, BS), f32(*every)],
        [VMEM] * 4 + [HBM] * 3 + [VMEM] * 4,
        inner, back, *early, matrix_tiles, cols, load_vector, z, z_face, y, y_face,
        scratch=own_scratch + [(NRHS, NL), cols_scratch, pltpu.SemaphoreType.DMA((1 + len(CHUNKS),))],
        copies=1,
    )
    v_face, w_face, dots, *sends = call(
        second_face_body, "face_second", [face, face, f32(devices, 2, BS)] + [small] * NF, [VMEM] * 12,
        acc, *came, u_face, block_high, block_low, swap, sums, load, y_face,
    )
    spread = lax.all_to_all(dots, AXES, 0, 0)
    came = trade_faces(sends)
    (v,) = call(
        last_image_body, "inside_last", [block], [VMEM] * 2 + [HBM] * 2, acc, w_face, cols, matrix_tiles,
        scratch=[face_tiles, every, cols_scratch], copies=2,
    )
    out = f32(1, NRHS, NL)
    return tuple(
        call(
            final_body, "combine", [out, out], [VMEM] * 15,
            spread, *came, load, r_face, z, z_face, y, q_face, w, w_face, v, v_face,
        )
    )


def solution(mesh):
    lead = P(AXES, None, None)
    flat = P(AXES, None)
    in_specs = (lead, P(AXES, None, None, None), flat, lead, lead, lead, lead, lead, flat, flat)
    return jax.shard_map(
        on_device, mesh=mesh, in_specs=in_specs, out_specs=(lead, lead), check_vma=False
    )
```

```python
import jax
import jax.numpy as jnp
from jax import lax
from jax.experimental import pallas as pl
from jax.experimental.pallas import tpu as pltpu
from jax.sharding import PartitionSpec as P

BS = 128
NIN = 12
NF = 4
NRHS = 32
CW = 32
CB = 4
OCAP = 8
SCAP = 2
EARLY = 6
LINE_PADS = (0, 8, 0)
CHUNKS = (4, 2)
NB = 16
TPR = 7
NL = 2048
AXES = ("gx", "gy", "gz")
F32 = jnp.float32
BF16 = jnp.bfloat16
NN = (((1,), (0,)), ((), ()))
NT = (((1,), (1,)), ((), ()))


def mm(left, right, dims=NN):
    return lax.dot_general(left, right, dims, preferred_element_type=F32)


def halves(value):
    high = value.astype(BF16)
    return high, (value - high.astype(F32)).astype(BF16)


def dot_halves(left, right, dims=NN):
    (lh, ll), (rh, rl) = left, right
    rows = lh.shape[0]
    both = mm(jnp.concatenate([lh, ll], axis=0), rh, dims)
    return both[:rows] + both[rows:] + mm(lh, rl, dims)


def select_lanes(value, onehot):
    rows = value.shape[0]
    high, rest = halves(value)
    low = (value - high.astype(F32) - rest.astype(F32)).astype(BF16)
    out = mm(jnp.concatenate([high, rest, low], axis=0), onehot)
    return out[:rows] + out[rows : 2 * rows] + out[2 * rows :]


def lanes(block):
    return slice(block * BS, (block + 1) * BS)


def start_all(sems, *pairs):
    copies = [pltpu.make_async_copy(src, dst, sems.at[k]) for k, (src, dst) in enumerate(pairs)]
    for copy in copies:
        copy.start()
    return copies


def prepare_body(
    load_ref, map_ref, id_ref, link_ref, target_ref, far_ref, column_ref, weight_ref, side0, side1, side2, side3,
    ids, links, maps, faces, sems,
):
    copies = start_all(
        sems,
        (id_ref, ids),
        (link_ref, links),
        (map_ref, maps),
        (load_ref.at[0, :, NIN * BS :], faces),
    )
    copies[0].wait()
    along = lax.broadcasted_iota(jnp.int32, (8, BS), 1)
    down = lax.broadcasted_iota(jnp.int32, (BS, BS), 0)
    target, place = along % CW, along % CW
    column, spot = down % CW, down % CW
    for b in range(CB):
        start = ids[0, b] * CW
        before = jnp.int32(0)
        for other in range(b):
            before = before + jnp.where(ids[0, other] // OCAP == ids[0, b] // OCAP, CW, 0)
        target = jnp.where(along // CW == b, target + start, target)
        place = jnp.where(along // CW == b, place + before, place)
        column = jnp.where(down // CW == b, column + start, column)
        spot = jnp.where(down // CW == b, spot + before, spot)
    line = lax.broadcasted_iota(jnp.int32, (8, BS), 0)
    target = jnp.where(line == 1, place, target).astype(F32)
    target_ref[...] = target
    far_ref[...] = jnp.zeros_like(far_ref)
    far_ref[:8, :] = target
    column_ref[0] = column
    column_ref[1] = spot
    copies[1].wait()
    for r in range(NF):
        link = jnp.full((1, BS), links[0, r], jnp.int32).astype(F32)
        weight_ref[r : r + 1, :] = 1.0 - 0.5 * link
        weight_ref[NF + r : NF + r + 1, :] = link
    copies[2].wait()
    copies[3].wait()
    for r, out in enumerate((side0, side1, side2, side3)):
        out[:NRHS, :] = faces[:, lanes(r)]
        out[NRHS : NRHS + 8, :] = jnp.broadcast_to(maps[0, r : r + 1, :], (8, BS)).astype(F32)
        out[NRHS + 8 :, :] = target


def face_rows(acc_ref, face_ref, tiles, cols, out_ref, spare_ref):
    spare_ref[...] = acc_ref[...]
    for r in range(NF):
        add_row(face_ref[r], NIN + r, tiles[r], cols, spare_ref)
    out_ref[...] = spare_ref[:NIN]


def solve_inside(x_of, inv, basis, copies, inner_ref, part_ref):
    copies[0].wait()
    pieces = []
    for b in range(NIN):
        xb = halves(x_of(b))
        pieces.append(xb)
        inner_ref[b] = dot_halves(xb, halves(inv[b]))
    cat = tuple(jnp.concatenate([p[h] for p in pieces], axis=1) for h in range(2))
    copies[1].wait()
    part_ref[...] = dot_halves(cat, halves(basis[:, : NIN * BS]), NT)


def load_inside_body(
    x_ref, inv_ref, basis_ref, schur_ref, coarse_ref,
    own0, own1, own2, own3,
    inner_ref, part_ref, schur_high, schur_low, basis_high, basis_low, coarse_parts, mine_ref,
    inv, basis, schur, x, coarse, sems,
):
    first, *copies = start_all(
        sems, (x_ref.at[0, :, : NIN * BS], x), (inv_ref, inv), (basis_ref.at[0], basis),
        (schur_ref.at[0], schur), (coarse_ref.at[0], coarse),
    )
    rows = lax.broadcasted_iota(jnp.int32, (BS, BS), 0).astype(F32)
    for r, side in enumerate((own0, own1, own2, own3)):
        mine_ref[r] = (rows == side[NRHS : NRHS + 1, :]).astype(F32).T.astype(BF16)
    first.wait()
    solve_inside(lambda b: x[:, lanes(b)], inv, basis, copies, inner_ref, part_ref)
    basis_high[...], basis_low[...] = halves(basis[:, NIN * BS :])
    copies[2].wait()
    schur_high[...], schur_low[...] = halves(schur[...])
    copies[3].wait()
    value = coarse[...]
    for k in range(3):
        coarse_parts[k] = value.astype(BF16)
        value = value - coarse_parts[k].astype(F32)


def image_inside_body(
    acc_ref, face_ref, cols_ref, tiles_ref, inv_ref, basis_ref, y_ref, inner_ref, part_ref,
    inv, basis, tiles, spare, cols, sems,
):
    first, second, *copies = start_all(
        sems, (cols_ref, cols), (tiles_ref.at[NIN:], tiles), (inv_ref, inv),
        (basis_ref.at[0, :, : NIN * BS], basis),
    )
    first.wait()
    second.wait()
    face_rows(acc_ref, face_ref, [wide_of(tiles, r) for r in range(NF)], cols, y_ref, spare)
    solve_inside(lambda b: y_ref[b], inv, basis, copies, inner_ref, part_ref)


def last_image_body(acc_ref, face_ref, cols_ref, tiles_ref, y_ref, tiles, spare, cols, sems):
    copies = start_all(sems, (cols_ref, cols), (tiles_ref.at[NIN:], tiles))
    for copy in copies:
        copy.wait()
    face_rows(acc_ref, face_ref, [wide_of(tiles, r) for r in range(NF)], cols, y_ref, spare)


def scaled_faces(faces, weight_ref):
    return halves(
        jnp.concatenate([faces[r] * weight_ref[r : r + 1, :] for r in range(NF)], axis=1)
    )


def add_faces(faces, weight_ref, basis_high, basis_low, part_ref, contrib_ref):
    scaled = scaled_faces(faces, weight_ref)
    contrib_ref[...] = part_ref[...] + dot_halves(scaled, (basis_high[...], basis_low[...]), NT)


def solve_faces(face_ref, weight_ref, schur_high, schur_low, outer_ref):
    outer = dot_halves(scaled_faces(face_ref, weight_ref), (schur_high[...], schur_low[...]))
    for r in range(NF):
        outer_ref[r] = outer[:, lanes(r)]


def onehot(equal):
    return equal.astype(F32).astype(BF16)


def maps_of(own, inc):
    rows = lax.broadcasted_iota(jnp.int32, (BS, BS), 0).astype(F32)
    return onehot(rows == own[NRHS : NRHS + 1, :]), onehot(rows == inc[NRHS : NRHS + 1, :])


def rows_for(targets, coarse_ref):
    here = lax.axis_index("gz")
    slots = lax.broadcasted_iota(jnp.int32, (SCAP * CW, BS), 0)
    places = lax.broadcasted_iota(jnp.int32, (OCAP * CW, BS), 0)
    takes = []
    for target in targets:
        goal = target.astype(jnp.int32)
        into = onehot(slots == goal[1:2, :])
        out_of = onehot(places == goal[0:1, :] - here * (OCAP * CW))
        takes.append(mm(into, out_of, NT).astype(BF16))
    take = jnp.concatenate(takes, axis=0)
    rows = mm(take, coarse_ref[0]) + mm(take, coarse_ref[1]) + mm(take, coarse_ref[2])
    return [rows[k * SCAP * CW : (k + 1) * SCAP * CW] for k in range(len(targets))]


def put_rows(ref, first, rows):
    ref[first : first + SCAP * CW, :] = rows[:, :BS]
    ref[first + SCAP * CW : first + 2 * SCAP * CW, :] = rows[:, BS:]


def first_faces_body(
    own0, own1, own2, own3, in0, in1, in2, in3, target_ref, weight_ref,
    basis_high, basis_low, part_ref, coarse_ref, turned_ref, *rest, line,
):
    targets = [target_ref[...], in0[NRHS + 8 :, :], in1[NRHS + 8 :, :]] + [
        ref[:8, :] for ref in rest[: line - 3]
    ]
    face_ref, contrib_ref, all_ref, *sides = rest[line - 3 :]
    faces = []
    for r, (own, inc) in enumerate(zip((own0, own1, own2, own3), (in0, in1, in2, in3))):
        theirs = maps_of(own, inc)[1]
        link = weight_ref[NF + r : NF + r + 1, :]
        came = select_lanes(inc[:NRHS, :], (mm(theirs, turned_ref[r]) * link).astype(BF16))
        faces.append(own[:NRHS, :] + came)
        face_ref[r] = faces[-1]
    add_faces(faces, weight_ref, basis_high, basis_low, part_ref, contrib_ref)
    all_ref[...] = jnp.concatenate([t[0:1, :] for t in targets], axis=1)
    for side, rows in zip(sides, rows_for(targets[1:], coarse_ref)):
        side[:NRHS, :] = contrib_ref[...]
        if side.shape[0] > NRHS + 2 * SCAP * CW:
            side[NRHS + 2 * SCAP * CW :, :] = jnp.zeros_like(side[NRHS + 2 * SCAP * CW :, :])
        put_rows(side, NRHS, rows)


def under_line_body(
    own0, own1, own2, own3, in0, in1, in2, in3, target_ref, weight_ref, face_ref, schur_high, schur_low,
    coarse_ref, all_ref, tiles_ref, cols_ref,
    basis_ref, high_ref, low_ref, outer_ref, swap_ref, rows_ref, pick_ref, mine_ref, early_ref, inside_ref,
    tiles, cols, sems, *, line,
):
    *copies, third, fourth = start_all(
        sems, (cols_ref, cols), (tiles_ref.at[NIN:], tiles), (tiles_ref.at[:EARLY], early_ref),
        (basis_ref.at[0, :, : NIN * BS], inside_ref),
    )
    solve_faces(face_ref, weight_ref, schur_high, schur_low, outer_ref)
    for r, (own, inc) in enumerate(zip((own0, own1, own2, own3), (in0, in1, in2, in3))):
        mine, theirs = maps_of(own, inc)
        swap_ref[r] = (mm(mine, theirs, NT) * weight_ref[NF + r : NF + r + 1, :]).astype(BF16)
    put_rows(rows_ref, 0, rows_for([target_ref[...]], coarse_ref)[0])
    here = lax.axis_index("gz")
    own = OCAP * CW
    goal = target_ref[...].astype(jnp.int32)
    slots = lax.broadcasted_iota(jnp.int32, (SCAP * CW, BS), 0)
    places = lax.broadcasted_iota(jnp.int32, (BS, own), 1)
    for e in range(line):
        down = jnp.broadcast_to(all_ref[:, lanes(e)], (BS, BS)).T.astype(jnp.int32)
        down = jnp.concatenate([down] * (own // BS), axis=1)
        for m in range(line):
            owner = jnp.bitwise_xor(here, m)
            pick_ref[lanes(e), m * own : (m + 1) * own] = onehot(places + owner * own == down)
    for m in range(line):
        owner = jnp.bitwise_xor(here, m)
        mine = (slots == goal[1:2, :]) & (goal[0:1, :] // own == owner)
        mine_ref[m * SCAP * CW : (m + 1) * SCAP * CW, :] = onehot(mine)
    high_ref[...] = jnp.zeros_like(high_ref)
    low_ref[...] = jnp.zeros_like(low_ref)
    for copy in copies:
        copy.wait()
    for r in range(NF):
        for t in range(TPR):
            place = cols[t, NIN + r] - NIN

            @pl.when(place >= 0)
            def _(r=r, t=t, place=place):
                high_ref[r, place], low_ref[r, place] = halves(tiles[r, t])

    third.wait()
    fourth.wait()


def next_faces_body(
    y_ref, in0, in1, in2, in3, weight_ref, basis_high, basis_low, part_ref, face_ref, contrib_ref,
):
    faces = []
    for r, inc in enumerate((in0, in1, in2, in3)):
        faces.append(y_ref[r] + inc[...])
        face_ref[r] = faces[-1]
    add_faces(faces, weight_ref, basis_high, basis_low, part_ref, contrib_ref)


def finish(back, outer_ref, basis, weight_ref, swap_ref, back_ref, face_ref, outs):
    back_ref[...] = back
    corr = dot_halves(halves(back), basis)
    for r in range(NF):
        value = weight_ref[r : r + 1, :] * (outer_ref[r] + corr[:, lanes(r)])
        face_ref[r] = value
        outs[r][...] = select_lanes(value, swap_ref[r])


def owner_rows(side, m):
    first = NRHS if m else 0
    return jnp.concatenate(
        [side[first : first + SCAP * CW, :], side[first + SCAP * CW : first + 2 * SCAP * CW, :]],
        axis=1,
    )


def pick_of(all_ref, owner):
    rows = lax.broadcasted_iota(jnp.int32, (OCAP * CW, all_ref.shape[1]), 0)
    return (rows + owner * (OCAP * CW) == all_ref[...].astype(jnp.int32)).astype(F32).astype(BF16)


def first_coarse_body(own_ref, rows_ref, pick_ref, mine_ref, *refs, line):
    sides = (rows_ref,) + refs[: line - 1]
    outer_ref, basis_high, basis_low, weight_ref, swap_ref, back_ref, face_ref, *outs = refs[line - 1 :]
    contribs = halves(jnp.concatenate([own_ref[...]] + [s[:NRHS, :] for s in sides[1:]], axis=1))
    both = mm(jnp.concatenate(contribs, axis=0), pick_ref[...])
    gathered = both[:NRHS] + both[NRHS:]
    own = OCAP * CW
    solved = [
        dot_halves(halves(gathered[:, m * own : (m + 1) * own]), halves(owner_rows(side, m)), NT)
        for m, side in enumerate(sides)
    ]
    back = select_lanes(jnp.concatenate(solved, axis=1), mine_ref[...])
    finish(back, outer_ref, (basis_high[...], basis_low[...]), weight_ref, swap_ref, back_ref, face_ref, outs)


def table_body(
    tiles_ref, basis_ref, rows_ref, all_ref, column_ref, face_ref, weight_ref, schur_high, schur_low, *refs, line
):
    sides = (rows_ref,) + refs[: line - 1]
    high_ref, low_ref, outer_ref, early_ref, inside_ref, sems = refs[line - 1 :]
    copies = start_all(
        sems, (tiles_ref.at[:EARLY], early_ref), (basis_ref.at[0, :, : NIN * BS], inside_ref)
    )
    solve_faces(face_ref, weight_ref, schur_high, schur_low, outer_ref)
    here = lax.axis_index("gz")
    slots = lax.broadcasted_iota(jnp.int32, (BS, BS), 1)
    table = jnp.zeros((2 * BS, all_ref.shape[1]), F32)
    for m in range(line):
        owner = jnp.bitwise_xor(here, m)
        mine = (slots == column_ref[1]) & (column_ref[0] // (OCAP * CW) == owner)
        take = mine.astype(F32).astype(BF16)[:, : SCAP * CW]
        high, low = halves(owner_rows(sides[m], m))
        both = jnp.concatenate([mm(take, high).astype(BF16), mm(take, low).astype(BF16)], axis=0)
        table = table + mm(both, pick_of(all_ref, owner))
    high_ref[...] = table[:BS].astype(BF16)
    low_ref[...] = table[BS:].astype(BF16)
    for copy in copies:
        copy.wait()


def next_coarse_body(*refs, line):
    contribs = [ref[...] for ref in refs[:line]]
    high_ref, low_ref, outer_ref, basis_high, basis_low, weight_ref, swap_ref = refs[line : 7 + line]
    back_ref, face_ref = refs[7 + line : 9 + line]
    table = (high_ref[...], low_ref[...])
    back = dot_halves(halves(jnp.concatenate(contribs, axis=1)), table, NT)
    finish(back, outer_ref, (basis_high[...], basis_low[...]), weight_ref, swap_ref, back_ref, face_ref,
           refs[9 + line :])


def add_row(x, i, wide, cols_ref, acc_ref):
    out = dot_halves(halves(x), wide)
    places = [cols_ref[t, i] for t in range(TPR)]
    before = [acc_ref[place] for place in places]
    for t in range(TPR):
        acc_ref[places[t]] = before[t] + out[:, lanes(t)]


def wide_of(tiles, i):
    return halves(jnp.concatenate([tiles[i, t] for t in range(TPR)], axis=1))


def own_apply(
    inner_ref, back_ref, early_ref, basis, tiles_ref, cols_ref, z_ref, acc_ref, tiles, cols, sems
):
    pairs = [(cols_ref, cols)]
    first = EARLY
    for count in CHUNKS:
        pairs.append(
            (tiles_ref.at[first : first + count], tiles.at[first - EARLY : first - EARLY + count])
        )
        first += count
    copies = start_all(sems, *pairs)
    acc_ref[...] = jnp.zeros_like(acc_ref)
    back = halves(back_ref[...])
    corr = dot_halves(back, halves(basis[...]))
    for b in range(NIN):
        z_ref[b] = inner_ref[b] + corr[:, lanes(b)]
    copies[0].wait()
    for i in range(EARLY):
        add_row(z_ref[i], i, wide_of(early_ref, i), cols, acc_ref)
    first = EARLY
    for k, count in enumerate(CHUNKS):
        copies[1 + k].wait()
        for i in range(first, first + count):
            add_row(z_ref[i], i, wide_of(tiles, i - EARLY), cols, acc_ref)
        first += count


def first_apply_body(*refs):
    own_apply(*refs)


def pair_sums(pairs):
    return [sum(left * right for left, right in blocks) for blocks in pairs]


def second_apply_body(
    inner_ref, back_ref, early_ref, basis, tiles_ref, cols_ref, load_hbm, zi, zf, yi, yf,
    z_ref, acc_ref, sums_ref, load_ref, tiles, load, cols, sems, more,
):
    (copy,) = start_all(more, (load_hbm.at[0], load))
    own_apply(inner_ref, back_ref, early_ref, basis, tiles_ref, cols_ref, z_ref, acc_ref, tiles, cols, sems)
    copy.wait()
    sums = pair_sums(
        (
            [(load[:, lanes(b)], zi[b]) for b in range(NIN)]
            + [(load[:, lanes(NIN + r)], zf[r]) for r in range(NF)],
            [(zi[b], yi[b]) for b in range(NIN)] + [(zf[r], yf[r]) for r in range(NF)],
            [(load[:, lanes(b)], z_ref[b]) for b in range(NIN)],
            [(yi[b], z_ref[b]) for b in range(NIN)],
            [(z_ref[b], acc_ref[b]) for b in range(NIN)],
        )
    )
    for k, value in enumerate(sums):
        sums_ref[k] = value
    for b in range(NB):
        load_ref[b] = load[:, lanes(b)]


def face_apply(acc_ref, incs, face_ref, block_high, block_low, swap_ref, y_ref, z_ref, outs):
    faces = [face_ref[r] + inc[...] for r, inc in enumerate(incs)]
    wide = [
        jnp.concatenate(
            [jnp.concatenate([ref[r, c] for c in range(NF)], axis=1) for r in range(NF)], axis=0
        )
        for ref in (block_high, block_low)
    ]
    more = dot_halves(halves(jnp.concatenate(faces, axis=1)), wide)
    for r, out in enumerate(outs):
        z_ref[r] = faces[r]
        y_ref[r] = acc_ref[NIN + r] + more[:, lanes(r)]
        out[...] = select_lanes(y_ref[r], swap_ref[r])
    return faces, more


def first_face_body(
    acc_ref, in0, in1, in2, in3, face_ref, block_high, block_low, swap_ref,
    y_ref, z_ref, out0, out1, out2, out3,
):
    face_apply(
        acc_ref, (in0, in1, in2, in3), face_ref, block_high, block_low, swap_ref, y_ref, z_ref,
        (out0, out1, out2, out3),
    )


def second_face_body(
    acc_ref, in0, in1, in2, in3, face_ref, block_high, block_low, swap_ref, sums_ref, load_ref, yf,
    y_ref, z_ref, dots_ref, out0, out1, out2, out3,
):
    faces, more = face_apply(
        acc_ref, (in0, in1, in2, in3), face_ref, block_high, block_low, swap_ref, y_ref, z_ref,
        (out0, out1, out2, out3),
    )
    late = pair_sums(
        (
            [(load_ref[NIN + r], faces[r]) for r in range(NF)],
            [(yf[r], faces[r]) for r in range(NF)],
            [(faces[r], 2.0 * acc_ref[NIN + r] + more[:, lanes(r)]) for r in range(NF)],
        )
    )
    sums = [sums_ref[0], sums_ref[1]] + [sums_ref[2 + k] + late[k] for k in range(3)]
    place = lax.broadcasted_iota(jnp.int32, (NRHS, BS), 1)
    case = lax.broadcasted_iota(jnp.int32, (NRHS, BS), 0)
    for row in range(2):
        total = jnp.zeros((NRHS, BS), F32)
        for k in range(4 * row, min(4 * row + 4, len(sums))):
            column = jnp.sum(sums[k], axis=1, keepdims=True)
            total = total + jnp.where(place == case + NRHS * (k % 4), column, 0.0)
        total = jnp.sum(total, axis=0, keepdims=True)
        dots_ref[:, row : row + 1, :] = jnp.broadcast_to(total[None], (dots_ref.shape[0], 1, BS))


def final_body(
    dots_ref, in0, in1, in2, in3, load, rf, zi, zf, yi, qf, wi, wf, vi, vf, sol_ref, res_ref,
):
    place = lax.broadcasted_iota(jnp.int32, (NRHS, BS), 1)
    case = lax.broadcasted_iota(jnp.int32, (NRHS, BS), 0)
    total = jnp.sum(dots_ref[...], axis=0)
    rz, zq, rw, qw, wv = [
        jnp.sum(
            jnp.where(place == case + NRHS * (k % 4), total[k // 4 : k // 4 + 1, :], 0.0),
            axis=1,
            keepdims=True,
        )
        for k in range(5)
    ]
    alpha = rz / zq
    rho = rz - alpha * (rw + zq) + alpha * alpha * qw
    grow = 1.0 + rho / rz
    curve = grow * grow * zq - 2.0 * grow * alpha * qw + alpha * alpha * wv
    step = rho / curve
    first = alpha + step * grow
    second = step * alpha
    for b in range(NB):
        if b < NIN:
            r_b, z_b, q_b, w_b, v_b = load[b], zi[b], yi[b], wi[b], vi[b]
        else:
            f = b - NIN
            r_b, z_b, q_b, w_b = rf[f], zf[f], qf[f], wf[f]
            v_b = vf[f] + (in0, in1, in2, in3)[f][...]
        sol_ref[0, :, lanes(b)] = first * z_b - second * w_b
        res_ref[0, :, lanes(b)] = r_b - first * q_b + second * v_b


def f32(*shape):
    return jax.ShapeDtypeStruct(shape, F32)


def bf16(*shape):
    return jax.ShapeDtypeStruct(shape, BF16)


SMEM = pl.BlockSpec(memory_space=pltpu.SMEM)
VMEM = pl.BlockSpec(memory_space=pltpu.VMEM)
HBM = pl.BlockSpec(memory_space=pltpu.HBM)


def call(body, name, outs, specs, *args, scratch=(), copies=0):
    scratch = [pltpu.VMEM(shape, F32) if isinstance(shape, tuple) else shape for shape in scratch]
    if copies:
        scratch.append(pltpu.SemaphoreType.DMA((copies,)))
    args = [
        pltpu.with_memory_space_constraint(arg, pltpu.HBM) if spec is HBM else arg
        for arg, spec in zip(args, specs, strict=True)
    ]
    return pl.pallas_call(
        body,
        name=name,
        out_shape=outs,
        in_specs=specs,
        out_specs=[VMEM] * len(outs),
        scratch_shapes=scratch,
        compiler_params=pltpu.CompilerParams(vmem_limit_bytes=16 << 20),
    )(*args)


def on_device(
    load_vector, matrix_tiles, tile_cols, interior_inv, schur_inv, coarse_basis, coarse_inv,
    row_map, face_link, coarse_id,
):
    cols = tile_cols.T
    line = lax.axis_size("gz")
    devices = line * lax.axis_size("gy") * lax.axis_size("gx")
    depth_z = line.bit_length() - 1
    depth_y = lax.axis_size("gy").bit_length() - 1
    masks = [1, 2, 1 << depth_z, 1 << (depth_z + depth_y)]

    def trade(value, mask):
        return lax.ppermute(value, AXES, [(i, i ^ mask) for i in range(devices)])

    def trade_faces(faces):
        return [trade(face, mask) for face, mask in zip(faces, masks)]

    def trade_line(value):
        return [trade(value, mask) for mask in range(1, line)]

    inside = (NIN, NRHS, BS)
    around = (NF, NRHS, BS)
    every = (NB, NRHS, BS)
    block, face, small, side = f32(*inside), f32(*around), f32(NRHS, BS), f32(NRHS + 16, BS)
    nf = NF * BS
    width = line * CB * CW
    target, for_far, column, weight, *sides = call(
        prepare_body, "prepare", [f32(8, BS), f32(NRHS + 24, BS), jax.ShapeDtypeStruct((2, BS, BS), jnp.int32), f32(2 * NF, BS)] + [side] * NF, [HBM] * 4,
        load_vector, row_map, coarse_id, face_link,
        scratch=[pltpu.SMEM((1, CB), jnp.int32), pltpu.SMEM((1, NF), jnp.int32),
                 pltpu.VMEM((1, NF, BS), jnp.int32), (NRHS, nf)],
        copies=4,
    )
    came = trade_faces(sides)
    far = [trade(for_far, mask) for mask in range(3, line)]

    own = OCAP * CW
    mat_outs = [block, small, bf16(nf, nf), bf16(nf, nf), bf16(BS, nf), bf16(BS, nf)]
    mat_scratch = [(NIN, BS, BS), (BS, NL), (nf, nf)]
    cols_scratch = pltpu.SMEM((TPR, NB), jnp.int32)
    face_tiles = (NF, TPR, BS, BS)

    inner, part, *mats, coarse_parts, turned = call(
        load_inside_body, "inside_load", mat_outs + [bf16(3, own, own), bf16(NF, BS, BS)],
        [HBM] * 5 + [VMEM] * NF, load_vector, interior_inv, coarse_basis, schur_inv, coarse_inv, *sides,
        scratch=mat_scratch + [(NRHS, NIN * BS), (own, own)], copies=5,
    )
    width = line * CB * CW
    half = 2 * SCAP * CW
    own_sides = sides
    pre_outs = [f32(EARLY, TPR, BS, BS), f32(BS, NIN * BS)]
    r_face, contrib, targets, *sides = call(
        lambda *refs: first_faces_body(*refs, line=line), "faces_load",
        [face, small, f32(1, width)] + [f32(NRHS + half + LINE_PADS[min(m, 3) - 1], BS) for m in range(1, line)], [VMEM] * (12 + line),
        *own_sides, *came, target, weight, *mats[2:], part, coarse_parts, turned, *far,
    )
    others = [trade(value, mask) for value, mask in zip(sides, range(1, line))]
    block_high, block_low, outer, swap, rows, picks, mine, *early = call(
        lambda *refs: under_line_body(*refs, line=line), "under_line",
        [bf16(NF, NF, BS, BS)] * 2 + [face, bf16(NF, BS, BS), f32(half, BS)]
        + [bf16(width, line * own), bf16(line * SCAP * CW, BS)] + pre_outs,
        [VMEM] * 15 + [HBM] * 3,
        *own_sides, *came, target, weight, r_face, *mats[:2], coarse_parts, targets, matrix_tiles, cols, coarse_basis,
        scratch=[face_tiles, cols_scratch], copies=4,
    )
    back, u_face, *sends = call(
        lambda *refs: first_coarse_body(*refs, line=line), "coarse_load",
        [small, face] + [small] * NF, [VMEM] * (line + 8),
        contrib, rows, picks, mine, *others, outer, *mats[2:], weight, swap,
    )

    came = trade_faces(sends)
    own_scratch = [(NIN - EARLY, TPR, BS, BS)]
    z, acc = call(
        first_apply_body, "own_first", [block, f32(*every)], [VMEM] * 4 + [HBM] * 2,
        inner, back, *early, matrix_tiles, cols,
        scratch=own_scratch + [cols_scratch], copies=1 + len(CHUNKS),
    )
    y_face, z_face, *sends = call(
        first_face_body, "face_first", [face, face] + [small] * NF, [VMEM] * 9,
        acc, *came, u_face, block_high, block_low, swap,
    )
    came = trade_faces(sends)
    y, inner, part = call(
        image_inside_body, "inside_image", [block, block, small], [VMEM] * 2 + [HBM] * 4,
        acc, z_face, cols, matrix_tiles, interior_inv, coarse_basis,
        scratch=[(NIN, BS, BS), (BS, NIN * BS), face_tiles, every, cols_scratch], copies=4,
    )
    q_face, contrib = call(
        next_faces_body, "faces_image", [face, small], [VMEM] * 9,
        y_face, *came, weight, *mats[2:], part,
    )
    sides = trade_line(contrib)
    high, low, outer, *early = call(
        lambda *refs: table_body(*refs, line=line), "table", [bf16(BS, width)] * 2 + [face] + pre_outs,
        [HBM] * 2 + [VMEM] * (line + 6), matrix_tiles, coarse_basis, rows, targets, column, q_face, weight, *mats[:2], *others, copies=2,
    )
    back, u_face, *sends = call(
        lambda *refs: next_coarse_body(*refs, line=line), "coarse_image",
        [small, face] + [small] * NF, [VMEM] * (line + 7),
        contrib, *sides, high, low, outer, *mats[2:], weight, swap,
    )
    came = trade_faces(sends)
    w, acc, sums, load = call(
        second_apply_body, "own_second", [block, f32(*every), f32(5, NRHS, BS), f32(*every)],
        [VMEM] * 4 + [HBM] * 3 + [VMEM] * 4,
        inner, back, *early, matrix_tiles, cols, load_vector, z, z_face, y, y_face,
        scratch=own_scratch + [(NRHS, NL), cols_scratch, pltpu.SemaphoreType.DMA((1 + len(CHUNKS),))],
        copies=1,
    )
    v_face, w_face, dots, *sends = call(
        second_face_body, "face_second", [face, face, f32(devices, 2, BS)] + [small] * NF, [VMEM] * 12,
        acc, *came, u_face, block_high, block_low, swap, sums, load, y_face,
    )
    spread = lax.all_to_all(dots, AXES, 0, 0)
    came = trade_faces(sends)
    (v,) = call(
        last_image_body, "inside_last", [block], [VMEM] * 2 + [HBM] * 2, acc, w_face, cols, matrix_tiles,
        scratch=[face_tiles, every, cols_scratch], copies=2,
    )
    out = f32(1, NRHS, NL)
    return tuple(
        call(
            final_body, "combine", [out, out], [VMEM] * 15,
            spread, *came, load, r_face, z, z_face, y, q_face, w, w_face, v, v_face,
        )
    )


def solution(mesh):
    lead = P(AXES, None, None)
    flat = P(AXES, None)
    in_specs = (lead, P(AXES, None, None, None), flat, lead, lead, lead, lead, lead, flat, flat)
    return jax.shard_map(
        on_device, mesh=mesh, in_specs=in_specs, out_specs=(lead, lead), check_vma=False
    )
```

```python
import jax
import jax.numpy as jnp
from jax import lax
from jax.experimental import pallas as pl
from jax.experimental.pallas import tpu as pltpu
from jax.sharding import PartitionSpec as P

BS = 128
NIN = 12
NF = 4
NRHS = 32
CW = 32
CB = 4
OCAP = 8
SCAP = 2
EARLY = 6
LINE_PADS = (0, 8, 0)
CHUNKS = (4, 2)
NB = 16
TPR = 7
NL = 2048
AXES = ("gx", "gy", "gz")
F32 = jnp.float32
BF16 = jnp.bfloat16
NN = (((1,), (0,)), ((), ()))
NT = (((1,), (1,)), ((), ()))


def mm(left, right, dims=NN):
    return lax.dot_general(left, right, dims, preferred_element_type=F32)


def halves(value):
    high = value.astype(BF16)
    return high, (value - high.astype(F32)).astype(BF16)


def dot_halves(left, right, dims=NN):
    (lh, ll), (rh, rl) = left, right
    rows = lh.shape[0]
    both = mm(jnp.concatenate([lh, ll], axis=0), rh, dims)
    return both[:rows] + both[rows:] + mm(lh, rl, dims)


def select_lanes(value, onehot):
    rows = value.shape[0]
    high, rest = halves(value)
    low = (value - high.astype(F32) - rest.astype(F32)).astype(BF16)
    out = mm(jnp.concatenate([high, rest, low], axis=0), onehot)
    return out[:rows] + out[rows : 2 * rows] + out[2 * rows :]


def lanes(block):
    return slice(block * BS, (block + 1) * BS)


def start_all(sems, *pairs):
    copies = [pltpu.make_async_copy(src, dst, sems.at[k]) for k, (src, dst) in enumerate(pairs)]
    for copy in copies:
        copy.start()
    return copies


def prepare_body(
    load_ref, map_ref, id_ref, link_ref, target_ref, far_ref, column_ref, weight_ref, side0, side1, side2, side3,
    ids, links, maps, faces, sems,
):
    copies = start_all(
        sems,
        (id_ref, ids),
        (link_ref, links),
        (map_ref, maps),
        (load_ref.at[0, :, NIN * BS :], faces),
    )
    copies[0].wait()
    along = lax.broadcasted_iota(jnp.int32, (8, BS), 1)
    down = lax.broadcasted_iota(jnp.int32, (BS, BS), 0)
    target, place = along % CW, along % CW
    column, spot = down % CW, down % CW
    for b in range(CB):
        start = ids[0, b] * CW
        before = jnp.int32(0)
        for other in range(b):
            before = before + jnp.where(ids[0, other] // OCAP == ids[0, b] // OCAP, CW, 0)
        target = jnp.where(along // CW == b, target + start, target)
        place = jnp.where(along // CW == b, place + before, place)
        column = jnp.where(down // CW == b, column + start, column)
        spot = jnp.where(down // CW == b, spot + before, spot)
    line = lax.broadcasted_iota(jnp.int32, (8, BS), 0)
    target = jnp.where(line == 1, place, target).astype(F32)
    target_ref[...] = target
    far_ref[...] = jnp.zeros_like(far_ref)
    far_ref[:8, :] = target
    column_ref[0] = column
    column_ref[1] = spot
    copies[1].wait()
    for r in range(NF):
        link = jnp.full((1, BS), links[0, r], jnp.int32).astype(F32)
        weight_ref[r : r + 1, :] = 1.0 - 0.5 * link
        weight_ref[NF + r : NF + r + 1, :] = link
    copies[2].wait()
    copies[3].wait()
    for r, out in enumerate((side0, side1, side2, side3)):
        out[:NRHS, :] = faces[:, lanes(r)]
        out[NRHS:, :] = jnp.where(line == 2, maps[0, r : r + 1, :].astype(F32), target)


def face_rows(acc_ref, face_ref, tiles, cols, out_ref, spare_ref):
    spare_ref[...] = acc_ref[...]
    for r in range(NF):
        add_row(face_ref[r], NIN + r, tiles[r], cols, spare_ref)
    out_ref[...] = spare_ref[:NIN]


def solve_inside(x_of, inv, basis, copies, inner_ref, part_ref):
    copies[0].wait()
    pieces = []
    for b in range(NIN):
        xb = halves(x_of(b))
        pieces.append(xb)
        inner_ref[b] = dot_halves(xb, halves(inv[b]))
    cat = tuple(jnp.concatenate([p[h] for p in pieces], axis=1) for h in range(2))
    copies[1].wait()
    part_ref[...] = dot_halves(cat, halves(basis[:, : NIN * BS]), NT)


def load_inside_body(
    x_ref, inv_ref, basis_ref, schur_ref, coarse_ref,
    own0, own1, own2, own3,
    inner_ref, part_ref, schur_high, schur_low, basis_high, basis_low, coarse_parts, mine_ref,
    inv, basis, schur, x, coarse, sems,
):
    first, *copies = start_all(
        sems, (x_ref.at[0, :, : NIN * BS], x), (inv_ref, inv), (basis_ref.at[0], basis),
        (schur_ref.at[0], schur), (coarse_ref.at[0], coarse),
    )
    rows = lax.broadcasted_iota(jnp.int32, (BS, BS), 0).astype(F32)
    for r, side in enumerate((own0, own1, own2, own3)):
        mine_ref[r] = (rows == side[NRHS + 2 : NRHS + 3, :]).astype(F32).T.astype(BF16)
    first.wait()
    solve_inside(lambda b: x[:, lanes(b)], inv, basis, copies, inner_ref, part_ref)
    basis_high[...], basis_low[...] = halves(basis[:, NIN * BS :])
    copies[2].wait()
    schur_high[...], schur_low[...] = halves(schur[...])
    copies[3].wait()
    value = coarse[...]
    for k in range(3):
        coarse_parts[k] = value.astype(BF16)
        value = value - coarse_parts[k].astype(F32)


def image_inside_body(
    acc_ref, face_ref, cols_ref, tiles_ref, inv_ref, basis_ref, y_ref, inner_ref, part_ref,
    inv, basis, tiles, spare, cols, sems,
):
    first, second, *copies = start_all(
        sems, (cols_ref, cols), (tiles_ref.at[NIN:], tiles), (inv_ref, inv),
        (basis_ref.at[0, :, : NIN * BS], basis),
    )
    first.wait()
    second.wait()
    face_rows(acc_ref, face_ref, [wide_of(tiles, r) for r in range(NF)], cols, y_ref, spare)
    solve_inside(lambda b: y_ref[b], inv, basis, copies, inner_ref, part_ref)


def last_image_body(acc_ref, face_ref, cols_ref, tiles_ref, y_ref, tiles, spare, cols, sems):
    copies = start_all(sems, (cols_ref, cols), (tiles_ref.at[NIN:], tiles))
    for copy in copies:
        copy.wait()
    face_rows(acc_ref, face_ref, [wide_of(tiles, r) for r in range(NF)], cols, y_ref, spare)


def scaled_faces(faces, weight_ref):
    return halves(
        jnp.concatenate([faces[r] * weight_ref[r : r + 1, :] for r in range(NF)], axis=1)
    )


def add_faces(faces, weight_ref, basis_high, basis_low, part_ref, contrib_ref):
    scaled = scaled_faces(faces, weight_ref)
    contrib_ref[...] = part_ref[...] + dot_halves(scaled, (basis_high[...], basis_low[...]), NT)


def solve_faces(face_ref, weight_ref, schur_high, schur_low, outer_ref):
    outer = dot_halves(scaled_faces(face_ref, weight_ref), (schur_high[...], schur_low[...]))
    for r in range(NF):
        outer_ref[r] = outer[:, lanes(r)]


def onehot(equal):
    return equal.astype(F32).astype(BF16)


def maps_of(own, inc):
    rows = lax.broadcasted_iota(jnp.int32, (BS, BS), 0).astype(F32)
    return onehot(rows == own[NRHS + 2 : NRHS + 3, :]), onehot(rows == inc[NRHS + 2 : NRHS + 3, :])


def rows_for(targets, coarse_ref):
    here = lax.axis_index("gz")
    slots = lax.broadcasted_iota(jnp.int32, (SCAP * CW, BS), 0)
    places = lax.broadcasted_iota(jnp.int32, (OCAP * CW, BS), 0)
    takes = []
    for target in targets:
        goal = target.astype(jnp.int32)
        into = onehot(slots == goal[1:2, :])
        out_of = onehot(places == goal[0:1, :] - here * (OCAP * CW))
        takes.append(mm(into, out_of, NT).astype(BF16))
    take = jnp.concatenate(takes, axis=0)
    rows = mm(take, coarse_ref[0]) + mm(take, coarse_ref[1]) + mm(take, coarse_ref[2])
    return [rows[k * SCAP * CW : (k + 1) * SCAP * CW] for k in range(len(targets))]


def put_rows(ref, first, rows):
    ref[first : first + SCAP * CW, :] = rows[:, :BS]
    ref[first + SCAP * CW : first + 2 * SCAP * CW, :] = rows[:, BS:]


def first_faces_body(
    own0, own1, own2, own3, in0, in1, in2, in3, target_ref, weight_ref,
    basis_high, basis_low, part_ref, coarse_ref, turned_ref, *rest, line,
):
    targets = [target_ref[...], in0[NRHS:, :], in1[NRHS:, :]] + [
        ref[:8, :] for ref in rest[: line - 3]
    ]
    face_ref, contrib_ref, all_ref, *sides = rest[line - 3 :]
    faces = []
    for r, (own, inc) in enumerate(zip((own0, own1, own2, own3), (in0, in1, in2, in3))):
        theirs = maps_of(own, inc)[1]
        link = weight_ref[NF + r : NF + r + 1, :]
        came = select_lanes(inc[:NRHS, :], (mm(theirs, turned_ref[r]) * link).astype(BF16))
        faces.append(own[:NRHS, :] + came)
        face_ref[r] = faces[-1]
    add_faces(faces, weight_ref, basis_high, basis_low, part_ref, contrib_ref)
    all_ref[...] = jnp.concatenate([t[0:1, :] for t in targets], axis=1)
    for side, rows in zip(sides, rows_for(targets[1:], coarse_ref)):
        side[:NRHS, :] = contrib_ref[...]
        if side.shape[0] > NRHS + 2 * SCAP * CW:
            side[NRHS + 2 * SCAP * CW :, :] = jnp.zeros_like(side[NRHS + 2 * SCAP * CW :, :])
        put_rows(side, NRHS, rows)


def under_line_body(
    own0, own1, own2, own3, in0, in1, in2, in3, target_ref, weight_ref, face_ref, schur_high, schur_low,
    coarse_ref, all_ref, tiles_ref, cols_ref,
    basis_ref, high_ref, low_ref, outer_ref, swap_ref, rows_ref, pick_ref, mine_ref, early_ref, inside_ref,
    tiles, cols, sems, *, line,
):
    *copies, third, fourth = start_all(
        sems, (cols_ref, cols), (tiles_ref.at[NIN:], tiles), (tiles_ref.at[:EARLY], early_ref),
        (basis_ref.at[0, :, : NIN * BS], inside_ref),
    )
    solve_faces(face_ref, weight_ref, schur_high, schur_low, outer_ref)
    for r, (own, inc) in enumerate(zip((own0, own1, own2, own3), (in0, in1, in2, in3))):
        mine, theirs = maps_of(own, inc)
        swap_ref[r] = (mm(mine, theirs, NT) * weight_ref[NF + r : NF + r + 1, :]).astype(BF16)
    put_rows(rows_ref, 0, rows_for([target_ref[...]], coarse_ref)[0])
    here = lax.axis_index("gz")
    own = OCAP * CW
    goal = target_ref[...].astype(jnp.int32)
    slots = lax.broadcasted_iota(jnp.int32, (SCAP * CW, BS), 0)
    places = lax.broadcasted_iota(jnp.int32, (BS, own), 1)
    for e in range(line):
        down = jnp.broadcast_to(all_ref[:, lanes(e)], (BS, BS)).T.astype(jnp.int32)
        down = jnp.concatenate([down] * (own // BS), axis=1)
        for m in range(line):
            owner = jnp.bitwise_xor(here, m)
            pick_ref[lanes(e), m * own : (m + 1) * own] = onehot(places + owner * own == down)
    for m in range(line):
        owner = jnp.bitwise_xor(here, m)
        mine = (slots == goal[1:2, :]) & (goal[0:1, :] // own == owner)
        mine_ref[m * SCAP * CW : (m + 1) * SCAP * CW, :] = onehot(mine)
    high_ref[...] = jnp.zeros_like(high_ref)
    low_ref[...] = jnp.zeros_like(low_ref)
    for copy in copies:
        copy.wait()
    for r in range(NF):
        for t in range(TPR):
            place = cols[t, NIN + r] - NIN

            @pl.when(place >= 0)
            def _(r=r, t=t, place=place):
                high_ref[r, place], low_ref[r, place] = halves(tiles[r, t])

    third.wait()
    fourth.wait()


def next_faces_body(
    y_ref, in0, in1, in2, in3, weight_ref, basis_high, basis_low, part_ref, face_ref, contrib_ref,
):
    faces = []
    for r, inc in enumerate((in0, in1, in2, in3)):
        faces.append(y_ref[r] + inc[...])
        face_ref[r] = faces[-1]
    add_faces(faces, weight_ref, basis_high, basis_low, part_ref, contrib_ref)


def finish(back, outer_ref, basis, weight_ref, swap_ref, back_ref, face_ref, outs):
    back_ref[...] = back
    corr = dot_halves(halves(back), basis)
    for r in range(NF):
        value = weight_ref[r : r + 1, :] * (outer_ref[r] + corr[:, lanes(r)])
        face_ref[r] = value
        outs[r][...] = select_lanes(value, swap_ref[r])


def owner_rows(side, m):
    first = NRHS if m else 0
    return jnp.concatenate(
        [side[first : first + SCAP * CW, :], side[first + SCAP * CW : first + 2 * SCAP * CW, :]],
        axis=1,
    )


def pick_of(all_ref, owner):
    rows = lax.broadcasted_iota(jnp.int32, (OCAP * CW, all_ref.shape[1]), 0)
    return (rows + owner * (OCAP * CW) == all_ref[...].astype(jnp.int32)).astype(F32).astype(BF16)


def first_coarse_body(own_ref, rows_ref, pick_ref, mine_ref, *refs, line):
    sides = (rows_ref,) + refs[: line - 1]
    outer_ref, basis_high, basis_low, weight_ref, swap_ref, back_ref, face_ref, *outs = refs[line - 1 :]
    contribs = halves(jnp.concatenate([own_ref[...]] + [s[:NRHS, :] for s in sides[1:]], axis=1))
    both = mm(jnp.concatenate(contribs, axis=0), pick_ref[...])
    gathered = both[:NRHS] + both[NRHS:]
    own = OCAP * CW
    solved = [
        dot_halves(halves(gathered[:, m * own : (m + 1) * own]), halves(owner_rows(side, m)), NT)
        for m, side in enumerate(sides)
    ]
    back = select_lanes(jnp.concatenate(solved, axis=1), mine_ref[...])
    finish(back, outer_ref, (basis_high[...], basis_low[...]), weight_ref, swap_ref, back_ref, face_ref, outs)


def table_body(
    tiles_ref, basis_ref, rows_ref, all_ref, column_ref, face_ref, weight_ref, schur_high, schur_low, *refs, line
):
    sides = (rows_ref,) + refs[: line - 1]
    high_ref, low_ref, outer_ref, early_ref, inside_ref, sems = refs[line - 1 :]
    copies = start_all(
        sems, (tiles_ref.at[:EARLY], early_ref), (basis_ref.at[0, :, : NIN * BS], inside_ref)
    )
    solve_faces(face_ref, weight_ref, schur_high, schur_low, outer_ref)
    here = lax.axis_index("gz")
    slots = lax.broadcasted_iota(jnp.int32, (BS, BS), 1)
    table = jnp.zeros((2 * BS, all_ref.shape[1]), F32)
    for m in range(line):
        owner = jnp.bitwise_xor(here, m)
        mine = (slots == column_ref[1]) & (column_ref[0] // (OCAP * CW) == owner)
        take = mine.astype(F32).astype(BF16)[:, : SCAP * CW]
        high, low = halves(owner_rows(sides[m], m))
        both = jnp.concatenate([mm(take, high).astype(BF16), mm(take, low).astype(BF16)], axis=0)
        table = table + mm(both, pick_of(all_ref, owner))
    high_ref[...] = table[:BS].astype(BF16)
    low_ref[...] = table[BS:].astype(BF16)
    for copy in copies:
        copy.wait()


def next_coarse_body(*refs, line):
    contribs = [ref[...] for ref in refs[:line]]
    high_ref, low_ref, outer_ref, basis_high, basis_low, weight_ref, swap_ref = refs[line : 7 + line]
    back_ref, face_ref = refs[7 + line : 9 + line]
    table = (high_ref[...], low_ref[...])
    back = dot_halves(halves(jnp.concatenate(contribs, axis=1)), table, NT)
    finish(back, outer_ref, (basis_high[...], basis_low[...]), weight_ref, swap_ref, back_ref, face_ref,
           refs[9 + line :])


def add_row(x, i, wide, cols_ref, acc_ref):
    out = dot_halves(halves(x), wide)
    places = [cols_ref[t, i] for t in range(TPR)]
    before = [acc_ref[place] for place in places]
    for t in range(TPR):
        acc_ref[places[t]] = before[t] + out[:, lanes(t)]


def wide_of(tiles, i):
    return halves(jnp.concatenate([tiles[i, t] for t in range(TPR)], axis=1))


def own_apply(
    inner_ref, back_ref, early_ref, basis, tiles_ref, cols_ref, z_ref, acc_ref, tiles, cols, sems
):
    pairs = [(cols_ref, cols)]
    first = EARLY
    for count in CHUNKS:
        pairs.append(
            (tiles_ref.at[first : first + count], tiles.at[first - EARLY : first - EARLY + count])
        )
        first += count
    copies = start_all(sems, *pairs)
    acc_ref[...] = jnp.zeros_like(acc_ref)
    back = halves(back_ref[...])
    corr = dot_halves(back, halves(basis[...]))
    for b in range(NIN):
        z_ref[b] = inner_ref[b] + corr[:, lanes(b)]
    copies[0].wait()
    for i in range(EARLY):
        add_row(z_ref[i], i, wide_of(early_ref, i), cols, acc_ref)
    first = EARLY
    for k, count in enumerate(CHUNKS):
        copies[1 + k].wait()
        for i in range(first, first + count):
            add_row(z_ref[i], i, wide_of(tiles, i - EARLY), cols, acc_ref)
        first += count


def first_apply_body(*refs):
    own_apply(*refs)


def pair_sums(pairs):
    return [sum(left * right for left, right in blocks) for blocks in pairs]


def second_apply_body(
    inner_ref, back_ref, early_ref, basis, tiles_ref, cols_ref, load_hbm, zi, zf, yi, yf,
    z_ref, acc_ref, sums_ref, load_ref, tiles, load, cols, sems, more,
):
    (copy,) = start_all(more, (load_hbm.at[0], load))
    own_apply(inner_ref, back_ref, early_ref, basis, tiles_ref, cols_ref, z_ref, acc_ref, tiles, cols, sems)
    copy.wait()
    sums = pair_sums(
        (
            [(load[:, lanes(b)], zi[b]) for b in range(NIN)]
            + [(load[:, lanes(NIN + r)], zf[r]) for r in range(NF)],
            [(zi[b], yi[b]) for b in range(NIN)] + [(zf[r], yf[r]) for r in range(NF)],
            [(load[:, lanes(b)], z_ref[b]) for b in range(NIN)],
            [(yi[b], z_ref[b]) for b in range(NIN)],
            [(z_ref[b], acc_ref[b]) for b in range(NIN)],
        )
    )
    for k, value in enumerate(sums):
        sums_ref[k] = value
    for b in range(NB):
        load_ref[b] = load[:, lanes(b)]


def face_apply(acc_ref, incs, face_ref, block_high, block_low, swap_ref, y_ref, z_ref, outs):
    faces = [face_ref[r] + inc[...] for r, inc in enumerate(incs)]
    wide = [
        jnp.concatenate(
            [jnp.concatenate([ref[r, c] for c in range(NF)], axis=1) for r in range(NF)], axis=0
        )
        for ref in (block_high, block_low)
    ]
    more = dot_halves(halves(jnp.concatenate(faces, axis=1)), wide)
    for r, out in enumerate(outs):
        z_ref[r] = faces[r]
        y_ref[r] = acc_ref[NIN + r] + more[:, lanes(r)]
        out[...] = select_lanes(y_ref[r], swap_ref[r])
    return faces, more


def first_face_body(
    acc_ref, in0, in1, in2, in3, face_ref, block_high, block_low, swap_ref,
    y_ref, z_ref, out0, out1, out2, out3,
):
    face_apply(
        acc_ref, (in0, in1, in2, in3), face_ref, block_high, block_low, swap_ref, y_ref, z_ref,
        (out0, out1, out2, out3),
    )


def second_face_body(
    acc_ref, in0, in1, in2, in3, face_ref, block_high, block_low, swap_ref, sums_ref, load_ref, yf,
    y_ref, z_ref, dots_ref, out0, out1, out2, out3,
):
    faces, more = face_apply(
        acc_ref, (in0, in1, in2, in3), face_ref, block_high, block_low, swap_ref, y_ref, z_ref,
        (out0, out1, out2, out3),
    )
    late = pair_sums(
        (
            [(load_ref[NIN + r], faces[r]) for r in range(NF)],
            [(yf[r], faces[r]) for r in range(NF)],
            [(faces[r], 2.0 * acc_ref[NIN + r] + more[:, lanes(r)]) for r in range(NF)],
        )
    )
    sums = [sums_ref[0], sums_ref[1]] + [sums_ref[2 + k] + late[k] for k in range(3)]
    place = lax.broadcasted_iota(jnp.int32, (NRHS, BS), 1)
    case = lax.broadcasted_iota(jnp.int32, (NRHS, BS), 0)
    for row in range(2):
        total = jnp.zeros((NRHS, BS), F32)
        for k in range(4 * row, min(4 * row + 4, len(sums))):
            column = jnp.sum(sums[k], axis=1, keepdims=True)
            total = total + jnp.where(place == case + NRHS * (k % 4), column, 0.0)
        total = jnp.sum(total, axis=0, keepdims=True)
        dots_ref[:, row : row + 1, :] = jnp.broadcast_to(total[None], (dots_ref.shape[0], 1, BS))


def final_body(
    dots_ref, in0, in1, in2, in3, load, rf, zi, zf, yi, qf, wi, wf, vi, vf, sol_ref, res_ref,
):
    place = lax.broadcasted_iota(jnp.int32, (NRHS, BS), 1)
    case = lax.broadcasted_iota(jnp.int32, (NRHS, BS), 0)
    total = jnp.sum(dots_ref[...], axis=0)
    rz, zq, rw, qw, wv = [
        jnp.sum(
            jnp.where(place == case + NRHS * (k % 4), total[k // 4 : k // 4 + 1, :], 0.0),
            axis=1,
            keepdims=True,
        )
        for k in range(5)
    ]
    alpha = rz / zq
    rho = rz - alpha * (rw + zq) + alpha * alpha * qw
    grow = 1.0 + rho / rz
    curve = grow * grow * zq - 2.0 * grow * alpha * qw + alpha * alpha * wv
    step = rho / curve
    first = alpha + step * grow
    second = step * alpha
    for b in range(NB):
        if b < NIN:
            r_b, z_b, q_b, w_b, v_b = load[b], zi[b], yi[b], wi[b], vi[b]
        else:
            f = b - NIN
            r_b, z_b, q_b, w_b = rf[f], zf[f], qf[f], wf[f]
            v_b = vf[f] + (in0, in1, in2, in3)[f][...]
        sol_ref[0, :, lanes(b)] = first * z_b - second * w_b
        res_ref[0, :, lanes(b)] = r_b - first * q_b + second * v_b


def f32(*shape):
    return jax.ShapeDtypeStruct(shape, F32)


def bf16(*shape):
    return jax.ShapeDtypeStruct(shape, BF16)


SMEM = pl.BlockSpec(memory_space=pltpu.SMEM)
VMEM = pl.BlockSpec(memory_space=pltpu.VMEM)
HBM = pl.BlockSpec(memory_space=pltpu.HBM)


def call(body, name, outs, specs, *args, scratch=(), copies=0):
    scratch = [pltpu.VMEM(shape, F32) if isinstance(shape, tuple) else shape for shape in scratch]
    if copies:
        scratch.append(pltpu.SemaphoreType.DMA((copies,)))
    args = [
        pltpu.with_memory_space_constraint(arg, pltpu.HBM) if spec is HBM else arg
        for arg, spec in zip(args, specs, strict=True)
    ]
    return pl.pallas_call(
        body,
        name=name,
        out_shape=outs,
        in_specs=specs,
        out_specs=[VMEM] * len(outs),
        scratch_shapes=scratch,
        compiler_params=pltpu.CompilerParams(vmem_limit_bytes=16 << 20),
    )(*args)


def on_device(
    load_vector, matrix_tiles, tile_cols, interior_inv, schur_inv, coarse_basis, coarse_inv,
    row_map, face_link, coarse_id,
):
    cols = tile_cols.T
    line = lax.axis_size("gz")
    devices = line * lax.axis_size("gy") * lax.axis_size("gx")
    depth_z = line.bit_length() - 1
    depth_y = lax.axis_size("gy").bit_length() - 1
    masks = [1, 2, 1 << depth_z, 1 << (depth_z + depth_y)]

    def trade(value, mask):
        return lax.ppermute(value, AXES, [(i, i ^ mask) for i in range(devices)])

    def trade_faces(faces):
        return [trade(face, mask) for face, mask in zip(faces, masks)]

    def trade_line(value):
        return [trade(value, mask) for mask in range(1, line)]

    inside = (NIN, NRHS, BS)
    around = (NF, NRHS, BS)
    every = (NB, NRHS, BS)
    block, face, small, side = f32(*inside), f32(*around), f32(NRHS, BS), f32(NRHS + 8, BS)
    nf = NF * BS
    width = line * CB * CW
    target, for_far, column, weight, *sides = call(
        prepare_body, "prepare", [f32(8, BS), f32(NRHS + 16, BS), jax.ShapeDtypeStruct((2, BS, BS), jnp.int32), f32(2 * NF, BS)] + [side] * NF, [HBM] * 4,
        load_vector, row_map, coarse_id, face_link,
        scratch=[pltpu.SMEM((1, CB), jnp.int32), pltpu.SMEM((1, NF), jnp.int32),
                 pltpu.VMEM((1, NF, BS), jnp.int32), (NRHS, nf)],
        copies=4,
    )
    came = trade_faces(sides)
    far = [trade(for_far, mask) for mask in range(3, line)]

    own = OCAP * CW
    mat_outs = [block, small, bf16(nf, nf), bf16(nf, nf), bf16(BS, nf), bf16(BS, nf)]
    mat_scratch = [(NIN, BS, BS), (BS, NL), (nf, nf)]
    cols_scratch = pltpu.SMEM((TPR, NB), jnp.int32)
    face_tiles = (NF, TPR, BS, BS)

    inner, part, *mats, coarse_parts, turned = call(
        load_inside_body, "inside_load", mat_outs + [bf16(3, own, own), bf16(NF, BS, BS)],
        [HBM] * 5 + [VMEM] * NF, load_vector, interior_inv, coarse_basis, schur_inv, coarse_inv, *sides,
        scratch=mat_scratch + [(NRHS, NIN * BS), (own, own)], copies=5,
    )
    width = line * CB * CW
    half = 2 * SCAP * CW
    own_sides = sides
    pre_outs = [f32(EARLY, TPR, BS, BS), f32(BS, NIN * BS)]
    r_face, contrib, targets, *sides = call(
        lambda *refs: first_faces_body(*refs, line=line), "faces_load",
        [face, small, f32(1, width)] + [f32(NRHS + half + LINE_PADS[min(m, 3) - 1], BS) for m in range(1, line)], [VMEM] * (12 + line),
        *own_sides, *came, target, weight, *mats[2:], part, coarse_parts, turned, *far,
    )
    others = [trade(value, mask) for value, mask in zip(sides, range(1, line))]
    block_high, block_low, outer, swap, rows, picks, mine, *early = call(
        lambda *refs: under_line_body(*refs, line=line), "under_line",
        [bf16(NF, NF, BS, BS)] * 2 + [face, bf16(NF, BS, BS), f32(half, BS)]
        + [bf16(width, line * own), bf16(line * SCAP * CW, BS)] + pre_outs,
        [VMEM] * 15 + [HBM] * 3,
        *own_sides, *came, target, weight, r_face, *mats[:2], coarse_parts, targets, matrix_tiles, cols, coarse_basis,
        scratch=[face_tiles, cols_scratch], copies=4,
    )
    back, u_face, *sends = call(
        lambda *refs: first_coarse_body(*refs, line=line), "coarse_load",
        [small, face] + [small] * NF, [VMEM] * (line + 8),
        contrib, rows, picks, mine, *others, outer, *mats[2:], weight, swap,
    )

    came = trade_faces(sends)
    own_scratch = [(NIN - EARLY, TPR, BS, BS)]
    z, acc = call(
        first_apply_body, "own_first", [block, f32(*every)], [VMEM] * 4 + [HBM] * 2,
        inner, back, *early, matrix_tiles, cols,
        scratch=own_scratch + [cols_scratch], copies=1 + len(CHUNKS),
    )
    y_face, z_face, *sends = call(
        first_face_body, "face_first", [face, face] + [small] * NF, [VMEM] * 9,
        acc, *came, u_face, block_high, block_low, swap,
    )
    came = trade_faces(sends)
    y, inner, part = call(
        image_inside_body, "inside_image", [block, block, small], [VMEM] * 2 + [HBM] * 4,
        acc, z_face, cols, matrix_tiles, interior_inv, coarse_basis,
        scratch=[(NIN, BS, BS), (BS, NIN * BS), face_tiles, every, cols_scratch], copies=4,
    )
    q_face, contrib = call(
        next_faces_body, "faces_image", [face, small], [VMEM] * 9,
        y_face, *came, weight, *mats[2:], part,
    )
    sides = trade_line(contrib)
    high, low, outer, *early = call(
        lambda *refs: table_body(*refs, line=line), "table", [bf16(BS, width)] * 2 + [face] + pre_outs,
        [HBM] * 2 + [VMEM] * (line + 6), matrix_tiles, coarse_basis, rows, targets, column, q_face, weight, *mats[:2], *others, copies=2,
    )
    back, u_face, *sends = call(
        lambda *refs: next_coarse_body(*refs, line=line), "coarse_image",
        [small, face] + [small] * NF, [VMEM] * (line + 7),
        contrib, *sides, high, low, outer, *mats[2:], weight, swap,
    )
    came = trade_faces(sends)
    w, acc, sums, load = call(
        second_apply_body, "own_second", [block, f32(*every), f32(5, NRHS, BS), f32(*every)],
        [VMEM] * 4 + [HBM] * 3 + [VMEM] * 4,
        inner, back, *early, matrix_tiles, cols, load_vector, z, z_face, y, y_face,
        scratch=own_scratch + [(NRHS, NL), cols_scratch, pltpu.SemaphoreType.DMA((1 + len(CHUNKS),))],
        copies=1,
    )
    v_face, w_face, dots, *sends = call(
        second_face_body, "face_second", [face, face, f32(devices, 2, BS)] + [small] * NF, [VMEM] * 12,
        acc, *came, u_face, block_high, block_low, swap, sums, load, y_face,
    )
    spread = lax.all_to_all(dots, AXES, 0, 0)
    came = trade_faces(sends)
    (v,) = call(
        last_image_body, "inside_last", [block], [VMEM] * 2 + [HBM] * 2, acc, w_face, cols, matrix_tiles,
        scratch=[face_tiles, every, cols_scratch], copies=2,
    )
    out = f32(1, NRHS, NL)
    return tuple(
        call(
            final_body, "combine", [out, out], [VMEM] * 15,
            spread, *came, load, r_face, z, z_face, y, q_face, w, w_face, v, v_face,
        )
    )


def solution(mesh):
    lead = P(AXES, None, None)
    flat = P(AXES, None)
    in_specs = (lead, P(AXES, None, None, None), flat, lead, lead, lead, lead, lead, flat, flat)
    return jax.shard_map(
        on_device, mesh=mesh, in_specs=in_specs, out_specs=(lead, lead), check_vma=False
    )
```
